128 devices in a mesh: rep: 4 (over z), dom: 32 (over y, x, core).
Axes of the slice: x: 4, y: 4, z: 4, core: 2. Of those that a mesh axis runs over, the one named last changes fastest.
Arguments:
- features: bfloat16 [4, 524288, 128], P('rep', 'dom'), may hold values from -30 to 30, as said below
- edges: int32 [4, 524288, 4], P('rep', 'dom'), may hold values from -128 to 128, as said below
- route: int32 [4, 1024, 256], P('rep', 'dom'), may hold values from 0 to 524287, as said below
- cotangent: bfloat16 [4, 1024, 256, 128], P('rep', 'dom'), may hold values from -6 to 6
- w_self: bfloat16 [128, 128], replicated, may hold values from -0.5 to 0.5
- w_neighbor: bfloat16 [128, 128], replicated, may hold values from -0.5 to 0.5
- bias: float32 [128], replicated, may hold values from -3 to 3
- gain: float32 [128], replicated, may hold values from 0.5 to 2
- w_expand: bfloat16 [128, 512], replicated, may hold values from -0.5 to 0.5
- w_reduce: bfloat16 [512, 128], replicated, may hold values from -0.25 to 0.25
Outputs:
- grad_features: bfloat16 [4, 524288, 128], P('rep', 'dom')
- grad_self: float32 [128, 128], replicated
- grad_neighbor: float32 [128, 128], replicated
- grad_bias: float32 [128], replicated
- grad_gain: float32 [128], replicated
- grad_expand: float32 [128, 512], replicated
- grad_reduce: float32 [512, 128], replicated
The draws below stay inside these ranges and needn't reach their ends.
Inputs may be any that keep to these rules, and one draw needn't show every extreme that they name: In `features`, rows and columns differ in scale. `edges`: an entry of row i is 0 or a distance d with 1 <= |d| <= 128 and 0 <= i + d < 524288; the largest distance 128 occurs. `route`: entries are segments of the same tile; segment s lies on index s // 16384 of dom. Among the 8192 entries of the trips on one index of dom, at most 512 lie on any one index of dom, and in every tile some index of dom holds exactly 512 entries of the trips of every index.
All inputs are finite; a program needn't handle non-finite values.
Results may differ from the reference program's by a relative error of at most 0.0075.
Values may be sent and summed in bfloat16 or wider, within the bound.
A program may use at most 192 MiB of HBM per device.

```python
import math
import jax
import jax.numpy as jnp
from jax import lax

D = 128
FF = 512
NEIGHBORS = 4
HALO = 128
SEG_DEV = 16384
TRIP_DEV = 32
L = 256
TILES = 4
PARTS_SIZE = 32
SEGS = 524288
TRIPS = 1024
ROWS_DEV = 8192
CAP = 512


def draw_features(key, part):
    key_rows, key_cols, key_base = jax.random.split(key, 3)
    row_scale = jnp.exp(jax.random.uniform(key_rows, (TILES, SEGS, 1)) * math.log(10.0))
    col_scale = jnp.exp(jax.random.uniform(key_cols, (1, 1, D), minval=-0.69, maxval=0.69))
    values = jnp.clip(jax.random.normal(key_base, (TILES, SEGS, D)), -5.0, 5.0)
    return (0.3 * row_scale * col_scale * values).astype(jnp.bfloat16)


def draw_edges(key, part):
    key_dist, key_sign, key_keep = jax.random.split(key, 3)
    distance = jax.random.randint(key_dist, (TILES, SEGS, NEIGHBORS), 1, HALO + 1)
    signs = 2 * jax.random.randint(key_sign, (TILES, SEGS, NEIGHBORS), 0, 2) - 1
    rows = jnp.arange(SEGS, dtype=jnp.int32)[None, :, None]
    offset = distance * signs
    target = rows + offset
    keep = jax.random.randint(key_keep, (TILES, SEGS, NEIGHBORS), 0, 4) > 0
    inside = (target >= 0) & (target < SEGS)
    return jnp.where(keep & inside, offset, 0).astype(jnp.int32)


def draw_route(key, part):
    key_weight, key_hot, key_slot, key_order, key_offset = jax.random.split(key, 5)
    slots_all = PARTS_SIZE * CAP
    weight = jax.random.randint(key_weight, (TILES, PARTS_SIZE), 0, 4)
    hot = jax.random.randint(key_hot, (TILES, 1), 0, PARTS_SIZE)
    weight = jnp.where(jnp.arange(PARTS_SIZE)[None, :] == hot, -1, weight)
    slot_owner = jnp.arange(slots_all, dtype=jnp.int32) // CAP
    slot_weight = weight[:, slot_owner]
    noise = jax.random.randint(key_slot, (TILES, PARTS_SIZE, slots_all), 0, 1024)
    score = ((slot_weight[:, None, :] + 1) * 1024 + noise) * slots_all + jnp.arange(slots_all, dtype=jnp.int32)
    chosen = jnp.argsort(score, axis=-1, stable=True)[:, :, :ROWS_DEV]
    owners = chosen // CAP
    shuffle_score = jax.random.randint(key_order, (TILES, PARTS_SIZE, ROWS_DEV), 0, 1 << 20) * ROWS_DEV + jnp.arange(ROWS_DEV, dtype=jnp.int32)
    shuffle = jnp.argsort(shuffle_score, axis=-1, stable=True)
    owners = jnp.take_along_axis(owners, shuffle, axis=-1)
    offsets = jax.random.randint(key_offset, (TILES, PARTS_SIZE, ROWS_DEV), 0, SEG_DEV)
    ids = owners * SEG_DEV + offsets
    return ids.reshape(TILES, TRIPS, L).astype(jnp.int32)


def block_scale(stream_key, shape, cuts, smallest, top_value):
    loudness = 1.0
    for position, parts in cuts:
        draws = jax.random.uniform(jax.random.fold_in(jax.random.fold_in(stream_key, 6), position), (parts,), jnp.float32, smallest / len(cuts), top_value / len(cuts))
        loudness = loudness * jnp.repeat(jnp.exp(draws), shape[position] // parts).reshape((-1,) + (1,) * (len(shape) - 1 - position))
    return loudness


def normal_values(stream_key, dims, scale, bound, cuts=(), held_as=jnp.bfloat16):
    drawn = scale * jax.random.normal(stream_key, dims, jnp.float32)
    if cuts:
        drawn = drawn * block_scale(stream_key, dims, cuts, -0.22, 0.18)
    return jnp.clip(drawn, -bound, bound).astype(held_as)


def setup_inputs(seed: int = 0) -> dict:
    seeds = jax.random.split(jax.random.key(seed), 11)
    return {
        "features": draw_features(jax.random.fold_in(seeds[10], 71), 0),
        "edges": draw_edges(jax.random.fold_in(seeds[10], 71), 0),
        "route": draw_route(jax.random.fold_in(seeds[10], 71), 0),
        "cotangent": normal_values(seeds[3], (TILES, TRIPS, L, D), 1.0, 6.0, ((0, 4), (1, 32))),
        "w_self": normal_values(seeds[4], (D, D), D ** -0.5, 0.5),
        "w_neighbor": normal_values(seeds[5], (D, D), D ** -0.5, 0.5),
        "bias": normal_values(seeds[6], (D,), 0.5, 3.0, (), jnp.float32),
        "gain": jnp.clip(jnp.exp(jax.random.uniform(seeds[7], (D,), jnp.float32, math.log(0.5), math.log(2.0))), 0.5, 2.0),
        "w_expand": normal_values(seeds[8], (D, FF), D ** -0.5, 0.5),
        "w_reduce": normal_values(seeds[9], (FF, D), FF ** -0.5, 0.25),
    }


def silu_slope(value):
    logistic = jax.nn.sigmoid(value)
    return logistic * (1.0 + value * (1.0 - logistic))

def encoder_back(tokens, cot_rows, gain, w_expand, w_reduce):
    values = tokens.astype(jnp.float32)
    spread = jnp.sqrt(lax.optimization_barrier(jnp.mean(values * values, axis=-1, keepdims=True)) + 1e-06)
    unit = values / spread
    normed = (unit * gain).astype(jnp.bfloat16)
    inner = jnp.dot(normed, w_expand, preferred_element_type=jnp.float32)
    active = jax.nn.silu(inner).astype(jnp.bfloat16)
    grad_reduce = jnp.dot(active.T, cot_rows, preferred_element_type=jnp.float32)
    back_active = jnp.dot(cot_rows, w_reduce.T, preferred_element_type=jnp.float32)
    back_inner = (back_active * silu_slope(inner)).astype(jnp.bfloat16)
    grad_expand = jnp.dot(normed.T, back_inner, preferred_element_type=jnp.float32)
    back_normed = jnp.dot(back_inner, w_expand.T, preferred_element_type=jnp.float32)
    grad_gain = lax.optimization_barrier(jnp.sum(back_normed * unit, axis=0))
    weighted = gain * back_normed
    back_tokens = cot_rows.astype(jnp.float32) + (weighted - unit * lax.optimization_barrier(jnp.mean(weighted * unit, axis=-1, keepdims=True))) / spread
    return (back_tokens, grad_expand, grad_reduce, grad_gain)

def tile_grads(features, edges, route, cotangent, w_self, w_neighbor, bias, gain, w_expand, w_reduce):
    valid = edges != 0
    rows = jnp.arange(SEGS, dtype=jnp.int32)[:, None]
    safe_ids = jnp.where(valid, rows + edges, 0).astype(jnp.int32)
    total = features.astype(jnp.float32)
    for slot in range(NEIGHBORS):
        picked = features[safe_ids[:, slot]].astype(jnp.float32)
        total = total + jnp.where(valid[:, slot:slot + 1], picked, 0.0)
    degree = 1.0 + lax.optimization_barrier(jnp.sum(valid.astype(jnp.float32), axis=1, keepdims=True))
    messages = (total / degree).astype(jnp.bfloat16)
    pre = jnp.dot(features, w_self, preferred_element_type=jnp.float32) + jnp.dot(messages, w_neighbor, preferred_element_type=jnp.float32) + bias
    hidden = (features.astype(jnp.float32) + jax.nn.silu(pre)).astype(jnp.bfloat16)
    flat_ids = route.reshape(PARTS_SIZE, TRIP_DEV * L).astype(jnp.int32)
    cot_groups = cotangent.reshape(PARTS_SIZE, TRIP_DEV * L, D)

    def per_group(pair):
        group_ids, group_cot = pair
        return encoder_back(hidden[group_ids], group_cot, gain, w_expand, w_reduce)
    back_tokens, grad_expand, grad_reduce, grad_gain = lax.map(per_group, (flat_ids, cot_groups))
    back_hidden = jnp.zeros((SEGS, D), jnp.float32).at[flat_ids.reshape(-1)].add(back_tokens.reshape(-1, D))
    back_pre = (back_hidden * silu_slope(pre)).astype(jnp.bfloat16)
    grad_self = jnp.dot(features.T, back_pre, preferred_element_type=jnp.float32)
    grad_neighbor = jnp.dot(messages.T, back_pre, preferred_element_type=jnp.float32)
    grad_bias = lax.optimization_barrier(jnp.sum(back_pre.astype(jnp.float32), axis=0))
    back_message = jnp.dot(back_pre, w_neighbor.T, preferred_element_type=jnp.float32)
    shared_low = lax.optimization_barrier((back_message / degree).astype(jnp.bfloat16))
    shared = shared_low.astype(jnp.float32)
    result = back_hidden + jnp.dot(back_pre, w_self.T, preferred_element_type=jnp.float32) + shared
    for slot in range(NEIGHBORS):
        result = result.at[safe_ids[:, slot]].add(jnp.where(valid[:, slot:slot + 1], shared, 0.0))
    return (result.astype(jnp.bfloat16), grad_self, grad_neighbor, grad_bias, lax.optimization_barrier(jnp.sum(grad_gain, axis=0)), lax.optimization_barrier(jnp.sum(grad_expand, axis=0)), lax.optimization_barrier(jnp.sum(grad_reduce, axis=0)))

def reference(features, edges, route, cotangent, w_self, w_neighbor, bias, gain, w_expand, w_reduce):

    def per_tile(pack):
        return tile_grads(pack[0], pack[1], pack[2], pack[3], w_self, w_neighbor, bias, gain, w_expand, w_reduce)
    results = lax.map(per_tile, (features, edges, route, cotangent))
    graph_scale = 1.0 / math.sqrt(TILES * SEGS)
    route_scale = 1.0 / math.sqrt(TILES * TRIPS * L)
    return (results[0], lax.optimization_barrier(jnp.sum(results[1], axis=0)) * graph_scale, lax.optimization_barrier(jnp.sum(results[2], axis=0)) * graph_scale, lax.optimization_barrier(jnp.sum(results[3], axis=0)) * graph_scale, lax.optimization_barrier(jnp.sum(results[4], axis=0)) * route_scale, lax.optimization_barrier(jnp.sum(results[5], axis=0)) * route_scale, lax.optimization_barrier(jnp.sum(results[6], axis=0)) * route_scale)
```

```python
import functools
import math

import jax
import jax.numpy as jnp
from jax import lax
from jax.experimental import pallas as pl
from jax.experimental.pallas import tpu as pltpu
from jax.sharding import PartitionSpec as P

HALO = 128
WIN = 16
GROUP = 256
STEP = 1024
F32 = jnp.float32
BF16 = jnp.bfloat16
VMEM_LIMIT = 56 * 1024 * 1024


def iota(shape, dim, dtype=jnp.int32):
    return lax.broadcasted_iota(jnp.int32, shape, dim).astype(dtype)


def dot(a, b, da=1, db=0):
    return lax.dot_general(a, b, (((da,), (db,)), ((), ())), preferred_element_type=F32)


def sigmoid(value):
    return 0.5 * jnp.tanh(0.5 * value) + 0.5


def neighbours(array, dim, width):
    size, length = lax.axis_size("dom"), array.shape[dim]
    up = [(i, i + 1) for i in range(size - 1)]
    down = [(j, i) for i, j in up]
    last = lax.slice_in_dim(array, length - width, length, axis=dim)
    first = lax.slice_in_dim(array, 0, width, axis=dim)
    return lax.ppermute(last, "dom", up), lax.ppermute(first, "dom", down)


def pack_kernel(capacity, seg_rows, order, bounds, ids, cot, rows_out, ids_out, rows, stage):
    owner = pl.program_id(0)
    chunk = 512

    @pl.when(owner == 0)
    def _():
        stage[...] = jnp.zeros_like(stage)

        @pl.loop(0, cot.shape[0] // chunk)
        def _(i):
            part = pl.ds(pl.multiple_of(i * chunk, chunk), chunk)
            rows[part, :] = cot[part, :].astype(F32)

    start = bounds[owner]
    count = bounds[owner + 1] - start

    def move(g, carry):
        base = pl.multiple_of(g * 16, 16)
        for j in range(16):
            source = order[start + base + j]
            stage[pl.ds(base + j, 1), :] = rows[pl.ds(source, 1), :]
        return carry

    lax.fori_loop(0, (count + 15) // 16, move, 0)
    rows_out[0] = stage[...].astype(BF16)

    lines = capacity // 128
    shift = lax.rem(start, 128)
    window = ids[pl.ds(start // 128, 8), :]
    turned = pltpu.roll(window, lax.rem(128 - shift, 128), 1)
    lane = iota((lines, 128), 1)
    joined = jnp.where(lane < 128 - shift, turned[:lines], turned[1 : lines + 1])
    place = iota((lines, 128), 0) * 128 + lane
    ids_out[0] = jnp.where(place < count, joined - owner * seg_rows, seg_rows)


def pack(order, bounds, ids, cot, parts, capacity, seg_rows):
    rows_dev, width = cot.shape
    return pl.pallas_call(
        functools.partial(pack_kernel, capacity, seg_rows),
        grid_spec=pltpu.PrefetchScalarGridSpec(
            num_scalar_prefetch=2,
            grid=(parts,),
            in_specs=[
                pl.BlockSpec(ids.shape, lambda i, *_: (0, 0)),
                pl.BlockSpec(cot.shape, lambda i, *_: (0, 0)),
            ],
            out_specs=[
                pl.BlockSpec((1, capacity, width), lambda i, *_: (i, 0, 0)),
                pl.BlockSpec((1, capacity // 128, 128), lambda i, *_: (i, 0, 0)),
            ],
            scratch_shapes=[
                pltpu.VMEM((rows_dev, width), F32),
                pltpu.VMEM((capacity, width), F32),
            ],
        ),
        out_shape=[
            jax.ShapeDtypeStruct((parts, capacity, width), BF16),
            jax.ShapeDtypeStruct((parts, capacity // 128, 128), jnp.int32),
        ],
        compiler_params=pltpu.CompilerParams(vmem_limit_bytes=VMEM_LIMIT),
        name="pack_rows",
    )(order, bounds, ids, cot)


def hits(local, shift, same):
    rows = iota((128, 128), 0, F32)
    table = same
    for slot in range(4):
        wanted = local[slot : slot + 1, :] + shift
        hit = jnp.where(wanted == rows, 1.0, 0.0)
        table = hit if table is None else table + hit
    return table.astype(BF16)


def ends(links):
    lane = iota(links.shape, 1)
    return jnp.where(links != 0, links + lane, -100000).astype(F32)


def forward_kernel(links, feat, before, after, w_cat, bias, msg_out, hid_out, slope_out, ext, sem):
    step = pl.program_id(0)
    seg_rows, width = feat.shape

    @pl.when(step == 0)
    def _():
        ext[:, width:] = jnp.ones((ext.shape[0], width), BF16)
        for source, at, size in (
            (before, 0, HALO),
            (feat, HALO, seg_rows),
            (after, HALO + seg_rows, HALO),
        ):
            copy = pltpu.make_async_copy(source, ext.at[pl.ds(at, size), pl.ds(0, width)], sem)
            copy.start()
            copy.wait()

    same = jnp.where(iota((128, 128), 0) == iota((128, 128), 1), 1.0, 0.0)
    for j in range(STEP // 128):
        base = pl.multiple_of(step * STEP + j * 128, 128)
        local = ends(links[:, j * 128 : (j + 1) * 128])
        table = jnp.concatenate(
            [hits(local, 128.0, None), hits(local, 0.0, same), hits(local, -128.0, None)], axis=0
        )
        summed = dot(table, ext[pl.ds(base, 384), :], 0, 0)
        messages = summed[:, :width] / summed[:, width:]
        msg_out[j * 128 : (j + 1) * 128, :] = messages.astype(BF16)
    own = ext[pl.ds(pl.multiple_of(step * STEP + HALO, 128), STEP), :width]
    pre = dot(jnp.concatenate([own, msg_out[...]], axis=1), w_cat[...]) + bias[...]
    gate = sigmoid(pre)
    swish = pre * gate
    hid_out[...] = (own.astype(F32) + swish).astype(BF16)
    slope_out[...] = gate + swish * (1.0 - gate)


def forward(links, feat, before, after, w_cat, bias):
    seg_rows, width = feat.shape
    whole = lambda a: pl.BlockSpec(a.shape, lambda i: (0,) * a.ndim)
    rows = pl.BlockSpec((STEP, width), lambda i: (i, 0))
    return pl.pallas_call(
        forward_kernel,
        grid=(seg_rows // STEP,),
        in_specs=[
            pl.BlockSpec((4, STEP), lambda i: (0, i)),
            pl.BlockSpec(memory_space=pl.ANY),
            pl.BlockSpec(memory_space=pl.ANY),
            pl.BlockSpec(memory_space=pl.ANY),
            whole(w_cat),
            whole(bias),
        ],
        out_specs=[rows, rows, rows],
        out_shape=[
            jax.ShapeDtypeStruct((seg_rows, width), BF16),
            jax.ShapeDtypeStruct((seg_rows, width), BF16),
            jax.ShapeDtypeStruct((seg_rows, width), F32),
        ],
        scratch_shapes=[
            pltpu.VMEM((seg_rows + 2 * HALO, 2 * width), BF16),
            pltpu.SemaphoreType.DMA,
        ],
        compiler_params=pltpu.CompilerParams(vmem_limit_bytes=VMEM_LIMIT),
        cost_estimate=pl.CostEstimate(
            flops=seg_rows * 384 * 512, bytes_accessed=seg_rows * width * 12, transcendentals=0
        ),
        name="forward_messages",
    )(links, feat, before, after, w_cat, bias)


def encoder_kernel(
    ids,
    got,
    links,
    feat,
    msg,
    hid,
    slope_pre,
    gain,
    w_expand,
    w_expand_t,
    w_reduce_t,
    w_back,
    shared_out,
    direct_out,
    ge_out,
    gr_out,
    gs_out,
    small_out,
    landed,
    rows,
    names,
    table,
    table_s,
    stage,
    onehot,
    sem,
):
    step = pl.program_id(0)
    sources, capacity = ids.shape
    width = feat.shape[1]
    stride = capacity + WIN
    seg_rows = pl.num_programs(0) * STEP

    @pl.when(step == 0)
    def _():
        fetch = pltpu.make_async_copy(got, landed, sem)
        fetch.start()
        weights = jnp.where(
            iota((16, 128), 0) == 0, 128.0, jnp.where(iota((16, 128), 0) == 1, 1.0, 0.0)
        ).astype(BF16)
        bound = iota((1, 128), 1, F32) * float(GROUP)
        most = jnp.zeros((1, 128), F32)
        for s in range(sources):
            line = ids[s : s + 1, :]
            place = iota((16, capacity), 0)
            high = jnp.broadcast_to(line >> 7, (16, capacity))
            low = jnp.broadcast_to(line & 127, (16, capacity))
            digits = jnp.where(place == 0, high, jnp.where(place == 1, low, 0))
            column = dot(digits.astype(F32).astype(BF16), weights, 0, 0)
            names[s * stride : s * stride + capacity, :] = column
            names[s * stride + capacity : (s + 1) * stride, :] = jnp.full((WIN, 128), 1e6, F32)
            below = jnp.sum(jnp.where(column < bound, 1.0, 0.0), axis=0, keepdims=True)
            table[s : s + 1, :] = below.astype(jnp.int32)
            most = jnp.maximum(most, pltpu.roll(below, 127, 1) - below)
        table[sources : sources + 8, :] = jnp.broadcast_to(most, (8, 128)).astype(jnp.int32)
        to_scalar = pltpu.make_async_copy(table, table_s, sem)
        fetch.wait()
        to_scalar.start()
        for s in range(sources):
            rows[s * stride : s * stride + capacity, :] = landed[
                s * capacity : (s + 1) * capacity, :
            ].astype(F32)
            rows[s * stride + capacity : (s + 1) * stride, :] = jnp.zeros((WIN, 128), F32)
        to_scalar.wait()
        for total in (ge_out, gr_out, gs_out, small_out):
            total[...] = jnp.zeros_like(total)

    scale = gain[...]
    for j in range(STEP // GROUP):
        part = slice(j * GROUP, (j + 1) * GROUP)
        block = step * (STEP // GROUP) + j
        first = (block * GROUP).astype(F32)
        left = iota((WIN, 128), 1, F32) + first

        def collect(turn):
            for s in range(sources):
                at = jnp.minimum(table_s[s, block] + turn * WIN, capacity) + s * stride
                name = names[pl.ds(at, WIN), :]
                stage[s * WIN : (s + 1) * WIN, :] = rows[pl.ds(at, WIN), :].astype(BF16)
                onehot[s * WIN : (s + 1) * WIN, :128] = jnp.where(name == left, 1.0, 0.0).astype(
                    BF16
                )
                onehot[s * WIN : (s + 1) * WIN, 128:] = jnp.where(
                    name == left + 128.0, 1.0, 0.0
                ).astype(BF16)
            return dot(onehot[...], stage[...], 0, 0)

        turns = (table_s[sources, block] + (WIN - 1)) // WIN
        cot = lax.fori_loop(1, turns, lambda t, c: c + collect(t), collect(0))
        cot_low = cot.astype(BF16)
        values = hid[part, :].astype(F32)
        rate = lax.rsqrt(jnp.mean(values * values, axis=-1, keepdims=True) + 1e-06)
        unit = values * rate
        normed = (unit * scale).astype(BF16)
        inner = dot(normed, w_expand[...])
        gate = sigmoid(inner)
        swish = inner * gate
        gr_out[...] += dot(cot_low, swish.astype(BF16), 0, 0)
        slope = gate + swish * (1.0 - gate)
        back_inner = (dot(cot_low, w_reduce_t[...]) * slope).astype(BF16)
        ge_out[...] += dot(normed, back_inner, 0, 0)
        back_normed = dot(back_inner, w_expand_t[...])
        small_out[0:1, :] += jnp.sum(back_normed * unit, axis=0, keepdims=True)
        weighted = scale * back_normed
        mean = jnp.mean(weighted * unit, axis=-1, keepdims=True)
        back_hidden = cot + (weighted - unit * mean) * rate
        back_pre = back_hidden * slope_pre[part, :]
        low = back_pre.astype(BF16)
        small_out[1:2, :] += jnp.sum(low.astype(F32), axis=0, keepdims=True)
        gs_out[...] += dot(jnp.concatenate([feat[part, :], msg[part, :]], axis=1), low, 0, 0)
        both = dot(low, w_back[...])
        used = jnp.sum(jnp.where(links[:, part] != 0, 1.0, 0.0), axis=0, keepdims=True)
        used = jnp.broadcast_to(used, (16, GROUP)).astype(BF16)
        degree = 1.0 + dot(used, jnp.full((16, 128), 1.0 / 16.0, BF16), 0, 0)
        shared_out[part, :] = (both[:, :width] / degree).astype(BF16)
        direct_out[part, :] = back_hidden + both[:, width:]


def encoder(ids, got, links, feat, msg, hid, slope_pre, gain, w_expand, w_reduce, w_back):
    seg_rows, width = feat.shape
    sources, capacity = ids.shape
    hidden = w_expand.shape[1]
    stride = capacity + WIN
    whole = lambda shape: pl.BlockSpec(shape, lambda i: (0,) * len(shape))
    rows = pl.BlockSpec((STEP, width), lambda i: (i, 0))
    return pl.pallas_call(
        encoder_kernel,
        grid=(seg_rows // STEP,),
        in_specs=[
            whole(ids.shape),
            pl.BlockSpec(memory_space=pl.ANY),
            pl.BlockSpec((4, STEP), lambda i: (0, i)),
            rows,
            rows,
            rows,
            rows,
            whole((1, width)),
            whole((width, hidden)),
            whole((hidden, width)),
            whole((width, hidden)),
            whole((width, 2 * width)),
        ],
        out_specs=[
            rows,
            rows,
            whole((width, hidden)),
            whole((width, hidden)),
            whole((2 * width, width)),
            whole((8, width)),
        ],
        out_shape=[
            jax.ShapeDtypeStruct((seg_rows, width), BF16),
            jax.ShapeDtypeStruct((seg_rows, width), F32),
            jax.ShapeDtypeStruct((width, hidden), F32),
            jax.ShapeDtypeStruct((width, hidden), F32),
            jax.ShapeDtypeStruct((2 * width, width), F32),
            jax.ShapeDtypeStruct((8, width), F32),
        ],
        scratch_shapes=[
            pltpu.VMEM((sources * capacity, width), BF16),
            pltpu.VMEM((sources * stride, width), F32),
            pltpu.VMEM((sources * stride, 128), F32),
            pltpu.VMEM((sources + 8, 128), jnp.int32),
            pltpu.SMEM((sources + 8, 128), jnp.int32),
            pltpu.VMEM((sources * WIN, width), BF16),
            pltpu.VMEM((sources * WIN, GROUP), BF16),
            pltpu.SemaphoreType.DMA,
        ],
        compiler_params=pltpu.CompilerParams(vmem_limit_bytes=VMEM_LIMIT),
        cost_estimate=pl.CostEstimate(
            flops=seg_rows * width * hidden * 10, bytes_accessed=seg_rows * width * 20, transcendentals=0
        ),
        name="encoder_backward",
    )(ids, got, links, feat, msg, hid, slope_pre, gain, w_expand, w_expand.T, w_reduce.T, w_back)


def spread_kernel(links, shared, before, after, direct, out, ext, sem):
    step = pl.program_id(0)
    seg_rows, width = shared.shape

    @pl.when(step == 0)
    def _():
        for source, at, size in (
            (before, 0, HALO),
            (shared, HALO, seg_rows),
            (after, HALO + seg_rows, HALO),
        ):
            copy = pltpu.make_async_copy(source, ext.at[pl.ds(at, size), :], sem)
            copy.start()
            copy.wait()

    same = jnp.where(iota((128, 128), 0) == iota((128, 128), 1), 1.0, 0.0)
    for j in range(STEP // 128):
        base = pl.multiple_of(step * STEP + j * 128, 128)
        near = [
            ends(links[:, pl.ds(pl.multiple_of(base + k * 128, 128), 128)]) for k in range(3)
        ]
        table = jnp.concatenate(
            [hits(near[0], -128.0, None), hits(near[1], 0.0, same), hits(near[2], 128.0, None)],
            axis=1,
        )
        summed = dot(table, ext[pl.ds(base, 384), :])
        part = slice(j * 128, (j + 1) * 128)
        out[part, :] = (direct[part, :] + summed).astype(BF16)


def spread(links_ext, shared, before, after, direct):
    seg_rows, width = shared.shape
    rows = pl.BlockSpec((STEP, width), lambda i: (i, 0))
    return pl.pallas_call(
        spread_kernel,
        grid=(seg_rows // STEP,),
        in_specs=[
            pl.BlockSpec(links_ext.shape, lambda i: (0, 0)),
            pl.BlockSpec(memory_space=pl.ANY),
            pl.BlockSpec(memory_space=pl.ANY),
            pl.BlockSpec(memory_space=pl.ANY),
            rows,
        ],
        out_specs=rows,
        out_shape=jax.ShapeDtypeStruct((seg_rows, width), BF16),
        scratch_shapes=[
            pltpu.VMEM((seg_rows + 2 * HALO, width), BF16),
            pltpu.SemaphoreType.DMA,
        ],
        compiler_params=pltpu.CompilerParams(vmem_limit_bytes=VMEM_LIMIT),
        cost_estimate=pl.CostEstimate(
            flops=seg_rows * 384 * 256, bytes_accessed=seg_rows * width * 8, transcendentals=0
        ),
        name="spread_back",
    )(links_ext, shared, before, after, direct)


def per_device(
    features, edges, route, cotangent, w_self, w_neighbor, bias, gain, w_expand, w_reduce
):
    feat = features[0]
    links = edges[0].T
    seg_rows, width = feat.shape
    parts = lax.axis_size("dom")
    trip_ids = route[0].reshape(-1)
    rows_dev = trip_ids.shape[0]
    capacity = 2 * rows_dev // parts
    cot_rows = cotangent[0].reshape(rows_dev, width)

    bits = (rows_dev - 1).bit_length()
    keys = (trip_ids.astype(jnp.uint32) << bits) | jnp.arange(rows_dev, dtype=jnp.uint32)
    keys = lax.sort(keys)
    order = jnp.pad((keys & (rows_dev - 1)).astype(jnp.int32), (0, 128))
    sorted_ids = jnp.pad((keys >> bits).astype(jnp.int32).reshape(-1, 128), ((0, 8), (0, 0)))
    edges_of = jnp.arange(parts + 1, dtype=jnp.int32) * seg_rows
    bounds = jnp.sum((trip_ids[None, :] < edges_of[:, None]).astype(jnp.int32), axis=1)
    sent_rows, sent_ids = pack(order, bounds, sorted_ids, cot_rows, parts, capacity, seg_rows)
    got_ids = lax.all_to_all(sent_ids, "dom", split_axis=0, concat_axis=0, tiled=True)
    got_rows = lax.all_to_all(sent_rows, "dom", split_axis=0, concat_axis=0, tiled=True)

    feat_before, feat_after = neighbours(feat, 0, HALO)
    links_before, links_after = neighbours(links, 1, HALO)
    links_ext = jnp.concatenate([links_before, links, links_after], axis=1)
    msg, hid, slope_pre = forward(
        links,
        feat,
        feat_before,
        feat_after,
        jnp.concatenate([w_self, w_neighbor], axis=0),
        bias[None],
    )
    shared, direct, grad_expand, grad_reduce_t, grad_pair, small = encoder(
        got_ids.reshape(parts, capacity),
        got_rows.reshape(parts * capacity, width),
        links,
        feat,
        msg,
        hid,
        slope_pre,
        gain[None],
        w_expand,
        w_reduce,
        jnp.concatenate([w_neighbor.T, w_self.T], axis=1),
    )
    shared_before, shared_after = neighbours(shared, 0, HALO)
    grad_features = spread(links_ext, shared, shared_before, shared_after, direct)[None]

    tiles = lax.axis_size("rep")
    graph_scale = 1.0 / math.sqrt(tiles * parts * seg_rows)
    route_scale = 1.0 / math.sqrt(tiles * parts * rows_dev)
    grad_expand, grad_reduce_t, grad_pair, small = lax.psum(
        (grad_expand, grad_reduce_t, grad_pair, small), ("rep", "dom")
    )
    return (
        grad_features,
        grad_pair[:width] * graph_scale,
        grad_pair[width:] * graph_scale,
        small[1] * graph_scale,
        small[0] * route_scale,
        grad_expand * route_scale,
        grad_reduce_t.T * route_scale,
    )


def solution(mesh):
    return jax.shard_map(
        per_device,
        mesh=mesh,
        in_specs=(
            P("rep", "dom", None),
            P("rep", "dom", None),
            P("rep", "dom", None),
            P("rep", "dom", None, None),
            P(),
            P(),
            P(),
            P(),
            P(),
            P(),
        ),
        out_specs=(P("rep", "dom", None), P(), P(), P(), P(), P(), P()),
        check_vma=False,
    )
```

```python
import functools
import math

import jax
import jax.numpy as jnp
from jax import lax
from jax.experimental import pallas as pl
from jax.experimental.pallas import tpu as pltpu
from jax.sharding import PartitionSpec as P

HALO = 128
WIN = 16
GROUP = 256
STEP = 1024
F32 = jnp.float32
BF16 = jnp.bfloat16
VMEM_LIMIT = 56 * 1024 * 1024


def iota(shape, dim, dtype=jnp.int32):
    return lax.broadcasted_iota(jnp.int32, shape, dim).astype(dtype)


def dot(a, b, da=1, db=0):
    return lax.dot_general(a, b, (((da,), (db,)), ((), ())), preferred_element_type=F32)


def sigmoid(value):
    return 0.5 * jnp.tanh(0.5 * value) + 0.5


def neighbours(array, dim, width):
    size, length = lax.axis_size("dom"), array.shape[dim]
    up = [(i, i + 1) for i in range(size - 1)]
    down = [(j, i) for i, j in up]
    last = lax.slice_in_dim(array, length - width, length, axis=dim)
    first = lax.slice_in_dim(array, 0, width, axis=dim)
    return lax.ppermute(last, "dom", up), lax.ppermute(first, "dom", down)


def pack_kernel(capacity, seg_rows, order, bounds, ids, cot, rows_out, ids_out, rows, stage):
    owner = pl.program_id(0)
    chunk = 512

    @pl.when(owner == 0)
    def _():
        stage[...] = jnp.zeros_like(stage)

        @pl.loop(0, cot.shape[0] // chunk)
        def _(i):
            part = pl.ds(pl.multiple_of(i * chunk, chunk), chunk)
            rows[part, :] = cot[part, :].astype(F32)

    start = bounds[owner]
    count = bounds[owner + 1] - start

    def move(g, carry):
        base = pl.multiple_of(g * 16, 16)
        for j in range(16):
            source = order[start + base + j]
            stage[pl.ds(base + j, 1), :] = rows[pl.ds(source, 1), :]
        return carry

    lax.fori_loop(0, (count + 15) // 16, move, 0)
    rows_out[0] = stage[...].astype(BF16)

    lines = capacity // 128
    shift = lax.rem(start, 128)
    window = ids[pl.ds(start // 128, 8), :]
    turned = pltpu.roll(window, lax.rem(128 - shift, 128), 1)
    lane = iota((lines, 128), 1)
    joined = jnp.where(lane < 128 - shift, turned[:lines], turned[1 : lines + 1])
    place = iota((lines, 128), 0) * 128 + lane
    ids_out[0] = jnp.where(place < count, joined - owner * seg_rows, seg_rows)


def pack(order, bounds, ids, cot, parts, capacity, seg_rows):
    rows_dev, width = cot.shape
    return pl.pallas_call(
        functools.partial(pack_kernel, capacity, seg_rows),
        grid_spec=pltpu.PrefetchScalarGridSpec(
            num_scalar_prefetch=2,
            grid=(parts,),
            in_specs=[
                pl.BlockSpec(ids.shape, lambda i, *_: (0, 0)),
                pl.BlockSpec(cot.shape, lambda i, *_: (0, 0)),
            ],
            out_specs=[
                pl.BlockSpec((1, capacity, width), lambda i, *_: (i, 0, 0)),
                pl.BlockSpec((1, capacity // 128, 128), lambda i, *_: (i, 0, 0)),
            ],
            scratch_shapes=[
                pltpu.VMEM((rows_dev, width), F32),
                pltpu.VMEM((capacity, width), F32),
            ],
        ),
        out_shape=[
            jax.ShapeDtypeStruct((parts, capacity, width), BF16),
            jax.ShapeDtypeStruct((parts, capacity // 128, 128), jnp.int32),
        ],
        compiler_params=pltpu.CompilerParams(vmem_limit_bytes=VMEM_LIMIT),
        name="pack_rows",
    )(order, bounds, ids, cot)


def hits(local, shift, same):
    rows = iota((128, 128), 0, F32)
    table = same
    for slot in range(4):
        wanted = local[slot : slot + 1, :] + shift
        hit = jnp.where(wanted == rows, 1.0, 0.0)
        table = hit if table is None else table + hit
    return table.astype(BF16)


def ends(links):
    lane = iota(links.shape, 1)
    return jnp.where(links != 0, links + lane, -100000).astype(F32)


def forward_kernel(links, feat, before, after, w_cat, bias, msg_out, hid_out, slope_out, ext, sem):
    step = pl.program_id(0)
    seg_rows, width = feat.shape

    @pl.when(step == 0)
    def _():
        ext[:, width:] = jnp.ones((ext.shape[0], width), BF16)
        for source, at, size in (
            (before, 0, HALO),
            (feat, HALO, seg_rows),
            (after, HALO + seg_rows, HALO),
        ):
            copy = pltpu.make_async_copy(source, ext.at[pl.ds(at, size), pl.ds(0, width)], sem)
            copy.start()
            copy.wait()

    same = jnp.where(iota((128, 128), 0) == iota((128, 128), 1), 1.0, 0.0)
    for j in range(STEP // 128):
        base = pl.multiple_of(step * STEP + j * 128, 128)
        local = ends(links[:, j * 128 : (j + 1) * 128])
        table = jnp.concatenate(
            [hits(local, 128.0, None), hits(local, 0.0, same), hits(local, -128.0, None)], axis=0
        )
        summed = dot(table, ext[pl.ds(base, 384), :], 0, 0)
        messages = summed[:, :width] / summed[:, width:]
        msg_out[j * 128 : (j + 1) * 128, :] = messages.astype(BF16)
    own = ext[pl.ds(pl.multiple_of(step * STEP + HALO, 128), STEP), :width]
    pre = dot(jnp.concatenate([own, msg_out[...]], axis=1), w_cat[...]) + bias[...]
    gate = sigmoid(pre)
    swish = pre * gate
    hid_out[...] = (own.astype(F32) + swish).astype(BF16)
    slope_out[...] = gate + swish * (1.0 - gate)


def forward(links, feat, before, after, w_cat, bias):
    seg_rows, width = feat.shape
    whole = lambda a: pl.BlockSpec(a.shape, lambda i: (0,) * a.ndim)
    rows = pl.BlockSpec((STEP, width), lambda i: (i, 0))
    return pl.pallas_call(
        forward_kernel,
        grid=(seg_rows // STEP,),
        in_specs=[
            pl.BlockSpec((4, STEP), lambda i: (0, i)),
            pl.BlockSpec(memory_space=pl.ANY),
            pl.BlockSpec(memory_space=pl.ANY),
            pl.BlockSpec(memory_space=pl.ANY),
            whole(w_cat),
            whole(bias),
        ],
        out_specs=[rows, rows, rows],
        out_shape=[
            jax.ShapeDtypeStruct((seg_rows, width), BF16),
            jax.ShapeDtypeStruct((seg_rows, width), BF16),
            jax.ShapeDtypeStruct((seg_rows, width), F32),
        ],
        scratch_shapes=[
            pltpu.VMEM((seg_rows + 2 * HALO, 2 * width), BF16),
            pltpu.SemaphoreType.DMA,
        ],
        compiler_params=pltpu.CompilerParams(vmem_limit_bytes=VMEM_LIMIT),
        cost_estimate=pl.CostEstimate(
            flops=seg_rows * 384 * 512, bytes_accessed=seg_rows * width * 12, transcendentals=0
        ),
        name="forward_messages",
    )(links, feat, before, after, w_cat, bias)


def encoder_kernel(
    ids,
    got,
    links,
    feat,
    msg,
    hid,
    slope_pre,
    gain,
    w_expand,
    w_expand_t,
    w_reduce_t,
    w_back,
    shared_out,
    direct_out,
    ge_out,
    gr_out,
    gs_out,
    small_out,
    landed,
    rows,
    names,
    table,
    table_s,
    stage,
    onehot,
    sem,
):
    step = pl.program_id(0)
    sources, capacity = ids.shape
    width = feat.shape[1]
    stride = capacity + WIN
    seg_rows = pl.num_programs(0) * STEP

    @pl.when(step == 0)
    def _():
        fetch = pltpu.make_async_copy(got, landed, sem)
        fetch.start()
        weights = jnp.where(
            iota((16, 128), 0) == 0, 128.0, jnp.where(iota((16, 128), 0) == 1, 1.0, 0.0)
        ).astype(BF16)
        bound = iota((1, 128), 1, F32) * float(GROUP)
        most = jnp.zeros((1, 128), F32)
        for s in range(sources):
            line = ids[s : s + 1, :]
            place = iota((16, capacity), 0)
            high = jnp.broadcast_to(line >> 7, (16, capacity))
            low = jnp.broadcast_to(line & 127, (16, capacity))
            digits = jnp.where(place == 0, high, jnp.where(place == 1, low, 0))
            column = dot(digits.astype(F32).astype(BF16), weights, 0, 0)
            names[s * stride : s * stride + capacity, :] = column
            names[s * stride + capacity : (s + 1) * stride, :] = jnp.full((WIN, 128), 1e6, F32)
            below = jnp.sum(jnp.where(column < bound, 1.0, 0.0), axis=0, keepdims=True)
            table[s : s + 1, :] = below.astype(jnp.int32)
            most = jnp.maximum(most, pltpu.roll(below, 127, 1) - below)
        table[sources : sources + 8, :] = jnp.broadcast_to(most, (8, 128)).astype(jnp.int32)
        to_scalar = pltpu.make_async_copy(table, table_s, sem)
        fetch.wait()
        to_scalar.start()
        for s in range(sources):
            rows[s * stride : s * stride + capacity, :] = landed[
                s * capacity : (s + 1) * capacity, :
            ].astype(F32)
            rows[s * stride + capacity : (s + 1) * stride, :] = jnp.zeros((WIN, 128), F32)
        to_scalar.wait()
        for total in (ge_out, gr_out, gs_out, small_out):
            total[...] = jnp.zeros_like(total)

    scale = gain[...]
    for j in range(STEP // GROUP):
        part = slice(j * GROUP, (j + 1) * GROUP)
        block = step * (STEP // GROUP) + j
        first = (block * GROUP).astype(F32)
        left = iota((WIN, 128), 1, F32) + first

        def collect(turn):
            for s in range(sources):
                at = jnp.minimum(table_s[s, block] + turn * WIN, capacity) + s * stride
                name = names[pl.ds(at, WIN), :]
                stage[s * WIN : (s + 1) * WIN, :] = rows[pl.ds(at, WIN), :].astype(BF16)
                onehot[s * WIN : (s + 1) * WIN, :128] = jnp.where(name == left, 1.0, 0.0).astype(
                    BF16
                )
                onehot[s * WIN : (s + 1) * WIN, 128:] = jnp.where(
                    name == left + 128.0, 1.0, 0.0
                ).astype(BF16)
            return dot(onehot[...], stage[...], 0, 0)

        turns = (table_s[sources, block] + (WIN - 1)) // WIN
        cot = lax.fori_loop(1, turns, lambda t, c: c + collect(t), collect(0))
        cot_low = cot.astype(BF16)
        values = hid[part, :].astype(F32)
        rate = lax.rsqrt(jnp.mean(values * values, axis=-1, keepdims=True) + 1e-06)
        unit = values * rate
        normed = (unit * scale).astype(BF16)
        inner = dot(normed, w_expand[...])
        gate = sigmoid(inner)
        swish = inner * gate
        gr_out[...] += dot(cot_low, swish.astype(BF16), 0, 0)
        slope = gate + swish * (1.0 - gate)
        back_inner = (dot(cot_low, w_reduce_t[...]) * slope).astype(BF16)
        ge_out[...] += dot(normed, back_inner, 0, 0)
        back_normed = dot(back_inner, w_expand_t[...])
        small_out[0:1, :] += jnp.sum(back_normed * unit, axis=0, keepdims=True)
        weighted = scale * back_normed
        mean = jnp.mean(weighted * unit, axis=-1, keepdims=True)
        back_hidden = cot + (weighted - unit * mean) * rate
        back_pre = back_hidden * slope_pre[part, :]
        low = back_pre.astype(BF16)
        small_out[1:2, :] += jnp.sum(low.astype(F32), axis=0, keepdims=True)
        gs_out[...] += dot(jnp.concatenate([feat[part, :], msg[part, :]], axis=1), low, 0, 0)
        both = dot(low, w_back[...])
        used = jnp.sum(jnp.where(links[:, part] != 0, 1.0, 0.0), axis=0, keepdims=True)
        used = jnp.broadcast_to(used, (16, GROUP)).astype(BF16)
        degree = 1.0 + dot(used, jnp.full((16, 128), 1.0 / 16.0, BF16), 0, 0)
        shared_out[part, :] = (both[:, :width] / degree).astype(BF16)
        direct_out[part, :] = back_hidden + both[:, width:]


def encoder(ids, got, links, feat, msg, hid, slope_pre, gain, w_expand, w_reduce, w_back):
    seg_rows, width = feat.shape
    sources, capacity = ids.shape
    hidden = w_expand.shape[1]
    stride = capacity + WIN
    whole = lambda shape: pl.BlockSpec(shape, lambda i: (0,) * len(shape))
    rows = pl.BlockSpec((STEP, width), lambda i: (i, 0))
    return pl.pallas_call(
        encoder_kernel,
        grid=(seg_rows // STEP,),
        in_specs=[
            whole(ids.shape),
            pl.BlockSpec(memory_space=pl.ANY),
            pl.BlockSpec((4, STEP), lambda i: (0, i)),
            rows,
            rows,
            rows,
            rows,
            whole((1, width)),
            whole((width, hidden)),
            whole((hidden, width)),
            whole((width, hidden)),
            whole((width, 2 * width)),
        ],
        out_specs=[
            rows,
            rows,
            whole((width, hidden)),
            whole((width, hidden)),
            whole((2 * width, width)),
            whole((8, width)),
        ],
        out_shape=[
            jax.ShapeDtypeStruct((seg_rows, width), BF16),
            jax.ShapeDtypeStruct((seg_rows, width), F32),
            jax.ShapeDtypeStruct((width, hidden), F32),
            jax.ShapeDtypeStruct((width, hidden), F32),
            jax.ShapeDtypeStruct((2 * width, width), F32),
            jax.ShapeDtypeStruct((8, width), F32),
        ],
        scratch_shapes=[
            pltpu.VMEM((sources * capacity, width), BF16),
            pltpu.VMEM((sources * stride, width), F32),
            pltpu.VMEM((sources * stride, 128), F32),
            pltpu.VMEM((sources + 8, 128), jnp.int32),
            pltpu.SMEM((sources + 8, 128), jnp.int32),
            pltpu.VMEM((sources * WIN, width), BF16),
            pltpu.VMEM((sources * WIN, GROUP), BF16),
            pltpu.SemaphoreType.DMA,
        ],
        compiler_params=pltpu.CompilerParams(vmem_limit_bytes=VMEM_LIMIT),
        cost_estimate=pl.CostEstimate(
            flops=seg_rows * width * hidden * 10, bytes_accessed=seg_rows * width * 20, transcendentals=0
        ),
        name="encoder_backward",
    )(ids, got, links, feat, msg, hid, slope_pre, gain, w_expand, w_expand.T, w_reduce.T, w_back)


def spread_kernel(
    links,
    shared,
    direct,
    grad_expand,
    grad_reduce,
    grad_pair,
    small,
    out,
    expand_out,
    reduce_out,
    pair_out,
    small_out,
    ext,
    links_ext,
    mine,
    parts_in,
    part,
    tiles_in,
    whole,
    wholes_in,
    halo_send,
    halo_recv,
    part_send,
    part_recv,
    tile_send,
    tile_recv,
    whole_send,
    whole_recv,
    sem,
):
    step = pl.program_id(0)
    steps = pl.num_programs(0)
    seg_rows, width = shared.shape
    hidden = expand_out.shape[2]
    parts, tiles = parts_in.shape[0], tiles_in.shape[0]
    half = parts // 2
    me, tile = lax.axis_index("dom"), lax.axis_index("rep")
    right, left = lax.rem(me + 1, parts), lax.rem(me + parts - 1, parts)

    def remote(source, target, send, recv, device):
        return pltpu.make_async_remote_copy(
            src_ref=source,
            dst_ref=target,
            send_sem=send,
            recv_sem=recv,
            device_id=device,
            device_id_type=pl.DeviceIdType.MESH,
        )

    def halos():
        tail = pl.ds(seg_rows - HALO, HALO)
        head = pl.ds(0, HALO)
        far = pl.ds(seg_rows + HALO, HALO)
        for n, (source, target, device) in enumerate(
            (
                (shared.at[tail, :], ext.at[head, :], right),
                (shared.at[head, :], ext.at[far, :], left),
                (links.at[:, tail], links_ext.at[:, head], right),
                (links.at[:, head], links_ext.at[:, far], left),
            )
        ):
            yield remote(source, target, halo_send.at[n], halo_recv.at[n], (tile, device))

    def part_copy(k):
        to = lax.rem(me + k, parts)
        return remote(mine.at[to], parts_in.at[me], part_send.at[k], part_recv.at[me], (tile, to))

    def part_arrival(k):
        at = lax.rem(me + k, parts)
        return remote(mine.at[at], parts_in.at[at], part_send.at[k], part_recv.at[at], (tile, at))

    def tile_copy(k):
        to = lax.rem(tile + k, tiles)
        return remote(part, tiles_in.at[tile], tile_send.at[k], tile_recv.at[tile], (to, me))

    def tile_arrival(k):
        at = lax.rem(tile + k, tiles)
        return remote(part, tiles_in.at[at], tile_send.at[k], tile_recv.at[at], (at, me))

    def whole_copy(k):
        to = lax.rem(me + k, parts)
        return remote(whole, wholes_in.at[me], whole_send.at[k], whole_recv.at[me], (tile, to))

    def whole_arrival(k):
        at = lax.rem(me + k, parts)
        return remote(whole, wholes_in.at[at], whole_send.at[k], whole_recv.at[at], (tile, at))

    @pl.when(step == 0)
    def _():
        barrier = pltpu.get_barrier_semaphore()

        @pl.loop(1, parts)
        def _(k):
            to = lax.rem(me + k, parts)
            pl.semaphore_signal(
                barrier, inc=1, device_id=(tile, to), device_id_type=pl.DeviceIdType.MESH
            )

        for k in range(1, tiles):
            to = lax.rem(tile + k, tiles)
            pl.semaphore_signal(
                barrier, inc=1, device_id=(to, me), device_id_type=pl.DeviceIdType.MESH
            )
        pl.semaphore_wait(barrier, parts + tiles - 2)
        for copy in halos():
            copy.start()
        mine[:half, :, :hidden] = grad_expand[...].astype(BF16)
        mine[half:, :, :hidden] = grad_reduce[...].astype(BF16)
        mine[:, :, hidden : hidden + width] = grad_pair[...].astype(BF16)
        mine[:, :, hidden + width :] = jnp.broadcast_to(small[...][None], (parts, 8, width)).astype(
            BF16
        )
        @pl.loop(1, parts)
        def _(k):
            part_copy(k).start()

        local = pltpu.make_async_copy(shared, ext.at[pl.ds(HALO, seg_rows), :], sem.at[0])
        edges = pltpu.make_async_copy(links, links_ext.at[:, pl.ds(HALO, seg_rows)], sem.at[1])
        local.start()
        edges.start()
        local.wait()
        edges.wait()

    @pl.when(step == 5)
    def _():
        @pl.loop(1, parts)
        def _(k):
            part_arrival(k).wait_recv()

        parts_in[me] = mine[me]
        part[...] = lax.fori_loop(
            1,
            parts,
            lambda p, total: total + parts_in[p].astype(F32),
            parts_in[0].astype(F32),
        )
        for k in range(1, tiles):
            tile_copy(k).start()

    @pl.when(step == 8)
    def _():
        for k in range(1, tiles):
            tile_arrival(k).wait_recv()
        tiles_in[tile] = part[...]
        total = tiles_in[0]
        for t in range(1, tiles):
            total = total + tiles_in[t]
        whole[...] = total.astype(BF16)

        @pl.loop(1, parts)
        def _(k):
            whole_copy(k).start()

    @pl.when(step == steps - 2)
    def _():
        for copy in halos():
            copy.wait_recv()
        head, far = pl.ds(0, HALO), pl.ds(seg_rows + HALO, HALO)
        links_ext[:, head] = jnp.where(me > 0, links_ext[:, head], 0)
        links_ext[:, far] = jnp.where(me < parts - 1, links_ext[:, far], 0)

    at = lax.rem(step + 1, steps) * STEP
    same = jnp.where(iota((128, 128), 0) == iota((128, 128), 1), 1.0, 0.0)
    for j in range(STEP // 128):
        base = pl.multiple_of(at + j * 128, 128)
        near = [
            ends(links_ext[:, pl.ds(pl.multiple_of(base + k * 128, 128), 128)]) for k in range(3)
        ]
        table = jnp.concatenate(
            [hits(near[0], -128.0, None), hits(near[1], 0.0, same), hits(near[2], 128.0, None)],
            axis=1,
        )
        summed = dot(table, ext[pl.ds(base, 384), :])
        rows = slice(j * 128, (j + 1) * 128)
        out[rows, :] = (direct[rows, :] + summed).astype(BF16)

    @pl.when(step == steps - 1)
    def _():
        @pl.loop(1, parts)
        def _(k):
            whole_arrival(k).wait_recv()

        wholes_in[me] = whole[...]
        expand_out[...] = wholes_in[:half, :, :hidden].astype(F32)
        reduce_out[...] = wholes_in[half:, :, :hidden].astype(F32)
        pair_out[...] = wholes_in[:, :, hidden : hidden + width].astype(F32)
        small_out[...] = wholes_in[0, :, hidden + width :].astype(F32)
        for copy in halos():
            copy.wait_send()

        @pl.loop(1, parts)
        def _(k):
            part_copy(k).wait_send()
            whole_copy(k).wait_send()

        for k in range(1, tiles):
            tile_copy(k).wait_send()


def spread(links, shared, direct, grad_expand, grad_reduce, grad_pair, small):
    seg_rows, width = shared.shape
    hidden = grad_expand.shape[1]
    parts, tiles = lax.axis_size("dom"), lax.axis_size("rep")
    steps = seg_rows // STEP
    slab = hidden + 2 * width
    cut = lambda a: a.reshape(-1, 8, a.shape[1])
    grads = [cut(grad_expand), cut(grad_reduce), cut(grad_pair)]
    whole = lambda a: pl.BlockSpec(a.shape, lambda i: (0,) * a.ndim)
    rows = pl.BlockSpec((STEP, width), lambda i: (lax.rem(i + 1, steps), 0))
    dma = pltpu.SemaphoreType.DMA
    got = pl.pallas_call(
        spread_kernel,
        grid=(steps,),
        in_specs=[
            pl.BlockSpec(memory_space=pl.ANY),
            pl.BlockSpec(memory_space=pl.ANY),
            rows,
            *[whole(g) for g in grads],
            whole(small),
        ],
        out_specs=[rows, *[whole(g) for g in grads], whole(small)],
        out_shape=[
            jax.ShapeDtypeStruct((seg_rows, width), BF16),
            *[jax.ShapeDtypeStruct(g.shape, F32) for g in grads],
            jax.ShapeDtypeStruct(small.shape, F32),
        ],
        scratch_shapes=[
            pltpu.VMEM((seg_rows + 2 * HALO, width), BF16),
            pltpu.VMEM((4, seg_rows + 2 * HALO), jnp.int32),
            pltpu.VMEM((parts, 8, slab), BF16),
            pltpu.VMEM((parts, 8, slab), BF16),
            pltpu.VMEM((8, slab), F32),
            pltpu.VMEM((tiles, 8, slab), F32),
            pltpu.VMEM((8, slab), BF16),
            pltpu.VMEM((parts, 8, slab), BF16),
            dma((4,)),
            dma((4,)),
            dma((parts,)),
            dma((parts,)),
            dma((tiles,)),
            dma((tiles,)),
            dma((parts,)),
            dma((parts,)),
            dma((2,)),
        ],
        compiler_params=pltpu.CompilerParams(
            vmem_limit_bytes=VMEM_LIMIT, collective_id=1, has_side_effects=True
        ),
        cost_estimate=pl.CostEstimate(
            flops=seg_rows * 384 * 256, bytes_accessed=seg_rows * width * 8, transcendentals=0
        ),
        name="spread_back",
    )(links, shared, direct, *grads, small)
    return (
        got[0],
        got[1].reshape(grad_expand.shape),
        got[2].reshape(grad_reduce.shape),
        got[3].reshape(grad_pair.shape),
        got[4],
    )


def per_device(
    features, edges, route, cotangent, w_self, w_neighbor, bias, gain, w_expand, w_reduce
):
    feat = features[0]
    links = edges[0].T
    seg_rows, width = feat.shape
    parts = lax.axis_size("dom")
    trip_ids = route[0].reshape(-1)
    rows_dev = trip_ids.shape[0]
    capacity = 2 * rows_dev // parts
    cot_rows = cotangent[0].reshape(rows_dev, width)

    bits = (rows_dev - 1).bit_length()
    keys = (trip_ids.astype(jnp.uint32) << bits) | jnp.arange(rows_dev, dtype=jnp.uint32)
    keys = lax.sort(keys)
    order = jnp.pad((keys & (rows_dev - 1)).astype(jnp.int32), (0, 128))
    sorted_ids = jnp.pad((keys >> bits).astype(jnp.int32).reshape(-1, 128), ((0, 8), (0, 0)))
    edges_of = jnp.arange(parts + 1, dtype=jnp.int32) * seg_rows
    bounds = jnp.sum((trip_ids[None, :] < edges_of[:, None]).astype(jnp.int32), axis=1)
    sent_rows, sent_ids = pack(order, bounds, sorted_ids, cot_rows, parts, capacity, seg_rows)
    got_ids = lax.all_to_all(sent_ids, "dom", split_axis=0, concat_axis=0, tiled=True)
    got_rows = lax.all_to_all(sent_rows, "dom", split_axis=0, concat_axis=0, tiled=True)

    feat_before, feat_after = neighbours(feat, 0, HALO)
    msg, hid, slope_pre = forward(
        links,
        feat,
        feat_before,
        feat_after,
        jnp.concatenate([w_self, w_neighbor], axis=0),
        bias[None],
    )
    shared, direct, grad_expand, grad_reduce_t, grad_pair, small = encoder(
        got_ids.reshape(parts, capacity),
        got_rows.reshape(parts * capacity, width),
        links,
        feat,
        msg,
        hid,
        slope_pre,
        gain[None],
        w_expand,
        w_reduce,
        jnp.concatenate([w_neighbor.T, w_self.T], axis=1),
    )
    grad_features, grad_expand, grad_reduce_t, grad_pair, small = spread(
        links, shared, direct, grad_expand, grad_reduce_t, grad_pair, small
    )
    tiles = lax.axis_size("rep")
    graph_scale = 1.0 / math.sqrt(tiles * parts * seg_rows)
    route_scale = 1.0 / math.sqrt(tiles * parts * rows_dev)
    return (
        grad_features[None],
        grad_pair[:width] * graph_scale,
        grad_pair[width:] * graph_scale,
        small[1] * graph_scale,
        small[0] * route_scale,
        grad_expand * route_scale,
        grad_reduce_t.T * route_scale,
    )


def solution(mesh):
    return jax.shard_map(
        per_device,
        mesh=mesh,
        in_specs=(
            P("rep", "dom", None),
            P("rep", "dom", None),
            P("rep", "dom", None),
            P("rep", "dom", None, None),
            P(),
            P(),
            P(),
            P(),
            P(),
            P(),
        ),
        out_specs=(P("rep", "dom", None), P(), P(), P(), P(), P(), P()),
        check_vma=False,
    )
```

```python
import functools
import math

import jax
import jax.numpy as jnp
from jax import lax
from jax.experimental import pallas as pl
from jax.experimental.pallas import tpu as pltpu
from jax.sharding import PartitionSpec as P

HALO = 128
WIN = 32
GROUP = 512
CHUNK = 256
STEP = 1024
F32 = jnp.float32
BF16 = jnp.bfloat16
VMEM_LIMIT = 56 * 1024 * 1024


def iota(shape, dim, dtype=jnp.int32):
    return lax.broadcasted_iota(jnp.int32, shape, dim).astype(dtype)


def dot(a, b, da=1, db=0):
    return lax.dot_general(a, b, (((da,), (db,)), ((), ())), preferred_element_type=F32)


def sigmoid(value):
    return 0.5 * jnp.tanh(0.5 * value) + 0.5


def pack_kernel(capacity, seg_rows, order, bounds, ids, cot, rows_out, ids_out, rows, stage):
    owner = pl.program_id(0)
    chunk = 512

    @pl.when(owner == 0)
    def _():
        stage[...] = jnp.zeros_like(stage)

        @pl.loop(0, cot.shape[0] // chunk)
        def _(i):
            part = pl.ds(pl.multiple_of(i * chunk, chunk), chunk)
            rows[part, :] = cot[part, :].astype(F32)

    start = bounds[owner]
    count = bounds[owner + 1] - start

    def move(g, carry):
        base = pl.multiple_of(g * 16, 16)
        for j in range(16):
            source = order[start + base + j]
            stage[pl.ds(base + j, 1), :] = rows[pl.ds(source, 1), :]
        return carry

    lax.fori_loop(0, (count + 15) // 16, move, 0)
    rows_out[0] = stage[...].astype(BF16)

    lines = capacity // 128
    shift = lax.rem(start, 128)
    window = ids[pl.ds(start // 128, 8), :]
    turned = pltpu.roll(window, lax.rem(128 - shift, 128), 1)
    lane = iota((lines, 128), 1)
    joined = jnp.where(lane < 128 - shift, turned[:lines], turned[1 : lines + 1])
    place = iota((lines, 128), 0) * 128 + lane
    ids_out[0] = jnp.where(place < count, joined - owner * seg_rows, seg_rows)


def pack(order, bounds, ids, cot, parts, capacity, seg_rows):
    rows_dev, width = cot.shape
    return pl.pallas_call(
        functools.partial(pack_kernel, capacity, seg_rows),
        grid_spec=pltpu.PrefetchScalarGridSpec(
            num_scalar_prefetch=2,
            grid=(parts,),
            in_specs=[
                pl.BlockSpec(ids.shape, lambda i, *_: (0, 0)),
                pl.BlockSpec(cot.shape, lambda i, *_: (0, 0)),
            ],
            out_specs=[
                pl.BlockSpec((1, capacity, width), lambda i, *_: (i, 0, 0)),
                pl.BlockSpec((1, capacity // 128, 128), lambda i, *_: (i, 0, 0)),
            ],
            scratch_shapes=[
                pltpu.VMEM((rows_dev, width), F32),
                pltpu.VMEM((capacity, width), F32),
            ],
        ),
        out_shape=[
            jax.ShapeDtypeStruct((parts, capacity, width), BF16),
            jax.ShapeDtypeStruct((parts, capacity // 128, 128), jnp.int32),
        ],
        compiler_params=pltpu.CompilerParams(vmem_limit_bytes=VMEM_LIMIT),
        name="pack_rows",
    )(order, bounds, ids, cot)


def hits(local, shift, same):
    rows = iota((128, 128), 0, F32).astype(BF16)
    table = same
    for slot in range(4):
        wanted = jnp.broadcast_to(local[slot : slot + 1, :] + shift, (16, 128)).astype(BF16)
        wanted = jnp.concatenate([wanted] * 8, axis=0)
        hit = jnp.where(wanted == rows, jnp.ones((), BF16), jnp.zeros((), BF16))
        table = hit if table is None else table + hit
    return table


def identity():
    return jnp.where(iota((128, 128), 0) == iota((128, 128), 1), 1.0, 0.0).astype(BF16)


def ends(links):
    lane = iota(links.shape, 1)
    return jnp.where(links != 0, links + lane, -100000).astype(F32)


def normalised(hid):
    values = hid.astype(F32)
    rate = lax.rsqrt(jnp.mean(values * values, axis=-1, keepdims=True) + 1e-06)
    return values * rate, rate


def remote(source, target, send, recv, device):
    return pltpu.make_async_remote_copy(
        src_ref=source,
        dst_ref=target,
        send_sem=send,
        recv_sem=recv,
        device_id=device,
        device_id_type=pl.DeviceIdType.MESH,
    )


def greet(barrier, device):
    pl.semaphore_signal(barrier, inc=1, device_id=device, device_id_type=pl.DeviceIdType.MESH)


def forward_kernel(
    links,
    feat,
    sent_rows,
    sent_ids,
    w_cat,
    bias,
    gain,
    w_expand,
    msg_out,
    hid_out,
    slope_out,
    act_out,
    bend_out,
    got_rows,
    got_ids,
    ext,
    halo_send,
    halo_recv,
    rows_send,
    rows_recv,
    ids_send,
    ids_recv,
    sem,
):
    step = pl.program_id(0)
    steps = pl.num_programs(0)
    seg_rows, width = feat.shape
    parts = got_ids.shape[0]
    me, tile = lax.axis_index("dom"), lax.axis_index("rep")
    right, left = lax.rem(me + 1, parts), lax.rem(me + parts - 1, parts)

    def halos():
        tail, head = pl.ds(seg_rows - HALO, HALO), pl.ds(0, HALO)
        far, lanes = pl.ds(seg_rows + HALO, HALO), pl.ds(0, width)
        for n, (source, target, device) in enumerate(
            (
                (feat.at[tail, :], ext.at[head, lanes], right),
                (feat.at[head, :], ext.at[far, lanes], left),
            )
        ):
            yield remote(source, target, halo_send.at[n], halo_recv.at[n], (tile, device))

    def rows_copy(k):
        to = lax.rem(me + k, parts)
        return remote(sent_rows.at[to], got_rows.at[me], rows_send.at[k], rows_recv.at[me], (tile, to))

    def rows_arrival(k):
        at = lax.rem(me + k, parts)
        return remote(sent_rows.at[at], got_rows.at[at], rows_send.at[k], rows_recv.at[at], (tile, at))

    def ids_copy(k):
        to = lax.rem(me + k, parts)
        return remote(sent_ids.at[to], got_ids.at[me], ids_send.at[k], ids_recv.at[me], (tile, to))

    def ids_arrival(k):
        at = lax.rem(me + k, parts)
        return remote(sent_ids.at[at], got_ids.at[at], ids_send.at[k], ids_recv.at[at], (tile, at))

    def own_copies():
        yield pltpu.make_async_copy(sent_rows.at[me], got_rows.at[me], sem.at[1])
        yield pltpu.make_async_copy(sent_ids.at[me], got_ids.at[me], sem.at[2])

    @pl.when(step == 0)
    def _():
        barrier = pltpu.get_barrier_semaphore()

        @pl.loop(1, parts)
        def _(k):
            greet(barrier, (tile, lax.rem(me + k, parts)))

        pl.semaphore_wait(barrier, parts - 1)
        for copy in halos():
            copy.start()

        @pl.loop(1, parts)
        def _(k):
            ids_copy(k).start()
            rows_copy(k).start()

        local = pltpu.make_async_copy(
            feat, ext.at[pl.ds(HALO, seg_rows), pl.ds(0, width)], sem.at[0]
        )
        local.start()
        for copy in own_copies():
            copy.start()
        ext[:, width:] = jnp.ones((ext.shape[0], width), BF16)
        local.wait()

    @pl.when(step == steps - 2)
    def _():
        for copy in halos():
            copy.wait_recv()

    start = lax.rem(step + 1, steps) * STEP
    same = identity()
    for j in range(STEP // 128):
        base = pl.multiple_of(start + j * 128, 128)
        local = ends(links[:, j * 128 : (j + 1) * 128])
        table = jnp.concatenate(
            [hits(local, 128.0, None), hits(local, 0.0, same), hits(local, -128.0, None)], axis=0
        )
        summed = dot(table, ext[pl.ds(base, 384), :], 0, 0)
        messages = summed[:, :width] / summed[:, width:]
        msg_out[j * 128 : (j + 1) * 128, :] = messages.astype(BF16)
    own = ext[pl.ds(pl.multiple_of(start + HALO, 128), STEP), :width]
    pre = dot(jnp.concatenate([own, msg_out[...]], axis=1), w_cat[...]) + bias[...]
    gate = sigmoid(pre)
    swish = pre * gate
    hidden = (own.astype(F32) + swish).astype(BF16)
    hid_out[...] = hidden
    slope_out[...] = gate + swish * (1.0 - gate)
    unit, _ = normalised(hidden)
    normed = (unit * gain[...]).astype(BF16)
    for j in range(STEP // CHUNK):
        part = slice(j * CHUNK, (j + 1) * CHUNK)
        inner = dot(normed[part], w_expand[...])
        gate = sigmoid(inner)
        swish = inner * gate
        act_out[part, :] = swish.astype(BF16)
        bend_out[part, :] = (gate + swish * (1.0 - gate)).astype(BF16)

    @pl.when(step == steps - 1)
    def _():
        for copy in own_copies():
            copy.wait()
        for copy in halos():
            copy.wait_send()

        @pl.loop(1, parts)
        def _(k):
            ids_arrival(k).wait_recv()
            rows_arrival(k).wait_recv()
            ids_copy(k).wait_send()
            rows_copy(k).wait_send()


def forward(links, feat, sent_rows, sent_ids, w_cat, bias, gain, w_expand):
    seg_rows, width = feat.shape
    hidden = w_expand.shape[1]
    steps, parts = seg_rows // STEP, sent_ids.shape[0]
    whole = lambda a: pl.BlockSpec(a.shape, lambda i: (0,) * a.ndim)
    rows = lambda n: pl.BlockSpec((STEP, n), lambda i: (lax.rem(i + 1, steps), 0))
    away = pl.BlockSpec(memory_space=pl.ANY)
    dma = pltpu.SemaphoreType.DMA
    return pl.pallas_call(
        forward_kernel,
        grid=(steps,),
        in_specs=[
            pl.BlockSpec((4, STEP), lambda i: (0, lax.rem(i + 1, steps))),
            away,
            away,
            away,
            whole(w_cat),
            whole(bias),
            whole(gain),
            whole(w_expand),
        ],
        out_specs=[rows(width), rows(width), rows(width), rows(hidden), rows(hidden), away, away],
        out_shape=[
            jax.ShapeDtypeStruct((seg_rows, width), BF16),
            jax.ShapeDtypeStruct((seg_rows, width), BF16),
            jax.ShapeDtypeStruct((seg_rows, width), F32),
            jax.ShapeDtypeStruct((seg_rows, hidden), BF16),
            jax.ShapeDtypeStruct((seg_rows, hidden), BF16),
            jax.ShapeDtypeStruct(sent_rows.shape, BF16),
            jax.ShapeDtypeStruct(sent_ids.shape, jnp.int32),
        ],
        scratch_shapes=[
            pltpu.VMEM((seg_rows + 2 * HALO, 2 * width), BF16),
            dma((2,)),
            dma((2,)),
            dma((parts,)),
            dma((parts,)),
            dma((parts,)),
            dma((parts,)),
            dma((3,)),
        ],
        compiler_params=pltpu.CompilerParams(
            vmem_limit_bytes=VMEM_LIMIT, collective_id=2, has_side_effects=True
        ),
        cost_estimate=pl.CostEstimate(
            flops=seg_rows * 384 * 512, bytes_accessed=seg_rows * width * 12, transcendentals=0
        ),
        name="forward_messages",
    )(links, feat, sent_rows, sent_ids, w_cat, bias, gain, w_expand)


def encoder_kernel(
    ids,
    got,
    links,
    feat,
    msg,
    hid,
    slope_pre,
    act,
    bend,
    gain,
    w_expand_t,
    w_reduce_t,
    w_back,
    shared_out,
    direct_out,
    ge_out,
    gr_out,
    gs_out,
    small_out,
    landed,
    rows,
    names,
    table,
    table_s,
    stage,
    onehot,
    cot_s,
    low_s,
    inner_s,
    pair_s,
    sem,
):
    step = pl.program_id(0)
    sources, capacity = ids.shape
    width = feat.shape[1]
    stride = capacity + WIN
    seg_rows = pl.num_programs(0) * STEP

    @pl.when(step == 0)
    def _():
        fetch = pltpu.make_async_copy(got, landed, sem)
        fetch.start()
        weights = jnp.where(
            iota((16, 128), 0) == 0, 128.0, jnp.where(iota((16, 128), 0) == 1, 1.0, 0.0)
        ).astype(BF16)
        bound = iota((1, 128), 1, F32) * float(GROUP)
        most = jnp.zeros((1, 128), F32)
        for s in range(sources):
            line = ids[s : s + 1, :]
            place = iota((16, capacity), 0)
            high = jnp.broadcast_to(line >> 7, (16, capacity))
            low = jnp.broadcast_to(line & 127, (16, capacity))
            digits = jnp.where(place == 0, high, jnp.where(place == 1, low, 0))
            column = dot(digits.astype(F32).astype(BF16), weights, 0, 0)
            names[s * stride : s * stride + capacity, :] = column
            names[s * stride + capacity : (s + 1) * stride, :] = jnp.full((WIN, 128), 1e6, F32)
            below = jnp.sum(jnp.where(column < bound, 1.0, 0.0), axis=0, keepdims=True)
            table[s : s + 1, :] = below.astype(jnp.int32)
            most = jnp.maximum(most, pltpu.roll(below, 127, 1) - below)
        table[sources : sources + 8, :] = jnp.broadcast_to(most, (8, 128)).astype(jnp.int32)
        to_scalar = pltpu.make_async_copy(table, table_s, sem)
        fetch.wait()
        to_scalar.start()
        for s in range(sources):
            rows[s * stride : s * stride + capacity, :] = landed[
                s * capacity : (s + 1) * capacity, :
            ].astype(F32)
            rows[s * stride + capacity : (s + 1) * stride, :] = jnp.zeros((WIN, 128), F32)
        to_scalar.wait()
        for total in (ge_out, gr_out, pair_s, small_out):
            total[...] = jnp.zeros_like(total)

    def collect(block, turn):
        first = (block * GROUP).astype(F32)
        left = iota((WIN, 128), 1, F32) + first
        for s in range(sources):
            at = jnp.minimum(table_s[s, block] + turn * WIN, capacity) + s * stride
            name = names[pl.ds(at, WIN), :]
            stage[s * WIN : (s + 1) * WIN, :] = rows[pl.ds(at, WIN), :].astype(BF16)
            for k in range(GROUP // 128):
                onehot[s * WIN : (s + 1) * WIN, k * 128 : (k + 1) * 128] = jnp.where(
                    name == left + 128.0 * k, 1.0, 0.0
                ).astype(BF16)
        return dot(stage[...], onehot[...], 0, 0).T

    for j in range(STEP // GROUP):
        part = slice(j * GROUP, (j + 1) * GROUP)
        block = step * (STEP // GROUP) + j
        cot_s[part, :] = collect(block, 0)
        turns = (table_s[sources, block] + (WIN - 1)) // WIN

        @pl.when(turns > 1)
        def _():
            @pl.loop(1, turns)
            def _(turn):
                cot_s[part, :] += collect(block, turn)

    scale = gain[...]
    unit, rate = normalised(hid[...])
    normed = (unit * scale).astype(BF16)
    low_s[...] = cot_s[...].astype(BF16)
    for j in range(STEP // CHUNK):
        part = slice(j * CHUNK, (j + 1) * CHUNK)
        back_active = dot(low_s[part, :], w_reduce_t[...])
        inner_s[part, :] = (back_active * bend[part, :].astype(F32)).astype(BF16)
    gr_out[...] += dot(low_s[...], act[...], 0, 0)
    ge_out[...] += dot(normed, inner_s[...], 0, 0)
    back_normed = dot(inner_s[...], w_expand_t[...])
    small_out[0:1, :] += jnp.sum(back_normed * unit, axis=0, keepdims=True)
    weighted = scale * back_normed
    mean = jnp.mean(weighted * unit, axis=-1, keepdims=True)
    back_hidden = cot_s[...] + (weighted - unit * mean) * rate
    back_pre = back_hidden * slope_pre[...]
    low = back_pre.astype(BF16)
    small_out[1:2, :] += jnp.sum(low.astype(F32), axis=0, keepdims=True)
    pair_s[...] += dot(low, jnp.concatenate([feat[...], msg[...]], axis=1), 0, 0)
    both = dot(low, w_back[...])
    used = jnp.sum(jnp.where(links[...] != 0, 1.0, 0.0), axis=0, keepdims=True)
    used = jnp.broadcast_to(used, (16, STEP)).astype(BF16)
    degree = 1.0 + dot(used, jnp.full((16, 128), 1.0 / 16.0, BF16), 0, 0)
    shared_out[...] = (both[:, :width] / degree).astype(BF16)
    direct_out[...] = back_hidden + both[:, width:]

    @pl.when(step == pl.num_programs(0) - 1)
    def _():
        gs_out[...] = pair_s[...].T


def encoder(
    ids, got, links, feat, msg, hid, slope_pre, act, bend, gain, w_expand, w_reduce, w_back
):
    seg_rows, width = feat.shape
    sources, capacity = ids.shape
    hidden = w_expand.shape[1]
    stride = capacity + WIN
    whole = lambda shape: pl.BlockSpec(shape, lambda i: (0,) * len(shape))
    rows = pl.BlockSpec((STEP, width), lambda i: (i, 0))
    wide = pl.BlockSpec((STEP, hidden), lambda i: (i, 0))
    return pl.pallas_call(
        encoder_kernel,
        grid=(seg_rows // STEP,),
        in_specs=[
            whole(ids.shape),
            pl.BlockSpec(memory_space=pl.ANY),
            pl.BlockSpec((4, STEP), lambda i: (0, i)),
            rows,
            rows,
            rows,
            rows,
            wide,
            wide,
            whole((1, width)),
            whole((hidden, width)),
            whole((width, hidden)),
            whole((width, 2 * width)),
        ],
        out_specs=[
            rows,
            rows,
            whole((width, hidden)),
            whole((width, hidden)),
            whole((2 * width, width)),
            whole((8, width)),
        ],
        out_shape=[
            jax.ShapeDtypeStruct((seg_rows, width), BF16),
            jax.ShapeDtypeStruct((seg_rows, width), F32),
            jax.ShapeDtypeStruct((width, hidden), F32),
            jax.ShapeDtypeStruct((width, hidden), F32),
            jax.ShapeDtypeStruct((2 * width, width), F32),
            jax.ShapeDtypeStruct((8, width), F32),
        ],
        scratch_shapes=[
            pltpu.VMEM((sources * capacity, width), BF16),
            pltpu.VMEM((sources * stride, width), F32),
            pltpu.VMEM((sources * stride, 128), F32),
            pltpu.VMEM((sources + 8, 128), jnp.int32),
            pltpu.SMEM((sources + 8, 128), jnp.int32),
            pltpu.VMEM((sources * WIN, width), BF16),
            pltpu.VMEM((sources * WIN, GROUP), BF16),
            pltpu.VMEM((STEP, width), F32),
            pltpu.VMEM((STEP, width), BF16),
            pltpu.VMEM((STEP, hidden), BF16),
            pltpu.VMEM((width, 2 * width), F32),
            pltpu.SemaphoreType.DMA,
        ],
        compiler_params=pltpu.CompilerParams(vmem_limit_bytes=VMEM_LIMIT),
        cost_estimate=pl.CostEstimate(
            flops=seg_rows * width * hidden * 10, bytes_accessed=seg_rows * width * 20, transcendentals=0
        ),
        name="encoder_backward",
    )(
        ids, got, links, feat, msg, hid, slope_pre, act, bend, gain, w_expand.T, w_reduce.T, w_back
    )


def spread_kernel(
    links,
    shared,
    direct,
    grad_expand,
    grad_reduce,
    grad_pair,
    small,
    out,
    expand_out,
    reduce_out,
    pair_out,
    small_out,
    ext,
    links_ext,
    mine,
    parts_in,
    part,
    tiles_in,
    whole,
    wholes_in,
    halo_send,
    halo_recv,
    part_send,
    part_recv,
    tile_send,
    tile_recv,
    whole_send,
    whole_recv,
    sem,
):
    step = pl.program_id(0)
    steps = pl.num_programs(0)
    seg_rows, width = shared.shape
    hidden = expand_out.shape[2]
    parts, tiles = parts_in.shape[0], tiles_in.shape[0]
    half = parts // 2
    me, tile = lax.axis_index("dom"), lax.axis_index("rep")
    right, left = lax.rem(me + 1, parts), lax.rem(me + parts - 1, parts)

    def halos():
        tail = pl.ds(seg_rows - HALO, HALO)
        head = pl.ds(0, HALO)
        far = pl.ds(seg_rows + HALO, HALO)
        for n, (source, target, device) in enumerate(
            (
                (shared.at[tail, :], ext.at[head, :], right),
                (shared.at[head, :], ext.at[far, :], left),
                (links.at[:, tail], links_ext.at[:, head], right),
                (links.at[:, head], links_ext.at[:, far], left),
            )
        ):
            yield remote(source, target, halo_send.at[n], halo_recv.at[n], (tile, device))

    def part_copy(k):
        to = lax.rem(me + k, parts)
        return remote(mine.at[to], parts_in.at[me], part_send.at[k], part_recv.at[me], (tile, to))

    def part_arrival(k):
        at = lax.rem(me + k, parts)
        return remote(mine.at[at], parts_in.at[at], part_send.at[k], part_recv.at[at], (tile, at))

    def tile_copy(k):
        to = lax.rem(tile + k, tiles)
        return remote(part, tiles_in.at[tile], tile_send.at[k], tile_recv.at[tile], (to, me))

    def tile_arrival(k):
        at = lax.rem(tile + k, tiles)
        return remote(part, tiles_in.at[at], tile_send.at[k], tile_recv.at[at], (at, me))

    def whole_copy(k):
        to = lax.rem(me + k, parts)
        return remote(whole, wholes_in.at[me], whole_send.at[k], whole_recv.at[me], (tile, to))

    def whole_arrival(k):
        at = lax.rem(me + k, parts)
        return remote(whole, wholes_in.at[at], whole_send.at[k], whole_recv.at[at], (tile, at))

    @pl.when(step == 0)
    def _():
        barrier = pltpu.get_barrier_semaphore()

        @pl.loop(1, parts)
        def _(k):
            greet(barrier, (tile, lax.rem(me + k, parts)))

        for k in range(1, tiles):
            greet(barrier, (lax.rem(tile + k, tiles), me))
        pl.semaphore_wait(barrier, parts + tiles - 2)
        for copy in halos():
            copy.start()
        mine[:half, :, :hidden] = grad_expand[...].astype(BF16)
        mine[half:, :, :hidden] = grad_reduce[...].astype(BF16)
        mine[:, :, hidden : hidden + width] = grad_pair[...].astype(BF16)
        mine[:, :, hidden + width :] = jnp.broadcast_to(small[...][None], (parts, 8, width)).astype(
            BF16
        )
        @pl.loop(1, parts)
        def _(k):
            part_copy(k).start()

        local = pltpu.make_async_copy(shared, ext.at[pl.ds(HALO, seg_rows), :], sem.at[0])
        edges = pltpu.make_async_copy(links, links_ext.at[:, pl.ds(HALO, seg_rows)], sem.at[1])
        local.start()
        edges.start()
        local.wait()
        edges.wait()

    @pl.when(step == 5)
    def _():
        @pl.loop(1, parts)
        def _(k):
            part_arrival(k).wait_recv()

        parts_in[me] = mine[me]
        part[...] = lax.fori_loop(
            1,
            parts,
            lambda p, total: total + parts_in[p].astype(F32),
            parts_in[0].astype(F32),
        )
        for k in range(1, tiles):
            tile_copy(k).start()

    @pl.when(step == 8)
    def _():
        for k in range(1, tiles):
            tile_arrival(k).wait_recv()
        tiles_in[tile] = part[...]
        total = tiles_in[0]
        for t in range(1, tiles):
            total = total + tiles_in[t]
        whole[...] = total.astype(BF16)

        @pl.loop(1, parts)
        def _(k):
            whole_copy(k).start()

    @pl.when(step == steps - 2)
    def _():
        for copy in halos():
            copy.wait_recv()
        head, far = pl.ds(0, HALO), pl.ds(seg_rows + HALO, HALO)
        links_ext[:, head] = jnp.where(me > 0, links_ext[:, head], 0)
        links_ext[:, far] = jnp.where(me < parts - 1, links_ext[:, far], 0)

    at = lax.rem(step + 1, steps) * STEP
    same = identity()
    for j in range(STEP // 128):
        base = pl.multiple_of(at + j * 128, 128)
        near = [
            ends(links_ext[:, pl.ds(pl.multiple_of(base + k * 128, 128), 128)]) for k in range(3)
        ]
        table = jnp.concatenate(
            [hits(near[0], -128.0, None), hits(near[1], 0.0, same), hits(near[2], 128.0, None)],
            axis=1,
        )
        summed = dot(table, ext[pl.ds(base, 384), :])
        rows = slice(j * 128, (j + 1) * 128)
        out[rows, :] = (direct[rows, :] + summed).astype(BF16)

    @pl.when(step == steps - 1)
    def _():
        @pl.loop(1, parts)
        def _(k):
            whole_arrival(k).wait_recv()

        wholes_in[me] = whole[...]
        expand_out[...] = wholes_in[:half, :, :hidden].astype(F32)
        reduce_out[...] = wholes_in[half:, :, :hidden].astype(F32)
        pair_out[...] = wholes_in[:, :, hidden : hidden + width].astype(F32)
        small_out[...] = wholes_in[0, :, hidden + width :].astype(F32)
        for copy in halos():
            copy.wait_send()

        @pl.loop(1, parts)
        def _(k):
            part_copy(k).wait_send()
            whole_copy(k).wait_send()

        for k in range(1, tiles):
            tile_copy(k).wait_send()


def spread(links, shared, direct, grad_expand, grad_reduce, grad_pair, small):
    seg_rows, width = shared.shape
    hidden = grad_expand.shape[1]
    parts, tiles = lax.axis_size("dom"), lax.axis_size("rep")
    steps = seg_rows // STEP
    slab = hidden + 2 * width
    cut = lambda a: a.reshape(-1, 8, a.shape[1])
    grads = [cut(grad_expand), cut(grad_reduce), cut(grad_pair)]
    whole = lambda a: pl.BlockSpec(a.shape, lambda i: (0,) * a.ndim)
    rows = pl.BlockSpec((STEP, width), lambda i: (lax.rem(i + 1, steps), 0))
    dma = pltpu.SemaphoreType.DMA
    got = pl.pallas_call(
        spread_kernel,
        grid=(steps,),
        in_specs=[
            pl.BlockSpec(memory_space=pl.ANY),
            pl.BlockSpec(memory_space=pl.ANY),
            rows,
            *[whole(g) for g in grads],
            whole(small),
        ],
        out_specs=[rows, *[whole(g) for g in grads], whole(small)],
        out_shape=[
            jax.ShapeDtypeStruct((seg_rows, width), BF16),
            *[jax.ShapeDtypeStruct(g.shape, F32) for g in grads],
            jax.ShapeDtypeStruct(small.shape, F32),
        ],
        scratch_shapes=[
            pltpu.VMEM((seg_rows + 2 * HALO, width), BF16),
            pltpu.VMEM((4, seg_rows + 2 * HALO), jnp.int32),
            pltpu.VMEM((parts, 8, slab), BF16),
            pltpu.VMEM((parts, 8, slab), BF16),
            pltpu.VMEM((8, slab), F32),
            pltpu.VMEM((tiles, 8, slab), F32),
            pltpu.VMEM((8, slab), BF16),
            pltpu.VMEM((parts, 8, slab), BF16),
            dma((4,)),
            dma((4,)),
            dma((parts,)),
            dma((parts,)),
            dma((tiles,)),
            dma((tiles,)),
            dma((parts,)),
            dma((parts,)),
            dma((2,)),
        ],
        compiler_params=pltpu.CompilerParams(
            vmem_limit_bytes=VMEM_LIMIT, collective_id=1, has_side_effects=True
        ),
        cost_estimate=pl.CostEstimate(
            flops=seg_rows * 384 * 256, bytes_accessed=seg_rows * width * 8, transcendentals=0
        ),
        name="spread_back",
    )(links, shared, direct, *grads, small)
    return (
        got[0],
        got[1].reshape(grad_expand.shape),
        got[2].reshape(grad_reduce.shape),
        got[3].reshape(grad_pair.shape),
        got[4],
    )


def per_device(
    features, edges, route, cotangent, w_self, w_neighbor, bias, gain, w_expand, w_reduce
):
    feat = features[0]
    links = edges[0].T
    seg_rows, width = feat.shape
    parts = lax.axis_size("dom")
    trip_ids = route[0].reshape(-1)
    rows_dev = trip_ids.shape[0]
    capacity = 2 * rows_dev // parts
    cot_rows = cotangent[0].reshape(rows_dev, width)

    bits = (rows_dev - 1).bit_length()
    keys = (trip_ids.astype(jnp.uint32) << bits) | jnp.arange(rows_dev, dtype=jnp.uint32)
    keys = lax.sort(keys)
    order = jnp.pad((keys & (rows_dev - 1)).astype(jnp.int32), (0, 128))
    sorted_ids = jnp.pad((keys >> bits).astype(jnp.int32).reshape(-1, 128), ((0, 8), (0, 0)))
    edges_of = jnp.arange(parts + 1, dtype=jnp.int32) * seg_rows
    bounds = jnp.sum((trip_ids[None, :] < edges_of[:, None]).astype(jnp.int32), axis=1)
    sent_rows, sent_ids = pack(order, bounds, sorted_ids, cot_rows, parts, capacity, seg_rows)
    msg, hid, slope_pre, act, bend, got_rows, got_ids = forward(
        links,
        feat,
        sent_rows,
        sent_ids,
        jnp.concatenate([w_self, w_neighbor], axis=0),
        bias[None],
        gain[None],
        w_expand,
    )
    shared, direct, grad_expand, grad_reduce_t, grad_pair, small = encoder(
        got_ids.reshape(parts, capacity),
        got_rows.reshape(parts * capacity, width),
        links,
        feat,
        msg,
        hid,
        slope_pre,
        act,
        bend,
        gain[None],
        w_expand,
        w_reduce,
        jnp.concatenate([w_neighbor.T, w_self.T], axis=1),
    )
    grad_features, grad_expand, grad_reduce_t, grad_pair, small = spread(
        links, shared, direct, grad_expand, grad_reduce_t, grad_pair, small
    )
    tiles = lax.axis_size("rep")
    graph_scale = 1.0 / math.sqrt(tiles * parts * seg_rows)
    route_scale = 1.0 / math.sqrt(tiles * parts * rows_dev)
    return (
        grad_features[None],
        grad_pair[:width] * graph_scale,
        grad_pair[width:] * graph_scale,
        small[1] * graph_scale,
        small[0] * route_scale,
        grad_expand * route_scale,
        grad_reduce_t.T * route_scale,
    )


def solution(mesh):
    return jax.shard_map(
        per_device,
        mesh=mesh,
        in_specs=(
            P("rep", "dom", None),
            P("rep", "dom", None),
            P("rep", "dom", None),
            P("rep", "dom", None, None),
            P(),
            P(),
            P(),
            P(),
            P(),
            P(),
        ),
        out_specs=(P("rep", "dom", None), P(), P(), P(), P(), P(), P()),
        check_vma=False,
    )
```

```python
import functools
import math

import jax
import jax.numpy as jnp
from jax import lax
from jax.experimental import pallas as pl
from jax.experimental.pallas import tpu as pltpu
from jax.sharding import PartitionSpec as P

HALO = 128
WIN = 32
GROUP = 512
CHUNK = 256
OWNERS = 4
ROUTE = (
    (2, 1), (1, 2), (2, 3), (3, 2), (2, 2), (0, 2), (2, 0), (1, 1),
    (3, 3), (1, 3), (3, 1), (0, 1), (1, 0), (0, 3), (3, 0),
)
SIDE = 4
STEP = 1024
F32 = jnp.float32
BF16 = jnp.bfloat16
VMEM_LIMIT = 56 * 1024 * 1024


def iota(shape, dim, dtype=jnp.int32):
    return lax.broadcasted_iota(jnp.int32, shape, dim).astype(dtype)


def dot(a, b, da=1, db=0):
    return lax.dot_general(a, b, (((da,), (db,)), ((), ())), preferred_element_type=F32)


def sigmoid(value):
    return 0.5 * jnp.tanh(0.5 * value) + 0.5


def pack_kernel(capacity, seg_rows, order, bounds, ids, cot, rows_out, ids_out, rows, stage):
    turn = pl.program_id(0)
    chunk = 512

    @pl.when(turn == 0)
    def _():
        stage[...] = jnp.zeros_like(stage)

        @pl.loop(0, cot.shape[0] // chunk)
        def _(i):
            part = pl.ds(pl.multiple_of(i * chunk, chunk), chunk)
            rows[part, :] = cot[part, :].astype(F32)

    for n in range(OWNERS):
        owner = turn * OWNERS + n
        start = bounds[owner]
        count = bounds[owner + 1] - start
        at = n * capacity

        def move(g, carry):
            base = pl.multiple_of(g * 16, 16)
            for j in range(16):
                source = order[start + base + j]
                stage[pl.ds(base + (at + j), 1), :] = rows[pl.ds(source, 1), :]
            return carry

        lax.fori_loop(0, (count + 15) // 16, move, 0)
        rows_out[n] = stage[at : at + capacity, :].astype(BF16)

        lines = capacity // 128
        shift = lax.rem(start, 128)
        window = ids[pl.ds(start // 128, 8), :]
        turned = pltpu.roll(window, lax.rem(128 - shift, 128), 1)
        lane = iota((lines, 128), 1)
        joined = jnp.where(lane < 128 - shift, turned[:lines], turned[1 : lines + 1])
        place = iota((lines, 128), 0) * 128 + lane
        ids_out[n] = jnp.where(place < count, joined - owner * seg_rows, seg_rows)


def pack(order, bounds, ids, cot, parts, capacity, seg_rows):
    rows_dev, width = cot.shape
    return pl.pallas_call(
        functools.partial(pack_kernel, capacity, seg_rows),
        grid_spec=pltpu.PrefetchScalarGridSpec(
            num_scalar_prefetch=2,
            grid=(parts // OWNERS,),
            in_specs=[
                pl.BlockSpec(ids.shape, lambda i, *_: (0, 0)),
                pl.BlockSpec(cot.shape, lambda i, *_: (0, 0)),
            ],
            out_specs=[
                pl.BlockSpec((OWNERS, capacity, width), lambda i, *_: (i, 0, 0)),
                pl.BlockSpec((OWNERS, capacity // 128, 128), lambda i, *_: (i, 0, 0)),
            ],
            scratch_shapes=[
                pltpu.VMEM((rows_dev, width), F32),
                pltpu.VMEM((OWNERS * capacity, width), F32),
            ],
        ),
        out_shape=[
            jax.ShapeDtypeStruct((parts, capacity, width), BF16),
            jax.ShapeDtypeStruct((parts, capacity // 128, 128), jnp.int32),
        ],
        compiler_params=pltpu.CompilerParams(vmem_limit_bytes=VMEM_LIMIT),
        name="pack_rows",
    )(order, bounds, ids, cot)


def hits(local, shift, same):
    rows = iota((128, 128), 0, F32).astype(BF16)
    table = same
    for slot in range(4):
        wanted = jnp.broadcast_to(local[slot : slot + 1, :] + shift, (16, 128)).astype(BF16)
        wanted = jnp.concatenate([wanted] * 8, axis=0)
        hit = jnp.where(wanted == rows, jnp.ones((), BF16), jnp.zeros((), BF16))
        table = hit if table is None else table + hit
    return table


def identity():
    return jnp.where(iota((128, 128), 0) == iota((128, 128), 1), 1.0, 0.0).astype(BF16)


def ends(links):
    lane = iota(links.shape, 1)
    return jnp.where(links != 0, links + lane, -100000).astype(F32)


def normalised(hid):
    values = hid.astype(F32)
    rate = lax.rsqrt(jnp.mean(values * values, axis=-1, keepdims=True) + 1e-06)
    return values * rate, rate


def remote(source, target, send, recv, device):
    return pltpu.make_async_remote_copy(
        src_ref=source,
        dst_ref=target,
        send_sem=send,
        recv_sem=recv,
        device_id=device,
        device_id_type=pl.DeviceIdType.MESH,
    )


def greet(barrier, device):
    pl.semaphore_signal(barrier, inc=1, device_id=device, device_id_type=pl.DeviceIdType.MESH)


def forward_kernel(
    links,
    feat,
    sent_rows,
    sent_ids,
    w_self,
    w_neighbor,
    bias,
    gain,
    w_expand,
    msg_out,
    hid_out,
    slope_out,
    act_out,
    bend_out,
    table_out,
    got_rows,
    got_ids,
    names_out,
    ext,
    w_cat,
    ids,
    names,
    halo_send,
    halo_recv,
    rows_send,
    rows_recv,
    ids_send,
    ids_recv,
    sem,
):
    step = pl.program_id(0)
    steps = pl.num_programs(0)
    seg_rows, width = feat.shape
    parts = got_ids.shape[0]
    me, tile = lax.axis_index("dom"), lax.axis_index("rep")
    right, left = lax.rem(me + 1, parts), lax.rem(me + parts - 1, parts)

    def halos():
        tail, head = pl.ds(seg_rows - HALO, HALO), pl.ds(0, HALO)
        far, lanes = pl.ds(seg_rows + HALO, HALO), pl.ds(0, width)
        for n, (source, target, device) in enumerate(
            (
                (feat.at[tail, :], ext.at[head, lanes], right),
                (feat.at[head, :], ext.at[far, lanes], left),
            )
        ):
            yield remote(source, target, halo_send.at[n], halo_recv.at[n], (tile, device))

    def rows_copy(to):
        return remote(sent_rows.at[to], got_rows.at[me], rows_send.at[to], rows_recv.at[me], (tile, to))

    def rows_arrival(at):
        return remote(sent_rows.at[at], got_rows.at[at], rows_send.at[at], rows_recv.at[at], (tile, at))

    def ids_copy(to):
        return remote(sent_ids.at[to], got_ids.at[me], ids_send.at[to], ids_recv.at[me], (tile, to))

    def ids_arrival(at):
        return remote(sent_ids.at[at], got_ids.at[at], ids_send.at[at], ids_recv.at[at], (tile, at))

    def chip(down, along, swap):
        y, x, core = me // (2 * SIDE), lax.rem(me // 2, SIDE), lax.rem(me, 2)
        there = lax.rem(y + down, SIDE) * SIDE + lax.rem(x + along, SIDE)
        return there * 2 + lax.rem(core + swap, 2)

    def own_copies():
        yield pltpu.make_async_copy(sent_rows.at[me], got_rows.at[me], sem.at[1])
        yield pltpu.make_async_copy(sent_ids.at[me], got_ids.at[me], sem.at[2])

    @pl.when(step == 0)
    def _():
        barrier = pltpu.get_barrier_semaphore()

        @pl.loop(1, parts)
        def _(k):
            greet(barrier, (tile, lax.rem(me + k, parts)))

        pl.semaphore_wait(barrier, parts - 1)
        for copy in halos():
            copy.start()

        @pl.loop(1, parts)
        def _(k):
            ids_copy(lax.rem(me + k, parts)).start()

        for swap in range(2):
            for down, along in ROUTE:
                rows_copy(chip(down, along, swap)).start()
        rows_copy(chip(0, 0, 1)).start()
        local = pltpu.make_async_copy(
            feat, ext.at[pl.ds(HALO, seg_rows), pl.ds(0, width)], sem.at[0]
        )
        local.start()
        for copy in own_copies():
            copy.start()
        ext[:, width:] = jnp.ones((ext.shape[0], width), BF16)
        w_cat[:width, :] = w_self[...]
        w_cat[width:, :] = w_neighbor[...]
        local.wait()

    @pl.when(step == steps - 2)
    def _():
        for copy in halos():
            copy.wait_recv()

    start = lax.rem(step + 1, steps) * STEP
    same = identity()
    for j in range(STEP // 128):
        base = pl.multiple_of(start + j * 128, 128)
        local = ends(links[:, j * 128 : (j + 1) * 128])
        table = jnp.concatenate(
            [hits(local, 128.0, None), hits(local, 0.0, same), hits(local, -128.0, None)], axis=0
        )
        summed = dot(table, ext[pl.ds(base, 384), :], 0, 0)
        messages = summed[:, :width] / summed[:, width:]
        msg_out[j * 128 : (j + 1) * 128, :] = messages.astype(BF16)
    own = ext[pl.ds(pl.multiple_of(start + HALO, 128), STEP), :width]
    pre = dot(jnp.concatenate([own, msg_out[...]], axis=1), w_cat[...]) + bias[...]
    gate = sigmoid(pre)
    swish = pre * gate
    hidden = (own.astype(F32) + swish).astype(BF16)
    hid_out[...] = hidden
    slope_out[...] = gate + swish * (1.0 - gate)
    unit, _ = normalised(hidden)
    normed = (unit * gain[...]).astype(BF16)
    for j in range(STEP // CHUNK):
        part = slice(j * CHUNK, (j + 1) * CHUNK)
        inner = dot(normed[part], w_expand[...])
        gate = sigmoid(inner)
        swish = inner * gate
        act_out[part, :] = swish.astype(BF16)
        bend_out[part, :] = (gate + swish * (1.0 - gate)).astype(BF16)

    @pl.when(step == steps - 1)
    def _():
        for copy in own_copies():
            copy.wait()

        @pl.loop(1, parts)
        def _(k):
            ids_arrival(lax.rem(me + k, parts)).wait_recv()

        fetch = pltpu.make_async_copy(got_ids, ids, sem.at[0])
        fetch.start()
        fetch.wait()
        capacity = ids.shape[1] * 128
        stride = capacity + WIN
        place = iota((16, 128), 0)
        weights = jnp.where(place == 0, 128.0, jnp.where(place == 1, 1.0, 0.0)).astype(BF16)
        bound = iota((1, 128), 1, F32) * float(GROUP)
        most = jnp.zeros((1, 128), F32)
        for s in range(parts):
            below = jnp.zeros((1, 128), F32)
            for k in range(ids.shape[1]):
                line = ids[s, k : k + 1, :]
                high = jnp.broadcast_to(line >> 7, (16, 128))
                low = jnp.broadcast_to(line & 127, (16, 128))
                digits = jnp.where(place == 0, high, jnp.where(place == 1, low, 0))
                column = dot(digits.astype(F32).astype(BF16), weights, 0, 0)
                at = s * stride + k * 128
                names[at : at + 128, :] = column
                below += jnp.sum(jnp.where(column < bound, 1.0, 0.0), axis=0, keepdims=True)
            names[s * stride + capacity : (s + 1) * stride, :] = jnp.full((WIN, 128), 1e6, F32)
            table_out[s : s + 1, :] = below.astype(jnp.int32)
            most = jnp.maximum(most, pltpu.roll(below, 127, 1) - below)
        table_out[parts : parts + 8, :] = jnp.broadcast_to(most, (8, 128)).astype(jnp.int32)
        store = pltpu.make_async_copy(names, names_out, sem.at[0])
        store.start()
        for copy in halos():
            copy.wait_send()

        @pl.loop(1, parts)
        def _(k):
            other = lax.rem(me + k, parts)
            rows_arrival(other).wait_recv()
            ids_copy(other).wait_send()
            rows_copy(other).wait_send()

        store.wait()


def forward(links, feat, sent_rows, sent_ids, w_self, w_neighbor, bias, gain, w_expand):
    seg_rows, width = feat.shape
    hidden = w_expand.shape[1]
    steps, parts = seg_rows // STEP, sent_ids.shape[0]
    columns = parts * (sent_rows.shape[1] + WIN)
    whole = lambda a: pl.BlockSpec(a.shape, lambda i: (0,) * a.ndim)
    rows = lambda n: pl.BlockSpec((STEP, n), lambda i: (lax.rem(i + 1, steps), 0))
    away = pl.BlockSpec(memory_space=pl.ANY)
    dma = pltpu.SemaphoreType.DMA
    return pl.pallas_call(
        forward_kernel,
        grid=(steps,),
        in_specs=[
            pl.BlockSpec((4, STEP), lambda i: (0, lax.rem(i + 1, steps))),
            away,
            away,
            away,
            whole(w_self),
            whole(w_neighbor),
            whole(bias),
            whole(gain),
            whole(w_expand),
        ],
        out_specs=[
            rows(width),
            rows(width),
            rows(width),
            rows(hidden),
            rows(hidden),
            pl.BlockSpec((parts + 8, 128), lambda i: (0, 0)),
            away,
            away,
            away,
        ],
        out_shape=[
            jax.ShapeDtypeStruct((seg_rows, width), BF16),
            jax.ShapeDtypeStruct((seg_rows, width), BF16),
            jax.ShapeDtypeStruct((seg_rows, width), F32),
            jax.ShapeDtypeStruct((seg_rows, hidden), BF16),
            jax.ShapeDtypeStruct((seg_rows, hidden), BF16),
            jax.ShapeDtypeStruct((parts + 8, 128), jnp.int32),
            jax.ShapeDtypeStruct(sent_rows.shape, BF16),
            jax.ShapeDtypeStruct(sent_ids.shape, jnp.int32),
            jax.ShapeDtypeStruct((columns, 128), F32),
        ],
        scratch_shapes=[
            pltpu.VMEM((seg_rows + 2 * HALO, 2 * width), BF16),
            pltpu.VMEM((2 * width, width), BF16),
            pltpu.VMEM(sent_ids.shape, jnp.int32),
            pltpu.VMEM((columns, 128), F32),
            dma((2,)),
            dma((2,)),
            dma((parts,)),
            dma((parts,)),
            dma((parts,)),
            dma((parts,)),
            dma((3,)),
        ],
        compiler_params=pltpu.CompilerParams(
            vmem_limit_bytes=VMEM_LIMIT, collective_id=2, has_side_effects=True
        ),
        cost_estimate=pl.CostEstimate(
            flops=seg_rows * 384 * 512, bytes_accessed=seg_rows * width * 12, transcendentals=0
        ),
        name="forward_messages",
    )(links, feat, sent_rows, sent_ids, w_self, w_neighbor, bias, gain, w_expand)


def encoder_kernel(
    table_s,
    names_in,
    got,
    links,
    feat,
    msg,
    hid,
    slope_pre,
    act,
    bend,
    gain,
    w_expand,
    w_reduce,
    w_self,
    w_neighbor,
    shared_out,
    direct_out,
    ge_out,
    gr_out,
    gs_out,
    small_out,
    landed,
    rows,
    names,
    stage,
    onehot,
    cot_s,
    low_s,
    inner_s,
    pair_s,
    w_back,
    sem,
):
    step = pl.program_id(0)
    width = feat.shape[1]
    sources = table_s.shape[0] - 8
    capacity = got.shape[0] // sources
    stride = capacity + WIN

    @pl.when(step == 0)
    def _():
        fetch = pltpu.make_async_copy(got, landed, sem.at[0])
        label = pltpu.make_async_copy(names_in, names, sem.at[1])
        fetch.start()
        label.start()
        w_back[:, :width] = w_neighbor[...].astype(F32).T.astype(BF16)
        w_back[:, width:] = w_self[...].astype(F32).T.astype(BF16)
        for total in (ge_out, gr_out, pair_s, small_out):
            total[...] = jnp.zeros_like(total)
        fetch.wait()
        for s in range(sources):
            rows[s * stride : s * stride + capacity, :] = landed[
                s * capacity : (s + 1) * capacity, :
            ].astype(F32)
            rows[s * stride + capacity : (s + 1) * stride, :] = jnp.zeros((WIN, 128), F32)
        label.wait()

    def collect(block, turn):
        first = (block * GROUP).astype(F32)
        left = iota((WIN, 128), 1, F32) + first
        for s in range(sources):
            at = jnp.minimum(table_s[s, block] + turn * WIN, capacity) + s * stride
            name = names[pl.ds(at, WIN), :]
            stage[s * WIN : (s + 1) * WIN, :] = rows[pl.ds(at, WIN), :].astype(BF16)
            for k in range(GROUP // 128):
                onehot[s * WIN : (s + 1) * WIN, k * 128 : (k + 1) * 128] = jnp.where(
                    name == left + 128.0 * k, 1.0, 0.0
                ).astype(BF16)
        return dot(stage[...], onehot[...], 0, 0).T

    for j in range(STEP // GROUP):
        part = slice(j * GROUP, (j + 1) * GROUP)
        block = step * (STEP // GROUP) + j
        cot_s[part, :] = collect(block, 0)
        turns = (table_s[sources, block] + (WIN - 1)) // WIN

        @pl.when(turns > 1)
        def _():
            @pl.loop(1, turns)
            def _(turn):
                cot_s[part, :] += collect(block, turn)

    scale = gain[...]
    unit, rate = normalised(hid[...])
    normed = (unit * scale).astype(BF16)
    low_s[...] = cot_s[...].astype(BF16)
    for j in range(STEP // CHUNK):
        part = slice(j * CHUNK, (j + 1) * CHUNK)
        back_active = dot(low_s[part, :], w_reduce[...], 1, 1)
        inner_s[part, :] = (back_active * bend[part, :].astype(F32)).astype(BF16)
    gr_out[...] += dot(low_s[...], act[...], 0, 0)
    ge_out[...] += dot(normed, inner_s[...], 0, 0)
    back_normed = dot(inner_s[...], w_expand[...], 1, 1)
    small_out[0:1, :] += jnp.sum(back_normed * unit, axis=0, keepdims=True)
    weighted = scale * back_normed
    mean = jnp.mean(weighted * unit, axis=-1, keepdims=True)
    back_hidden = cot_s[...] + (weighted - unit * mean) * rate
    back_pre = back_hidden * slope_pre[...]
    low = back_pre.astype(BF16)
    small_out[1:2, :] += jnp.sum(low.astype(F32), axis=0, keepdims=True)
    pair_s[...] += dot(low, jnp.concatenate([feat[...], msg[...]], axis=1), 0, 0)
    both = dot(low, w_back[...])
    used = jnp.sum(jnp.where(links[...] != 0, 1.0, 0.0), axis=0, keepdims=True)
    used = jnp.broadcast_to(used, (16, STEP)).astype(BF16)
    degree = 1.0 + dot(used, jnp.full((16, 128), 1.0 / 16.0, BF16), 0, 0)
    shared_out[...] = (both[:, :width] / degree).astype(BF16)
    direct_out[...] = back_hidden + both[:, width:]

    @pl.when(step == pl.num_programs(0) - 1)
    def _():
        gs_out[...] = pair_s[...].T


def encoder(
    table, names, got, links, feat, msg, hid, slope_pre, act, bend, gain, w_expand, w_reduce, w_self, w_neighbor
):
    seg_rows, width = feat.shape
    sources, hidden = table.shape[0] - 8, w_expand.shape[1]
    whole = lambda shape: pl.BlockSpec(shape, lambda i: (0,) * len(shape))
    rows = pl.BlockSpec((STEP, width), lambda i: (i, 0))
    wide = pl.BlockSpec((STEP, hidden), lambda i: (i, 0))
    return pl.pallas_call(
        encoder_kernel,
        grid=(seg_rows // STEP,),
        in_specs=[
            pl.BlockSpec(memory_space=pltpu.SMEM),
            pl.BlockSpec(memory_space=pl.ANY),
            pl.BlockSpec(memory_space=pl.ANY),
            pl.BlockSpec((4, STEP), lambda i: (0, i)),
            rows,
            rows,
            rows,
            rows,
            wide,
            wide,
            whole((1, width)),
            whole((width, hidden)),
            whole((hidden, width)),
            whole((width, width)),
            whole((width, width)),
        ],
        out_specs=[
            rows,
            rows,
            whole((width, hidden)),
            whole((width, hidden)),
            whole((2 * width, width)),
            whole((8, width)),
        ],
        out_shape=[
            jax.ShapeDtypeStruct((seg_rows, width), BF16),
            jax.ShapeDtypeStruct((seg_rows, width), F32),
            jax.ShapeDtypeStruct((width, hidden), F32),
            jax.ShapeDtypeStruct((width, hidden), F32),
            jax.ShapeDtypeStruct((2 * width, width), F32),
            jax.ShapeDtypeStruct((8, width), F32),
        ],
        scratch_shapes=[
            pltpu.VMEM(got.shape, BF16),
            pltpu.VMEM(names.shape, F32),
            pltpu.VMEM(names.shape, F32),
            pltpu.VMEM((sources * WIN, width), BF16),
            pltpu.VMEM((sources * WIN, GROUP), BF16),
            pltpu.VMEM((STEP, width), F32),
            pltpu.VMEM((STEP, width), BF16),
            pltpu.VMEM((STEP, hidden), BF16),
            pltpu.VMEM((width, 2 * width), F32),
            pltpu.VMEM((width, 2 * width), BF16),
            pltpu.SemaphoreType.DMA((2,)),
        ],
        compiler_params=pltpu.CompilerParams(vmem_limit_bytes=VMEM_LIMIT),
        cost_estimate=pl.CostEstimate(
            flops=seg_rows * width * hidden * 10, bytes_accessed=seg_rows * width * 20, transcendentals=0
        ),
        name="encoder_backward",
    )(
        table, names, got, links, feat, msg, hid, slope_pre, act, bend, gain, w_expand, w_reduce, w_self, w_neighbor
    )


def spread_kernel(
    graph_scale,
    route_scale,
    links,
    shared,
    direct,
    grad_expand,
    grad_reduce,
    grad_pair,
    small,
    out,
    expand_out,
    reduce_out,
    self_out,
    neighbor_out,
    bias_out,
    gain_out,
    ext,
    links_ext,
    mine,
    parts_in,
    part,
    tiles_in,
    whole,
    wholes_in,
    halo_send,
    halo_recv,
    part_send,
    part_recv,
    tile_send,
    tile_recv,
    whole_send,
    whole_recv,
    sem,
):
    step = pl.program_id(0)
    steps = pl.num_programs(0)
    seg_rows, width = shared.shape
    hidden = expand_out.shape[1]
    parts, tiles = parts_in.shape[0], tiles_in.shape[0]
    half = parts // 2
    me, tile = lax.axis_index("dom"), lax.axis_index("rep")
    right, left = lax.rem(me + 1, parts), lax.rem(me + parts - 1, parts)

    def halos():
        tail = pl.ds(seg_rows - HALO, HALO)
        head = pl.ds(0, HALO)
        far = pl.ds(seg_rows + HALO, HALO)
        for n, (source, target, device) in enumerate(
            (
                (shared.at[tail, :], ext.at[head, :], right),
                (shared.at[head, :], ext.at[far, :], left),
                (links.at[:, tail], links_ext.at[:, head], right),
                (links.at[:, head], links_ext.at[:, far], left),
            )
        ):
            yield remote(source, target, halo_send.at[n], halo_recv.at[n], (tile, device))

    def part_copy(k):
        to = lax.rem(me + k, parts)
        return remote(mine.at[to], parts_in.at[me], part_send.at[k], part_recv.at[me], (tile, to))

    def part_arrival(k):
        at = lax.rem(me + k, parts)
        return remote(mine.at[at], parts_in.at[at], part_send.at[k], part_recv.at[at], (tile, at))

    def tile_copy(k):
        to = lax.rem(tile + k, tiles)
        return remote(part, tiles_in.at[tile], tile_send.at[k], tile_recv.at[tile], (to, me))

    def tile_arrival(k):
        at = lax.rem(tile + k, tiles)
        return remote(part, tiles_in.at[at], tile_send.at[k], tile_recv.at[at], (at, me))

    def whole_copy(k):
        to = lax.rem(me + k, parts)
        return remote(whole, wholes_in.at[me], whole_send.at[k], whole_recv.at[me], (tile, to))

    def whole_arrival(k):
        at = lax.rem(me + k, parts)
        return remote(whole, wholes_in.at[at], whole_send.at[k], whole_recv.at[at], (tile, at))

    @pl.when(step == 0)
    def _():
        barrier = pltpu.get_barrier_semaphore()

        @pl.loop(1, parts)
        def _(k):
            greet(barrier, (tile, lax.rem(me + k, parts)))

        for k in range(1, tiles):
            greet(barrier, (lax.rem(tile + k, tiles), me))
        pl.semaphore_wait(barrier, parts + tiles - 2)
        for copy in halos():
            copy.start()
        mine[:half, :, :hidden] = grad_expand[...].astype(BF16)
        mine[half:, :, :hidden] = grad_reduce[...].astype(BF16)
        mine[:, :, hidden : hidden + width] = grad_pair[...].astype(BF16)
        mine[:, :, hidden + width :] = jnp.broadcast_to(small[...][None], (parts, 8, width)).astype(
            BF16
        )
        @pl.loop(1, parts)
        def _(k):
            part_copy(k).start()

        local = pltpu.make_async_copy(shared, ext.at[pl.ds(HALO, seg_rows), :], sem.at[0])
        edges = pltpu.make_async_copy(links, links_ext.at[:, pl.ds(HALO, seg_rows)], sem.at[1])
        local.start()
        edges.start()
        local.wait()
        edges.wait()

    @pl.when(step == 5)
    def _():
        @pl.loop(1, parts)
        def _(k):
            part_arrival(k).wait_recv()

        parts_in[me] = mine[me]
        part[...] = lax.fori_loop(
            1,
            parts,
            lambda p, total: total + parts_in[p].astype(F32),
            parts_in[0].astype(F32),
        )
        for k in range(1, tiles):
            tile_copy(k).start()

    @pl.when(step == 8)
    def _():
        for k in range(1, tiles):
            tile_arrival(k).wait_recv()
        tiles_in[tile] = part[...]
        total = tiles_in[0]
        for t in range(1, tiles):
            total = total + tiles_in[t]
        whole[...] = total.astype(BF16)

        @pl.loop(1, parts)
        def _(k):
            whole_copy(k).start()

    @pl.when(step == steps - 2)
    def _():
        for copy in halos():
            copy.wait_recv()
        head, far = pl.ds(0, HALO), pl.ds(seg_rows + HALO, HALO)
        links_ext[:, head] = jnp.where(me > 0, links_ext[:, head], 0)
        links_ext[:, far] = jnp.where(me < parts - 1, links_ext[:, far], 0)

    at = lax.rem(step + 1, steps) * STEP
    same = identity()
    for j in range(STEP // 128):
        base = pl.multiple_of(at + j * 128, 128)
        near = [
            ends(links_ext[:, pl.ds(pl.multiple_of(base + k * 128, 128), 128)]) for k in range(3)
        ]
        table = jnp.concatenate(
            [hits(near[0], -128.0, None), hits(near[1], 0.0, same), hits(near[2], 128.0, None)],
            axis=1,
        )
        summed = dot(table, ext[pl.ds(base, 384), :])
        rows = slice(j * 128, (j + 1) * 128)
        out[rows, :] = (direct[rows, :] + summed).astype(BF16)

    @pl.when(step == steps - 1)
    def _():
        @pl.loop(1, parts)
        def _(k):
            whole_arrival(k).wait_recv()

        wholes_in[me] = whole[...]
        expand = wholes_in[:half, :, :hidden].astype(F32) * route_scale
        reduced = wholes_in[half:, :, :hidden].astype(F32) * route_scale
        pair = wholes_in[:, :, hidden : hidden + width].astype(F32) * graph_scale
        little = wholes_in[0, :, hidden + width :].astype(F32)
        expand_out[...] = expand.reshape(width, hidden)
        reduce_out[...] = reduced.reshape(width, hidden).T
        self_out[...] = pair[:half].reshape(width, width)
        neighbor_out[...] = pair[half:].reshape(width, width)
        gain_out[...] = little[0:1] * route_scale
        bias_out[...] = little[1:2] * graph_scale
        for copy in halos():
            copy.wait_send()

        @pl.loop(1, parts)
        def _(k):
            part_copy(k).wait_send()
            whole_copy(k).wait_send()

        for k in range(1, tiles):
            tile_copy(k).wait_send()


def spread(links, shared, direct, grad_expand, grad_reduce, grad_pair, small, scales):
    seg_rows, width = shared.shape
    hidden = grad_expand.shape[1]
    parts, tiles = lax.axis_size("dom"), lax.axis_size("rep")
    steps = seg_rows // STEP
    slab = hidden + 2 * width
    cut = lambda a: a.reshape(-1, 8, a.shape[1])
    grads = [cut(grad_expand), cut(grad_reduce), cut(grad_pair)]
    whole = lambda a: pl.BlockSpec(a.shape, lambda i: (0,) * a.ndim)
    rows = pl.BlockSpec((STEP, width), lambda i: (lax.rem(i + 1, steps), 0))
    dma = pltpu.SemaphoreType.DMA
    totals = [(width, hidden), (hidden, width), (width, width), (width, width), (1, width), (1, width)]
    return pl.pallas_call(
        functools.partial(spread_kernel, *scales),
        grid=(steps,),
        in_specs=[
            pl.BlockSpec(memory_space=pl.ANY),
            pl.BlockSpec(memory_space=pl.ANY),
            rows,
            *[whole(g) for g in grads],
            whole(small),
        ],
        out_specs=[rows, *[pl.BlockSpec(t, lambda i: (0, 0)) for t in totals]],
        out_shape=[
            jax.ShapeDtypeStruct((seg_rows, width), BF16),
            *[jax.ShapeDtypeStruct(t, F32) for t in totals],
        ],
        scratch_shapes=[
            pltpu.VMEM((seg_rows + 2 * HALO, width), BF16),
            pltpu.VMEM((4, seg_rows + 2 * HALO), jnp.int32),
            pltpu.VMEM((parts, 8, slab), BF16),
            pltpu.VMEM((parts, 8, slab), BF16),
            pltpu.VMEM((8, slab), F32),
            pltpu.VMEM((tiles, 8, slab), F32),
            pltpu.VMEM((8, slab), BF16),
            pltpu.VMEM((parts, 8, slab), BF16),
            dma((4,)),
            dma((4,)),
            dma((parts,)),
            dma((parts,)),
            dma((tiles,)),
            dma((tiles,)),
            dma((parts,)),
            dma((parts,)),
            dma((2,)),
        ],
        compiler_params=pltpu.CompilerParams(
            vmem_limit_bytes=VMEM_LIMIT, collective_id=1, has_side_effects=True
        ),
        cost_estimate=pl.CostEstimate(
            flops=seg_rows * 384 * 256, bytes_accessed=seg_rows * width * 8, transcendentals=0
        ),
        name="spread_back",
    )(links, shared, direct, *grads, small)


def per_device(
    features, edges, route, cotangent, w_self, w_neighbor, bias, gain, w_expand, w_reduce
):
    feat = features[0]
    links = edges[0].T
    seg_rows, width = feat.shape
    parts = lax.axis_size("dom")
    trip_ids = route[0].reshape(-1)
    rows_dev = trip_ids.shape[0]
    capacity = 2 * rows_dev // parts
    cot_rows = cotangent[0].reshape(rows_dev, width)

    bits = (rows_dev - 1).bit_length()
    keys = (trip_ids.astype(jnp.uint32) << bits) | jnp.arange(rows_dev, dtype=jnp.uint32)
    keys = lax.sort(keys)
    order = jnp.pad((keys & (rows_dev - 1)).astype(jnp.int32), (0, 128))
    sorted_ids = jnp.pad((keys >> bits).astype(jnp.int32).reshape(-1, 128), ((0, 8), (0, 0)))
    edges_of = jnp.arange(parts + 1, dtype=jnp.int32) * seg_rows
    bounds = jnp.sum((trip_ids[None, :] < edges_of[:, None]).astype(jnp.int32), axis=1)
    sent_rows, sent_ids = pack(order, bounds, sorted_ids, cot_rows, parts, capacity, seg_rows)
    msg, hid, slope_pre, act, bend, table, got_rows, _, names = forward(
        links, feat, sent_rows, sent_ids, w_self, w_neighbor, bias[None], gain[None], w_expand
    )
    shared, direct, grad_expand, grad_reduce_t, grad_pair, small = encoder(
        table,
        names,
        got_rows.reshape(parts * capacity, width),
        links,
        feat,
        msg,
        hid,
        slope_pre,
        act,
        bend,
        gain[None],
        w_expand,
        w_reduce,
        w_self,
        w_neighbor,
    )
    tiles = lax.axis_size("rep")
    scales = (
        1.0 / math.sqrt(tiles * parts * seg_rows),
        1.0 / math.sqrt(tiles * parts * rows_dev),
    )
    grad_features, grad_expand, grad_reduce, grad_self, grad_neighbor, grad_bias, grad_gain = spread(
        links, shared, direct, grad_expand, grad_reduce_t, grad_pair, small, scales
    )
    return (
        grad_features[None],
        grad_self,
        grad_neighbor,
        grad_bias[0],
        grad_gain[0],
        grad_expand,
        grad_reduce,
    )


def solution(mesh):
    return jax.shard_map(
        per_device,
        mesh=mesh,
        in_specs=(
            P("rep", "dom", None),
            P("rep", "dom", None),
            P("rep", "dom", None),
            P("rep", "dom", None, None),
            P(),
            P(),
            P(),
            P(),
            P(),
            P(),
        ),
        out_specs=(P("rep", "dom", None), P(), P(), P(), P(), P(), P()),
        check_vma=False,
    )
```

```python
import functools
import math

import jax
import jax.numpy as jnp
from jax import lax
from jax.experimental import pallas as pl
from jax.experimental.pallas import tpu as pltpu
from jax.sharding import PartitionSpec as P

HALO = 128
WIN = 16
GROUP = 256
CHUNK = 256
OWNERS = 4
ROUTE = (
    (2, 1), (1, 2), (2, 3), (3, 2), (2, 2), (0, 2), (2, 0), (1, 1),
    (3, 3), (1, 3), (3, 1), (0, 1), (1, 0), (0, 3), (3, 0),
)
SIDE = 4
PASSES = 2
STEP = 1024
SPAN = 2 * STEP
F32 = jnp.float32
BF16 = jnp.bfloat16
VMEM_LIMIT = 56 * 1024 * 1024


def iota(shape, dim, dtype=jnp.int32):
    return lax.broadcasted_iota(jnp.int32, shape, dim).astype(dtype)


def dot(a, b, da=1, db=0):
    return lax.dot_general(a, b, (((da,), (db,)), ((), ())), preferred_element_type=F32)


def sigmoid(value):
    return 0.5 * jnp.tanh(0.5 * value) + 0.5


def pack_kernel(capacity, seg_rows, order, bounds, ids, cot, rows_out, ids_out, rows, stage):
    turn = pl.program_id(0)
    chunk = 512

    @pl.when(turn == 0)
    def _():
        stage[...] = jnp.zeros_like(stage)

        @pl.loop(0, cot.shape[0] // chunk)
        def _(i):
            part = pl.ds(pl.multiple_of(i * chunk, chunk), chunk)
            rows[part, :] = cot[part, :].astype(F32)

    for n in range(OWNERS):
        owner = turn * OWNERS + n
        start = bounds[owner]
        count = bounds[owner + 1] - start
        at = n * capacity

        def move(g, carry):
            base = pl.multiple_of(g * 16, 16)
            for j in range(16):
                source = order[start + base + j]
                stage[pl.ds(base + (at + j), 1), :] = rows[pl.ds(source, 1), :]
            return carry

        lax.fori_loop(0, (count + 15) // 16, move, 0)
        rows_out[n] = stage[at : at + capacity, :].astype(BF16)

        lines = capacity // 128
        shift = lax.rem(start, 128)
        window = ids[pl.ds(start // 128, 8), :]
        turned = pltpu.roll(window, lax.rem(128 - shift, 128), 1)
        lane = iota((lines, 128), 1)
        joined = jnp.where(lane < 128 - shift, turned[:lines], turned[1 : lines + 1])
        place = iota((lines, 128), 0) * 128 + lane
        ids_out[n] = jnp.where(place < count, joined - owner * seg_rows, seg_rows)


def pack(order, bounds, ids, cot, parts, capacity, seg_rows):
    rows_dev, width = cot.shape
    return pl.pallas_call(
        functools.partial(pack_kernel, capacity, seg_rows),
        grid_spec=pltpu.PrefetchScalarGridSpec(
            num_scalar_prefetch=2,
            grid=(parts // OWNERS,),
            in_specs=[
                pl.BlockSpec(ids.shape, lambda i, *_: (0, 0)),
                pl.BlockSpec(cot.shape, lambda i, *_: (0, 0)),
            ],
            out_specs=[
                pl.BlockSpec((OWNERS, capacity, width), lambda i, *_: (i, 0, 0)),
                pl.BlockSpec((OWNERS, capacity // 128, 128), lambda i, *_: (i, 0, 0)),
            ],
            scratch_shapes=[
                pltpu.VMEM((rows_dev, width), F32),
                pltpu.VMEM((OWNERS * capacity, width), F32),
            ],
        ),
        out_shape=[
            jax.ShapeDtypeStruct((parts, capacity, width), BF16),
            jax.ShapeDtypeStruct((parts, capacity // 128, 128), jnp.int32),
        ],
        compiler_params=pltpu.CompilerParams(vmem_limit_bytes=VMEM_LIMIT),
        name="pack_rows",
    )(order, bounds, ids, cot)


def hits(local, shift, same):
    rows = iota((128, 128), 0, F32).astype(BF16)
    table = same
    for slot in range(4):
        wanted = jnp.broadcast_to(local[slot : slot + 1, :] + shift, (16, 128)).astype(BF16)
        wanted = jnp.concatenate([wanted] * 8, axis=0)
        hit = jnp.where(wanted == rows, jnp.ones((), BF16), jnp.zeros((), BF16))
        table = hit if table is None else table + hit
    return table


def identity():
    return jnp.where(iota((128, 128), 0) == iota((128, 128), 1), 1.0, 0.0).astype(BF16)


def ends(links):
    lane = iota(links.shape, 1)
    return jnp.where(links != 0, links + lane, -100000).astype(F32)


def normalised(hid):
    values = hid.astype(F32)
    rate = lax.rsqrt(jnp.mean(values * values, axis=-1, keepdims=True) + 1e-06)
    return values * rate, rate


def remote(source, target, send, recv, device):
    return pltpu.make_async_remote_copy(
        src_ref=source,
        dst_ref=target,
        send_sem=send,
        recv_sem=recv,
        device_id=device,
        device_id_type=pl.DeviceIdType.MESH,
    )


def greet(barrier, device):
    pl.semaphore_signal(barrier, inc=1, device_id=device, device_id_type=pl.DeviceIdType.MESH)


def forward_kernel(
    links,
    feat,
    sent_rows,
    sent_ids,
    w_self,
    w_neighbor,
    bias,
    gain,
    w_expand,
    msg_out,
    hid_out,
    slope_out,
    act_out,
    bend_out,
    table_out,
    got_rows,
    got_ids,
    names_out,
    ext,
    w_cat,
    ids,
    names,
    halo_send,
    halo_recv,
    rows_send,
    rows_recv,
    ids_send,
    ids_recv,
    sem,
):
    step = pl.program_id(0)
    steps = pl.num_programs(0)
    seg_rows, width = feat.shape
    parts = got_ids.shape[0]
    me, tile = lax.axis_index("dom"), lax.axis_index("rep")
    right, left = lax.rem(me + 1, parts), lax.rem(me + parts - 1, parts)

    def halos():
        tail, head = pl.ds(seg_rows - HALO, HALO), pl.ds(0, HALO)
        far, lanes = pl.ds(seg_rows + HALO, HALO), pl.ds(0, width)
        for n, (source, target, device) in enumerate(
            (
                (feat.at[tail, :], ext.at[head, lanes], right),
                (feat.at[head, :], ext.at[far, lanes], left),
            )
        ):
            yield remote(source, target, halo_send.at[n], halo_recv.at[n], (tile, device))

    def half(h):
        size = sent_rows.shape[1] // PASSES
        return pl.ds(h * size, size)

    def rows_copy(to, h):
        return remote(
            sent_rows.at[to, half(h)],
            got_rows.at[me, half(h)],
            rows_send.at[h, to],
            rows_recv.at[h, me],
            (tile, to),
        )

    def rows_arrival(at, h):
        return remote(
            sent_rows.at[at, half(h)],
            got_rows.at[at, half(h)],
            rows_send.at[h, at],
            rows_recv.at[h, at],
            (tile, at),
        )

    def ids_copy(to):
        return remote(sent_ids.at[to], got_ids.at[me], ids_send.at[to], ids_recv.at[me], (tile, to))

    def ids_arrival(at):
        return remote(sent_ids.at[at], got_ids.at[at], ids_send.at[at], ids_recv.at[at], (tile, at))

    def chip(down, along, swap):
        y, x, core = me // (2 * SIDE), lax.rem(me // 2, SIDE), lax.rem(me, 2)
        there = lax.rem(y + down, SIDE) * SIDE + lax.rem(x + along, SIDE)
        return there * 2 + lax.rem(core + swap, 2)

    def own_copies():
        yield pltpu.make_async_copy(sent_rows.at[me], got_rows.at[me], sem.at[1])
        yield pltpu.make_async_copy(sent_ids.at[me], got_ids.at[me], sem.at[2])

    @pl.when(step == 0)
    def _():
        barrier = pltpu.get_barrier_semaphore()

        @pl.loop(1, parts)
        def _(k):
            greet(barrier, (tile, lax.rem(me + k, parts)))

        pl.semaphore_wait(barrier, parts - 1)
        for copy in halos():
            copy.start()

        @pl.loop(1, parts)
        def _(k):
            ids_copy(lax.rem(me + k, parts)).start()

        for h in range(PASSES):
            for swap in range(2):
                for down, along in ROUTE:
                    rows_copy(chip(down, along, swap), h).start()
            rows_copy(chip(0, 0, 1), h).start()
        local = pltpu.make_async_copy(
            feat, ext.at[pl.ds(HALO, seg_rows), pl.ds(0, width)], sem.at[0]
        )
        local.start()
        for copy in own_copies():
            copy.start()
        ext[:, width:] = jnp.ones((ext.shape[0], width), BF16)
        w_cat[:width, :] = w_self[...]
        w_cat[width:, :] = w_neighbor[...]
        local.wait()

    @pl.when(step == steps - 2)
    def _():
        for copy in halos():
            copy.wait_recv()

    start = lax.rem(step + 1, steps) * STEP
    same = identity()
    for j in range(STEP // 128):
        base = pl.multiple_of(start + j * 128, 128)
        local = ends(links[:, j * 128 : (j + 1) * 128])
        table = jnp.concatenate(
            [hits(local, 128.0, None), hits(local, 0.0, same), hits(local, -128.0, None)], axis=0
        )
        summed = dot(table, ext[pl.ds(base, 384), :], 0, 0)
        messages = summed[:, :width] / summed[:, width:]
        msg_out[j * 128 : (j + 1) * 128, :] = messages.astype(BF16)
    own = ext[pl.ds(pl.multiple_of(start + HALO, 128), STEP), :width]
    pre = dot(jnp.concatenate([own, msg_out[...]], axis=1), w_cat[...]) + bias[...]
    gate = sigmoid(pre)
    swish = pre * gate
    hidden = (own.astype(F32) + swish).astype(BF16)
    hid_out[...] = hidden
    slope_out[...] = gate + swish * (1.0 - gate)
    unit, _ = normalised(hidden)
    normed = (unit * gain[...]).astype(BF16)
    for j in range(STEP // CHUNK):
        part = slice(j * CHUNK, (j + 1) * CHUNK)
        inner = dot(normed[part], w_expand[...])
        gate = sigmoid(inner)
        swish = inner * gate
        act_out[part, :] = swish.astype(BF16)
        bend_out[part, :] = (gate + swish * (1.0 - gate)).astype(BF16)

    @pl.when(step == steps - 1)
    def _():
        for copy in own_copies():
            copy.wait()

        @pl.loop(1, parts)
        def _(k):
            ids_arrival(lax.rem(me + k, parts)).wait_recv()

        fetch = pltpu.make_async_copy(got_ids, ids, sem.at[0])
        fetch.start()
        fetch.wait()
        capacity = ids.shape[1] * 128
        stride = capacity + WIN
        place = iota((16, 128), 0)
        weights = jnp.where(place == 0, 128.0, jnp.where(place == 1, 1.0, 0.0)).astype(BF16)
        bound = iota((1, 128), 1, F32) * float(GROUP)
        most = jnp.zeros((1, 128), F32)
        for s in range(parts):
            below = jnp.zeros((1, 128), F32)
            for k in range(ids.shape[1]):
                line = ids[s, k : k + 1, :]
                high = jnp.broadcast_to(line >> 7, (16, 128))
                low = jnp.broadcast_to(line & 127, (16, 128))
                digits = jnp.where(place == 0, high, jnp.where(place == 1, low, 0))
                column = dot(digits.astype(F32).astype(BF16), weights, 0, 0)
                at = s * stride + k * 128
                names[at : at + 128, :] = column
                below += jnp.sum(jnp.where(column < bound, 1.0, 0.0), axis=0, keepdims=True)
            names[s * stride + capacity : (s + 1) * stride, :] = jnp.full((WIN, 128), 1e6, F32)
            table_out[s : s + 1, :] = below.astype(jnp.int32)
            most = jnp.maximum(most, pltpu.roll(below, 127, 1) - below)
        table_out[parts : parts + 8, :] = jnp.broadcast_to(most, (8, 128)).astype(jnp.int32)
        store = pltpu.make_async_copy(names, names_out, sem.at[0])
        store.start()
        for copy in halos():
            copy.wait_send()

        @pl.loop(1, parts)
        def _(k):
            other = lax.rem(me + k, parts)
            ids_copy(other).wait_send()
            for h in range(PASSES):
                rows_arrival(other, h).wait_recv()
                rows_copy(other, h).wait_send()

        store.wait()


def forward(links, feat, sent_rows, sent_ids, w_self, w_neighbor, bias, gain, w_expand):
    seg_rows, width = feat.shape
    hidden = w_expand.shape[1]
    steps, parts = seg_rows // STEP, sent_ids.shape[0]
    columns = parts * (sent_rows.shape[1] + WIN)
    whole = lambda a: pl.BlockSpec(a.shape, lambda i: (0,) * a.ndim)
    rows = lambda n: pl.BlockSpec((STEP, n), lambda i: (lax.rem(i + 1, steps), 0))
    away = pl.BlockSpec(memory_space=pl.ANY)
    dma = pltpu.SemaphoreType.DMA
    return pl.pallas_call(
        forward_kernel,
        grid=(steps,),
        in_specs=[
            pl.BlockSpec((4, STEP), lambda i: (0, lax.rem(i + 1, steps))),
            away,
            away,
            away,
            whole(w_self),
            whole(w_neighbor),
            whole(bias),
            whole(gain),
            whole(w_expand),
        ],
        out_specs=[
            rows(width),
            rows(width),
            rows(width),
            rows(hidden),
            rows(hidden),
            pl.BlockSpec((parts + 8, 128), lambda i: (0, 0)),
            away,
            away,
            away,
        ],
        out_shape=[
            jax.ShapeDtypeStruct((seg_rows, width), BF16),
            jax.ShapeDtypeStruct((seg_rows, width), BF16),
            jax.ShapeDtypeStruct((seg_rows, width), F32),
            jax.ShapeDtypeStruct((seg_rows, hidden), BF16),
            jax.ShapeDtypeStruct((seg_rows, hidden), BF16),
            jax.ShapeDtypeStruct((parts + 8, 128), jnp.int32),
            jax.ShapeDtypeStruct(sent_rows.shape, BF16),
            jax.ShapeDtypeStruct(sent_ids.shape, jnp.int32),
            jax.ShapeDtypeStruct((columns, 128), F32),
        ],
        scratch_shapes=[
            pltpu.VMEM((seg_rows + 2 * HALO, 2 * width), BF16),
            pltpu.VMEM((2 * width, width), BF16),
            pltpu.VMEM(sent_ids.shape, jnp.int32),
            pltpu.VMEM((columns, 128), F32),
            dma((2,)),
            dma((2,)),
            dma((PASSES, parts)),
            dma((PASSES, parts)),
            dma((parts,)),
            dma((parts,)),
            dma((3,)),
        ],
        compiler_params=pltpu.CompilerParams(
            vmem_limit_bytes=VMEM_LIMIT, collective_id=2, has_side_effects=True
        ),
        cost_estimate=pl.CostEstimate(
            flops=seg_rows * 384 * 512, bytes_accessed=seg_rows * width * 12, transcendentals=0
        ),
        name="forward_messages",
    )(links, feat, sent_rows, sent_ids, w_self, w_neighbor, bias, gain, w_expand)


def encoder_kernel(
    table_s,
    names_in,
    got,
    links,
    feat,
    msg,
    hid,
    slope_pre,
    act,
    bend,
    gain,
    w_expand,
    w_reduce,
    w_self,
    w_neighbor,
    shared_out,
    direct_out,
    ge_out,
    gr_out,
    gs_out,
    small_out,
    landed,
    rows,
    names,
    stage,
    onehot,
    cot_a,
    cot_b,
    low_s,
    inner_s,
    pair_s,
    w_back,
    sem,
):
    step = pl.program_id(0)
    width = feat.shape[1]
    sources = table_s.shape[0] - 8
    capacity = got.shape[0] // sources
    stride = capacity + WIN

    @pl.when(step == 0)
    def _():
        fetch = pltpu.make_async_copy(got, landed, sem.at[0])
        label = pltpu.make_async_copy(names_in, names, sem.at[1])
        fetch.start()
        label.start()
        w_back[:, :width] = w_neighbor[...].astype(F32).T.astype(BF16)
        w_back[:, width:] = w_self[...].astype(F32).T.astype(BF16)
        for total in (ge_out, gr_out, pair_s, small_out):
            total[...] = jnp.zeros_like(total)
        fetch.wait()
        for s in range(sources):
            rows[s * stride : s * stride + capacity, :] = landed[
                s * capacity : (s + 1) * capacity, :
            ].astype(F32)
            rows[s * stride + capacity : (s + 1) * stride, :] = jnp.zeros((WIN, 128), F32)
        label.wait()

    def collect(block, turn, j):
        first = (block * GROUP).astype(F32)
        left = iota((WIN, 128), 1, F32) + first
        for s in range(sources):
            at = jnp.minimum(table_s[s, block] + turn * WIN, capacity) + s * stride
            name = names[pl.ds(at, WIN), :]
            stage[j, s * WIN : (s + 1) * WIN, :] = rows[pl.ds(at, WIN), :].astype(BF16)
            for k in range(GROUP // 128):
                onehot[j, s * WIN : (s + 1) * WIN, k * 128 : (k + 1) * 128] = jnp.where(
                    name == left + 128.0 * k, 1.0, 0.0
                ).astype(BF16)
        return dot(onehot[j], stage[j], 0, 0)

    def gather(target, first):
        blocks = [jnp.minimum(first + j, last) for j in range(STEP // GROUP)]
        for j, block in enumerate(blocks):
            target[j * GROUP : (j + 1) * GROUP, :] = collect(block, 0, j)

    def overflow(target, first):
        for j in range(STEP // GROUP):
            block = jnp.minimum(first + j, last)
            turns = (table_s[sources, block] + (WIN - 1)) // WIN

            @pl.when(turns > 1)
            def _():
                @pl.loop(1, turns)
                def _(turn):
                    target[j * GROUP : (j + 1) * GROUP, :] += collect(block, turn, j)

    def encode(part, cot_s):
        scale = gain[...]
        unit, rate = normalised(hid[part, :])
        normed = (unit * scale).astype(BF16)
        low_s[...] = cot_s[...].astype(BF16)
        for j in range(STEP // CHUNK):
            rows_at = slice(j * CHUNK, (j + 1) * CHUNK)
            back_active = dot(low_s[rows_at, :], w_reduce[...], 1, 1)
            gates = bend[part.start + j * CHUNK : part.start + (j + 1) * CHUNK, :]
            inner_s[rows_at, :] = (back_active * gates.astype(F32)).astype(BF16)
        gr_out[...] += dot(low_s[...], act[part, :], 0, 0)
        ge_out[...] += dot(normed, inner_s[...], 0, 0)
        back_normed = dot(inner_s[...], w_expand[...], 1, 1)
        small_out[0:1, :] += jnp.sum(back_normed * unit, axis=0, keepdims=True)
        weighted = scale * back_normed
        mean = jnp.mean(weighted * unit, axis=-1, keepdims=True)
        back_hidden = cot_s[...] + (weighted - unit * mean) * rate
        back_pre = back_hidden * slope_pre[part, :]
        low = back_pre.astype(BF16)
        small_out[1:2, :] += jnp.sum(low.astype(F32), axis=0, keepdims=True)
        pair_s[...] += dot(low, jnp.concatenate([feat[part, :], msg[part, :]], axis=1), 0, 0)
        both = dot(low, w_back[...])
        used = jnp.sum(jnp.where(links[:, part] != 0, 1.0, 0.0), axis=0, keepdims=True)
        used = jnp.broadcast_to(used, (16, STEP)).astype(BF16)
        degree = 1.0 + dot(used, jnp.full((16, 128), 1.0 / 16.0, BF16), 0, 0)
        shared_out[part, :] = (both[:, :width] / degree).astype(BF16)
        direct_out[part, :] = back_hidden + both[:, width:]

    blocks = STEP // GROUP
    last = pl.num_programs(0) * (SPAN // GROUP) - 1

    @pl.when(step == 0)
    def _():
        gather(cot_a, 0)
        overflow(cot_a, 0)

    head, tail = slice(0, STEP), slice(STEP, SPAN)
    gather(cot_b, 2 * step * blocks + blocks)
    encode(head, cot_a)
    overflow(cot_b, 2 * step * blocks + blocks)
    encode(tail, cot_b)
    gather(cot_a, 2 * step * blocks + 2 * blocks)
    overflow(cot_a, 2 * step * blocks + 2 * blocks)

    @pl.when(step == pl.num_programs(0) - 1)
    def _():
        gs_out[...] = pair_s[...].T


def encoder(
    table, names, got, links, feat, msg, hid, slope_pre, act, bend, gain, w_expand, w_reduce, w_self, w_neighbor
):
    seg_rows, width = feat.shape
    sources, hidden = table.shape[0] - 8, w_expand.shape[1]
    whole = lambda shape: pl.BlockSpec(shape, lambda i: (0,) * len(shape))
    rows = pl.BlockSpec((SPAN, width), lambda i: (i, 0))
    wide = pl.BlockSpec((SPAN, hidden), lambda i: (i, 0))
    return pl.pallas_call(
        encoder_kernel,
        grid=(seg_rows // SPAN,),
        in_specs=[
            pl.BlockSpec(memory_space=pltpu.SMEM),
            pl.BlockSpec(memory_space=pl.ANY),
            pl.BlockSpec(memory_space=pl.ANY),
            pl.BlockSpec((4, SPAN), lambda i: (0, i)),
            rows,
            rows,
            rows,
            rows,
            wide,
            wide,
            whole((1, width)),
            whole((width, hidden)),
            whole((hidden, width)),
            whole((width, width)),
            whole((width, width)),
        ],
        out_specs=[
            rows,
            rows,
            whole((width, hidden)),
            whole((width, hidden)),
            whole((2 * width, width)),
            whole((8, width)),
        ],
        out_shape=[
            jax.ShapeDtypeStruct((seg_rows, width), BF16),
            jax.ShapeDtypeStruct((seg_rows, width), F32),
            jax.ShapeDtypeStruct((width, hidden), F32),
            jax.ShapeDtypeStruct((width, hidden), F32),
            jax.ShapeDtypeStruct((2 * width, width), F32),
            jax.ShapeDtypeStruct((8, width), F32),
        ],
        scratch_shapes=[
            pltpu.VMEM(got.shape, BF16),
            pltpu.VMEM(names.shape, F32),
            pltpu.VMEM(names.shape, F32),
            pltpu.VMEM((STEP // GROUP, sources * WIN, width), BF16),
            pltpu.VMEM((STEP // GROUP, sources * WIN, GROUP), BF16),
            pltpu.VMEM((STEP, width), F32),
            pltpu.VMEM((STEP, width), F32),
            pltpu.VMEM((STEP, width), BF16),
            pltpu.VMEM((STEP, hidden), BF16),
            pltpu.VMEM((width, 2 * width), F32),
            pltpu.VMEM((width, 2 * width), BF16),
            pltpu.SemaphoreType.DMA((2,)),
        ],
        compiler_params=pltpu.CompilerParams(vmem_limit_bytes=VMEM_LIMIT),
        cost_estimate=pl.CostEstimate(
            flops=seg_rows * width * hidden * 10, bytes_accessed=seg_rows * width * 20, transcendentals=0
        ),
        name="encoder_backward",
    )(
        table, names, got, links, feat, msg, hid, slope_pre, act, bend, gain, w_expand, w_reduce, w_self, w_neighbor
    )


def spread_kernel(
    graph_scale,
    route_scale,
    links,
    shared,
    direct,
    grad_expand,
    grad_reduce,
    grad_pair,
    small,
    out,
    expand_out,
    reduce_out,
    self_out,
    neighbor_out,
    bias_out,
    gain_out,
    ext,
    links_ext,
    mine,
    parts_in,
    part,
    tiles_in,
    whole,
    wholes_in,
    halo_send,
    halo_recv,
    part_send,
    part_recv,
    tile_send,
    tile_recv,
    whole_send,
    whole_recv,
    sem,
):
    step = pl.program_id(0)
    steps = pl.num_programs(0)
    seg_rows, width = shared.shape
    hidden = expand_out.shape[1]
    parts, tiles = parts_in.shape[0], tiles_in.shape[0]
    half = parts // 2
    me, tile = lax.axis_index("dom"), lax.axis_index("rep")
    right, left = lax.rem(me + 1, parts), lax.rem(me + parts - 1, parts)

    def halos():
        tail = pl.ds(seg_rows - HALO, HALO)
        head = pl.ds(0, HALO)
        far = pl.ds(seg_rows + HALO, HALO)
        for n, (source, target, device) in enumerate(
            (
                (shared.at[tail, :], ext.at[head, :], right),
                (shared.at[head, :], ext.at[far, :], left),
                (links.at[:, tail], links_ext.at[:, head], right),
                (links.at[:, head], links_ext.at[:, far], left),
            )
        ):
            yield remote(source, target, halo_send.at[n], halo_recv.at[n], (tile, device))

    def part_copy(k):
        to = lax.rem(me + k, parts)
        return remote(mine.at[to], parts_in.at[me], part_send.at[k], part_recv.at[me], (tile, to))

    def part_arrival(k):
        at = lax.rem(me + k, parts)
        return remote(mine.at[at], parts_in.at[at], part_send.at[k], part_recv.at[at], (tile, at))

    def tile_copy(k):
        to = lax.rem(tile + k, tiles)
        return remote(part, tiles_in.at[tile], tile_send.at[k], tile_recv.at[tile], (to, me))

    def tile_arrival(k):
        at = lax.rem(tile + k, tiles)
        return remote(part, tiles_in.at[at], tile_send.at[k], tile_recv.at[at], (at, me))

    def whole_copy(k):
        to = lax.rem(me + k, parts)
        return remote(whole, wholes_in.at[me], whole_send.at[k], whole_recv.at[me], (tile, to))

    def whole_arrival(k):
        at = lax.rem(me + k, parts)
        return remote(whole, wholes_in.at[at], whole_send.at[k], whole_recv.at[at], (tile, at))

    @pl.when(step == 0)
    def _():
        barrier = pltpu.get_barrier_semaphore()

        @pl.loop(1, parts)
        def _(k):
            greet(barrier, (tile, lax.rem(me + k, parts)))

        for k in range(1, tiles):
            greet(barrier, (lax.rem(tile + k, tiles), me))
        pl.semaphore_wait(barrier, parts + tiles - 2)
        for copy in halos():
            copy.start()
        mine[:half, :, :hidden] = grad_expand[...].astype(BF16)
        mine[half:, :, :hidden] = grad_reduce[...].astype(BF16)
        mine[:, :, hidden : hidden + width] = grad_pair[...].astype(BF16)
        mine[:, :, hidden + width :] = jnp.broadcast_to(small[...][None], (parts, 8, width)).astype(
            BF16
        )
        @pl.loop(1, parts)
        def _(k):
            part_copy(k).start()

        local = pltpu.make_async_copy(shared, ext.at[pl.ds(HALO, seg_rows), :], sem.at[0])
        edges = pltpu.make_async_copy(links, links_ext.at[:, pl.ds(HALO, seg_rows)], sem.at[1])
        local.start()
        edges.start()
        local.wait()
        edges.wait()

    @pl.when(step == 5)
    def _():
        @pl.loop(1, parts)
        def _(k):
            part_arrival(k).wait_recv()

        parts_in[me] = mine[me]
        part[...] = lax.fori_loop(
            1,
            parts,
            lambda p, total: total + parts_in[p].astype(F32),
            parts_in[0].astype(F32),
        )
        for k in range(1, tiles):
            tile_copy(k).start()

    @pl.when(step == 8)
    def _():
        for k in range(1, tiles):
            tile_arrival(k).wait_recv()
        tiles_in[tile] = part[...]
        total = tiles_in[0]
        for t in range(1, tiles):
            total = total + tiles_in[t]
        whole[...] = total.astype(BF16)

        @pl.loop(1, parts)
        def _(k):
            whole_copy(k).start()

    @pl.when(step == steps - 2)
    def _():
        for copy in halos():
            copy.wait_recv()
        head, far = pl.ds(0, HALO), pl.ds(seg_rows + HALO, HALO)
        links_ext[:, head] = jnp.where(me > 0, links_ext[:, head], 0)
        links_ext[:, far] = jnp.where(me < parts - 1, links_ext[:, far], 0)

    at = lax.rem(step + 1, steps) * STEP
    same = identity()
    for j in range(STEP // 128):
        base = pl.multiple_of(at + j * 128, 128)
        near = [
            ends(links_ext[:, pl.ds(pl.multiple_of(base + k * 128, 128), 128)]) for k in range(3)
        ]
        table = jnp.concatenate(
            [hits(near[0], -128.0, None), hits(near[1], 0.0, same), hits(near[2], 128.0, None)],
            axis=1,
        )
        summed = dot(table, ext[pl.ds(base, 384), :])
        rows = slice(j * 128, (j + 1) * 128)
        out[rows, :] = (direct[rows, :] + summed).astype(BF16)

    @pl.when(step == steps - 1)
    def _():
        @pl.loop(1, parts)
        def _(k):
            whole_arrival(k).wait_recv()

        wholes_in[me] = whole[...]
        expand = wholes_in[:half, :, :hidden].astype(F32) * route_scale
        reduced = wholes_in[half:, :, :hidden].astype(F32) * route_scale
        pair = wholes_in[:, :, hidden : hidden + width].astype(F32) * graph_scale
        little = wholes_in[0, :, hidden + width :].astype(F32)
        expand_out[...] = expand.reshape(width, hidden)
        reduce_out[...] = reduced.reshape(width, hidden).T
        self_out[...] = pair[:half].reshape(width, width)
        neighbor_out[...] = pair[half:].reshape(width, width)
        gain_out[...] = little[0:1] * route_scale
        bias_out[...] = little[1:2] * graph_scale
        for copy in halos():
            copy.wait_send()

        @pl.loop(1, parts)
        def _(k):
            part_copy(k).wait_send()
            whole_copy(k).wait_send()

        for k in range(1, tiles):
            tile_copy(k).wait_send()


def spread(links, shared, direct, grad_expand, grad_reduce, grad_pair, small, scales):
    seg_rows, width = shared.shape
    hidden = grad_expand.shape[1]
    parts, tiles = lax.axis_size("dom"), lax.axis_size("rep")
    steps = seg_rows // STEP
    slab = hidden + 2 * width
    cut = lambda a: a.reshape(-1, 8, a.shape[1])
    grads = [cut(grad_expand), cut(grad_reduce), cut(grad_pair)]
    whole = lambda a: pl.BlockSpec(a.shape, lambda i: (0,) * a.ndim)
    rows = pl.BlockSpec((STEP, width), lambda i: (lax.rem(i + 1, steps), 0))
    dma = pltpu.SemaphoreType.DMA
    totals = [(width, hidden), (hidden, width), (width, width), (width, width), (1, width), (1, width)]
    return pl.pallas_call(
        functools.partial(spread_kernel, *scales),
        grid=(steps,),
        in_specs=[
            pl.BlockSpec(memory_space=pl.ANY),
            pl.BlockSpec(memory_space=pl.ANY),
            rows,
            *[whole(g) for g in grads],
            whole(small),
        ],
        out_specs=[rows, *[pl.BlockSpec(t, lambda i: (0, 0)) for t in totals]],
        out_shape=[
            jax.ShapeDtypeStruct((seg_rows, width), BF16),
            *[jax.ShapeDtypeStruct(t, F32) for t in totals],
        ],
        scratch_shapes=[
            pltpu.VMEM((seg_rows + 2 * HALO, width), BF16),
            pltpu.VMEM((4, seg_rows + 2 * HALO), jnp.int32),
            pltpu.VMEM((parts, 8, slab), BF16),
            pltpu.VMEM((parts, 8, slab), BF16),
            pltpu.VMEM((8, slab), F32),
            pltpu.VMEM((tiles, 8, slab), F32),
            pltpu.VMEM((8, slab), BF16),
            pltpu.VMEM((parts, 8, slab), BF16),
            dma((4,)),
            dma((4,)),
            dma((parts,)),
            dma((parts,)),
            dma((tiles,)),
            dma((tiles,)),
            dma((parts,)),
            dma((parts,)),
            dma((2,)),
        ],
        compiler_params=pltpu.CompilerParams(
            vmem_limit_bytes=VMEM_LIMIT, collective_id=1, has_side_effects=True
        ),
        cost_estimate=pl.CostEstimate(
            flops=seg_rows * 384 * 256, bytes_accessed=seg_rows * width * 8, transcendentals=0
        ),
        name="spread_back",
    )(links, shared, direct, *grads, small)


def per_device(
    features, edges, route, cotangent, w_self, w_neighbor, bias, gain, w_expand, w_reduce
):
    feat = features[0]
    links = edges[0].T
    seg_rows, width = feat.shape
    parts = lax.axis_size("dom")
    trip_ids = route[0].reshape(-1)
    rows_dev = trip_ids.shape[0]
    capacity = 2 * rows_dev // parts
    cot_rows = cotangent[0].reshape(rows_dev, width)

    bits = (rows_dev - 1).bit_length()
    keys = (trip_ids.astype(jnp.uint32) << bits) | jnp.arange(rows_dev, dtype=jnp.uint32)
    keys = lax.sort(keys)
    order = jnp.pad((keys & (rows_dev - 1)).astype(jnp.int32), (0, 128))
    sorted_ids = jnp.pad((keys >> bits).astype(jnp.int32).reshape(-1, 128), ((0, 8), (0, 0)))
    edges_of = jnp.arange(parts + 1, dtype=jnp.int32) * seg_rows
    bounds = jnp.sum((trip_ids[None, :] < edges_of[:, None]).astype(jnp.int32), axis=1)
    sent_rows, sent_ids = pack(order, bounds, sorted_ids, cot_rows, parts, capacity, seg_rows)
    msg, hid, slope_pre, act, bend, table, got_rows, _, names = forward(
        links, feat, sent_rows, sent_ids, w_self, w_neighbor, bias[None], gain[None], w_expand
    )
    shared, direct, grad_expand, grad_reduce_t, grad_pair, small = encoder(
        table,
        names,
        got_rows.reshape(parts * capacity, width),
        links,
        feat,
        msg,
        hid,
        slope_pre,
        act,
        bend,
        gain[None],
        w_expand,
        w_reduce,
        w_self,
        w_neighbor,
    )
    tiles = lax.axis_size("rep")
    scales = (
        1.0 / math.sqrt(tiles * parts * seg_rows),
        1.0 / math.sqrt(tiles * parts * rows_dev),
    )
    grad_features, grad_expand, grad_reduce, grad_self, grad_neighbor, grad_bias, grad_gain = spread(
        links, shared, direct, grad_expand, grad_reduce_t, grad_pair, small, scales
    )
    return (
        grad_features[None],
        grad_self,
        grad_neighbor,
        grad_bias[0],
        grad_gain[0],
        grad_expand,
        grad_reduce,
    )


def solution(mesh):
    return jax.shard_map(
        per_device,
        mesh=mesh,
        in_specs=(
            P("rep", "dom", None),
            P("rep", "dom", None),
            P("rep", "dom", None),
            P("rep", "dom", None, None),
            P(),
            P(),
            P(),
            P(),
            P(),
            P(),
        ),
        out_specs=(P("rep", "dom", None), P(), P(), P(), P(), P(), P()),
        check_vma=False,
    )
```

```python
import functools
import math

import jax
import jax.numpy as jnp
from jax import lax
from jax.experimental import pallas as pl
from jax.experimental.pallas import tpu as pltpu
from jax.sharding import PartitionSpec as P

HALO = 128
WIN = 16
GROUP = 256
CHUNK = 256
OWNERS = 8
ROUTE = (
    (2, 1), (1, 2), (2, 3), (3, 2), (2, 2), (0, 2), (2, 0), (1, 1),
    (3, 3), (1, 3), (3, 1), (0, 1), (1, 0), (0, 3), (3, 0),
)
SIDE = 4
PASSES = 2
PIECES = 8
STEP = 1024
SPAN = 2 * STEP
F32 = jnp.float32
BF16 = jnp.bfloat16
VMEM_LIMIT = 56 * 1024 * 1024


def iota(shape, dim, dtype=jnp.int32):
    return lax.broadcasted_iota(jnp.int32, shape, dim).astype(dtype)


def dot(a, b, da=1, db=0):
    return lax.dot_general(a, b, (((da,), (db,)), ((), ())), preferred_element_type=F32)


def sigmoid(value):
    return 0.5 * jnp.tanh(0.5 * value) + 0.5


def pack_kernel(capacity, seg_rows, order, bounds, ids, cot, rows_out, ids_out, rows, stage):
    turn = pl.program_id(0)
    chunk = 512

    @pl.when(turn == 0)
    def _():
        stage[...] = jnp.zeros_like(stage)

        @pl.loop(0, cot.shape[0] // chunk)
        def _(i):
            part = pl.ds(pl.multiple_of(i * chunk, chunk), chunk)
            rows[part, :] = cot[part, :].astype(F32)

    for n in range(OWNERS):
        owner = turn * OWNERS + n
        start = bounds[owner]
        count = bounds[owner + 1] - start
        at = n * capacity

        def move(g, carry):
            base = pl.multiple_of(g * 16, 16)
            for j in range(16):
                source = order[start + base + j]
                stage[pl.ds(base + (at + j), 1), :] = rows[pl.ds(source, 1), :]
            return carry

        lax.fori_loop(0, (count + 15) // 16, move, 0)
        rows_out[n] = stage[at : at + capacity, :].astype(BF16)

        lines = capacity // 128
        shift = lax.rem(start, 128)
        window = ids[pl.ds(start // 128, 8), :]
        turned = pltpu.roll(window, lax.rem(128 - shift, 128), 1)
        lane = iota((lines, 128), 1)
        joined = jnp.where(lane < 128 - shift, turned[:lines], turned[1 : lines + 1])
        place = iota((lines, 128), 0) * 128 + lane
        ids_out[n] = jnp.where(place < count, joined - owner * seg_rows, seg_rows)


def pack(order, bounds, ids, cot, parts, capacity, seg_rows):
    rows_dev, width = cot.shape
    return pl.pallas_call(
        functools.partial(pack_kernel, capacity, seg_rows),
        grid_spec=pltpu.PrefetchScalarGridSpec(
            num_scalar_prefetch=2,
            grid=(parts // OWNERS,),
            in_specs=[
                pl.BlockSpec(ids.shape, lambda i, *_: (0, 0)),
                pl.BlockSpec(cot.shape, lambda i, *_: (0, 0)),
            ],
            out_specs=[
                pl.BlockSpec((OWNERS, capacity, width), lambda i, *_: (i, 0, 0)),
                pl.BlockSpec((OWNERS, capacity // 128, 128), lambda i, *_: (i, 0, 0)),
            ],
            scratch_shapes=[
                pltpu.VMEM((rows_dev, width), F32),
                pltpu.VMEM((OWNERS * capacity, width), F32),
            ],
        ),
        out_shape=[
            jax.ShapeDtypeStruct((parts, capacity, width), BF16),
            jax.ShapeDtypeStruct((parts, capacity // 128, 128), jnp.int32),
        ],
        compiler_params=pltpu.CompilerParams(vmem_limit_bytes=VMEM_LIMIT),
        name="pack_rows",
    )(order, bounds, ids, cot)


def hits(local, shift, same):
    rows = iota((128, 128), 0, F32).astype(BF16)
    table = same
    for slot in range(4):
        wanted = jnp.broadcast_to(local[slot : slot + 1, :] + shift, (16, 128)).astype(BF16)
        wanted = jnp.concatenate([wanted] * 8, axis=0)
        hit = jnp.where(wanted == rows, jnp.ones((), BF16), jnp.zeros((), BF16))
        table = hit if table is None else table + hit
    return table


def identity():
    return jnp.where(iota((128, 128), 0) == iota((128, 128), 1), 1.0, 0.0).astype(BF16)


def ends(links):
    lane = iota(links.shape, 1)
    return jnp.where(links != 0, links + lane, -100000).astype(F32)


def normalised(hid):
    values = hid.astype(F32)
    rate = lax.rsqrt(jnp.mean(values * values, axis=-1, keepdims=True) + 1e-06)
    return values * rate, rate


def remote(source, target, send, recv, device):
    return pltpu.make_async_remote_copy(
        src_ref=source,
        dst_ref=target,
        send_sem=send,
        recv_sem=recv,
        device_id=device,
        device_id_type=pl.DeviceIdType.MESH,
    )


def greet(barrier, device):
    pl.semaphore_signal(barrier, inc=1, device_id=device, device_id_type=pl.DeviceIdType.MESH)


def forward_kernel(
    links,
    feat,
    sent_rows,
    sent_ids,
    w_self,
    w_neighbor,
    bias,
    gain,
    w_expand,
    msg_out,
    hid_out,
    slope_out,
    act_out,
    bend_out,
    table_out,
    got_rows,
    got_ids,
    names_out,
    ext,
    w_cat,
    ids,
    names,
    halo_send,
    halo_recv,
    rows_send,
    rows_recv,
    ids_send,
    ids_recv,
    sem,
):
    step = pl.program_id(0)
    steps = pl.num_programs(0)
    seg_rows, width = feat.shape
    parts = got_ids.shape[0]
    me, tile = lax.axis_index("dom"), lax.axis_index("rep")
    right, left = lax.rem(me + 1, parts), lax.rem(me + parts - 1, parts)

    def halos():
        tail, head = pl.ds(seg_rows - HALO, HALO), pl.ds(0, HALO)
        far, lanes = pl.ds(seg_rows + HALO, HALO), pl.ds(0, width)
        for n, (source, target, device) in enumerate(
            (
                (feat.at[tail, :], ext.at[head, lanes], right),
                (feat.at[head, :], ext.at[far, lanes], left),
            )
        ):
            yield remote(source, target, halo_send.at[n], halo_recv.at[n], (tile, device))

    def half(h):
        size = sent_rows.shape[1] // PASSES
        return pl.ds(h * size, size)

    def rows_copy(to, h):
        return remote(
            sent_rows.at[to, half(h)],
            got_rows.at[me, half(h)],
            rows_send.at[h, to],
            rows_recv.at[h, me],
            (tile, to),
        )

    def rows_arrival(at, h):
        return remote(
            sent_rows.at[at, half(h)],
            got_rows.at[at, half(h)],
            rows_send.at[h, at],
            rows_recv.at[h, at],
            (tile, at),
        )

    def ids_copy(to):
        return remote(sent_ids.at[to], got_ids.at[me], ids_send.at[to], ids_recv.at[me], (tile, to))

    def ids_arrival(at):
        return remote(sent_ids.at[at], got_ids.at[at], ids_send.at[at], ids_recv.at[at], (tile, at))

    def chip(down, along, swap):
        y, x, core = me // (2 * SIDE), lax.rem(me // 2, SIDE), lax.rem(me, 2)
        there = lax.rem(y + down, SIDE) * SIDE + lax.rem(x + along, SIDE)
        return there * 2 + lax.rem(core + swap, 2)

    def own_copies():
        yield pltpu.make_async_copy(sent_rows.at[me], got_rows.at[me], sem.at[1])
        yield pltpu.make_async_copy(sent_ids.at[me], got_ids.at[me], sem.at[2])

    @pl.when(step == 0)
    def _():
        barrier = pltpu.get_barrier_semaphore()

        @pl.loop(1, parts)
        def _(k):
            greet(barrier, (tile, lax.rem(me + k, parts)))

        pl.semaphore_wait(barrier, parts - 1)
        for copy in halos():
            copy.start()

        @pl.loop(1, parts)
        def _(k):
            ids_copy(lax.rem(me + k, parts)).start()

        for h in range(PASSES):
            for swap in range(2):
                for down, along in ROUTE:
                    rows_copy(chip(down, along, swap), h).start()
            rows_copy(chip(0, 0, 1), h).start()
        local = pltpu.make_async_copy(
            feat, ext.at[pl.ds(HALO, seg_rows), pl.ds(0, width)], sem.at[0]
        )
        local.start()
        for copy in own_copies():
            copy.start()
        ext[:, width:] = jnp.ones((ext.shape[0], width), BF16)
        w_cat[:width, :] = w_self[...]
        w_cat[width:, :] = w_neighbor[...]
        local.wait()

    @pl.when(step == steps - 2)
    def _():
        for copy in halos():
            copy.wait_recv()

    start = lax.rem(step + 1, steps) * STEP
    same = identity()
    for j in range(STEP // 128):
        base = pl.multiple_of(start + j * 128, 128)
        local = ends(links[:, j * 128 : (j + 1) * 128])
        table = jnp.concatenate(
            [hits(local, 128.0, None), hits(local, 0.0, same), hits(local, -128.0, None)], axis=0
        )
        summed = dot(table, ext[pl.ds(base, 384), :], 0, 0)
        messages = summed[:, :width] / summed[:, width:]
        msg_out[j * 128 : (j + 1) * 128, :] = messages.astype(BF16)
    own = ext[pl.ds(pl.multiple_of(start + HALO, 128), STEP), :width]
    pre = dot(jnp.concatenate([own, msg_out[...]], axis=1), w_cat[...]) + bias[...]
    gate = sigmoid(pre)
    swish = pre * gate
    hidden = (own.astype(F32) + swish).astype(BF16)
    hid_out[...] = hidden
    slope_out[...] = gate + swish * (1.0 - gate)
    unit, _ = normalised(hidden)
    normed = (unit * gain[...]).astype(BF16)
    for j in range(STEP // CHUNK):
        part = slice(j * CHUNK, (j + 1) * CHUNK)
        inner = dot(normed[part], w_expand[...])
        gate = sigmoid(inner)
        swish = inner * gate
        act_out[part, :] = swish.astype(BF16)
        bend_out[part, :] = (gate + swish * (1.0 - gate)).astype(BF16)

    @pl.when(step == steps - 1)
    def _():
        for copy in own_copies():
            copy.wait()

        @pl.loop(1, parts)
        def _(k):
            ids_arrival(lax.rem(me + k, parts)).wait_recv()

        fetch = pltpu.make_async_copy(got_ids, ids, sem.at[0])
        fetch.start()
        fetch.wait()
        capacity = ids.shape[1] * 128
        stride = capacity + WIN
        place = iota((16, 128), 0)
        weights = jnp.where(place == 0, 128.0, jnp.where(place == 1, 1.0, 0.0)).astype(BF16)
        bound = iota((1, 128), 1, F32) * float(GROUP)
        most = jnp.zeros((1, 128), F32)
        for s in range(parts):
            below = jnp.zeros((1, 128), F32)
            for k in range(ids.shape[1]):
                line = ids[s, k : k + 1, :]
                high = jnp.broadcast_to(line >> 7, (16, 128))
                low = jnp.broadcast_to(line & 127, (16, 128))
                digits = jnp.where(place == 0, high, jnp.where(place == 1, low, 0))
                column = dot(digits.astype(F32).astype(BF16), weights, 0, 0)
                at = s * stride + k * 128
                names[at : at + 128, :] = column
                below += jnp.sum(jnp.where(column < bound, 1.0, 0.0), axis=0, keepdims=True)
            names[s * stride + capacity : (s + 1) * stride, :] = jnp.full((WIN, 128), 1e6, F32)
            table_out[s : s + 1, :] = below.astype(jnp.int32)
            most = jnp.maximum(most, pltpu.roll(below, 127, 1) - below)
        table_out[parts : parts + 8, :] = jnp.broadcast_to(most, (8, 128)).astype(jnp.int32)
        store = pltpu.make_async_copy(names, names_out, sem.at[0])
        store.start()
        for copy in halos():
            copy.wait_send()

        @pl.loop(1, parts)
        def _(k):
            other = lax.rem(me + k, parts)
            ids_copy(other).wait_send()
            for h in range(PASSES):
                rows_arrival(other, h).wait_recv()
                rows_copy(other, h).wait_send()

        store.wait()


def forward(links, feat, sent_rows, sent_ids, w_self, w_neighbor, bias, gain, w_expand):
    seg_rows, width = feat.shape
    hidden = w_expand.shape[1]
    steps, parts = seg_rows // STEP, sent_ids.shape[0]
    columns = parts * (sent_rows.shape[1] + WIN)
    whole = lambda a: pl.BlockSpec(a.shape, lambda i: (0,) * a.ndim)
    rows = lambda n: pl.BlockSpec((STEP, n), lambda i: (lax.rem(i + 1, steps), 0))
    away = pl.BlockSpec(memory_space=pl.ANY)
    dma = pltpu.SemaphoreType.DMA
    return pl.pallas_call(
        forward_kernel,
        grid=(steps,),
        in_specs=[
            pl.BlockSpec((4, STEP), lambda i: (0, lax.rem(i + 1, steps))),
            away,
            away,
            away,
            whole(w_self),
            whole(w_neighbor),
            whole(bias),
            whole(gain),
            whole(w_expand),
        ],
        out_specs=[
            rows(width),
            rows(width),
            rows(width),
            rows(hidden),
            rows(hidden),
            pl.BlockSpec((parts + 8, 128), lambda i: (0, 0)),
            away,
            away,
            away,
        ],
        out_shape=[
            jax.ShapeDtypeStruct((seg_rows, width), BF16),
            jax.ShapeDtypeStruct((seg_rows, width), BF16),
            jax.ShapeDtypeStruct((seg_rows, width), F32),
            jax.ShapeDtypeStruct((seg_rows, hidden), BF16),
            jax.ShapeDtypeStruct((seg_rows, hidden), BF16),
            jax.ShapeDtypeStruct((parts + 8, 128), jnp.int32),
            jax.ShapeDtypeStruct(sent_rows.shape, BF16),
            jax.ShapeDtypeStruct(sent_ids.shape, jnp.int32),
            jax.ShapeDtypeStruct((columns, 128), F32),
        ],
        scratch_shapes=[
            pltpu.VMEM((seg_rows + 2 * HALO, 2 * width), BF16),
            pltpu.VMEM((2 * width, width), BF16),
            pltpu.VMEM(sent_ids.shape, jnp.int32),
            pltpu.VMEM((columns, 128), F32),
            dma((2,)),
            dma((2,)),
            dma((PASSES, parts)),
            dma((PASSES, parts)),
            dma((parts,)),
            dma((parts,)),
            dma((3,)),
        ],
        compiler_params=pltpu.CompilerParams(
            vmem_limit_bytes=VMEM_LIMIT, collective_id=2, has_side_effects=True
        ),
        cost_estimate=pl.CostEstimate(
            flops=seg_rows * 384 * 512, bytes_accessed=seg_rows * width * 12, transcendentals=0
        ),
        name="forward_messages",
    )(links, feat, sent_rows, sent_ids, w_self, w_neighbor, bias, gain, w_expand)


def encoder_kernel(
    table_s,
    names_in,
    got,
    links,
    feat,
    msg,
    hid,
    slope_pre,
    act,
    bend,
    gain,
    w_expand,
    w_reduce,
    w_self,
    w_neighbor,
    shared_out,
    direct_out,
    ge_out,
    gr_out,
    gs_out,
    small_out,
    landed,
    rows,
    names,
    stage,
    onehot,
    cot_a,
    cot_b,
    low_s,
    inner_s,
    pair_s,
    w_back,
    sem,
):
    step = pl.program_id(0)
    width = feat.shape[1]
    sources = table_s.shape[0] - 8
    capacity = got.shape[0] // sources
    stride = capacity + WIN

    @pl.when(step == 0)
    def _():
        fetch = pltpu.make_async_copy(got, landed, sem.at[0])
        label = pltpu.make_async_copy(names_in, names, sem.at[1])
        fetch.start()
        label.start()
        w_back[:, :width] = w_neighbor[...].astype(F32).T.astype(BF16)
        w_back[:, width:] = w_self[...].astype(F32).T.astype(BF16)
        for total in (ge_out, gr_out, pair_s, small_out):
            total[...] = jnp.zeros_like(total)
        fetch.wait()
        for s in range(sources):
            rows[s * stride : s * stride + capacity, :] = landed[
                s * capacity : (s + 1) * capacity, :
            ].astype(F32)
            rows[s * stride + capacity : (s + 1) * stride, :] = jnp.zeros((WIN, 128), F32)
        label.wait()

    def collect(block, turn, j):
        first = (block * GROUP).astype(F32)
        left = iota((WIN, 128), 1, F32) + first
        for s in range(sources):
            at = jnp.minimum(table_s[s, block] + turn * WIN, capacity) + s * stride
            name = names[pl.ds(at, WIN), :]
            stage[j, s * WIN : (s + 1) * WIN, :] = rows[pl.ds(at, WIN), :].astype(BF16)
            for k in range(GROUP // 128):
                onehot[j, s * WIN : (s + 1) * WIN, k * 128 : (k + 1) * 128] = jnp.where(
                    name == left + 128.0 * k, 1.0, 0.0
                ).astype(BF16)
        return dot(onehot[j], stage[j], 0, 0)

    def gather(target, first):
        blocks = [jnp.minimum(first + j, last) for j in range(STEP // GROUP)]
        for j, block in enumerate(blocks):
            target[j * GROUP : (j + 1) * GROUP, :] = collect(block, 0, j)

    def overflow(target, first):
        for j in range(STEP // GROUP):
            block = jnp.minimum(first + j, last)
            turns = (table_s[sources, block] + (WIN - 1)) // WIN

            @pl.when(turns > 1)
            def _():
                @pl.loop(1, turns)
                def _(turn):
                    target[j * GROUP : (j + 1) * GROUP, :] += collect(block, turn, j)

    def encode(part, cot_s):
        scale = gain[...]
        unit, rate = normalised(hid[part, :])
        normed = (unit * scale).astype(BF16)
        low_s[...] = cot_s[...].astype(BF16)
        for j in range(STEP // CHUNK):
            rows_at = slice(j * CHUNK, (j + 1) * CHUNK)
            back_active = dot(low_s[rows_at, :], w_reduce[...], 1, 1)
            gates = bend[part.start + j * CHUNK : part.start + (j + 1) * CHUNK, :]
            inner_s[rows_at, :] = (back_active * gates.astype(F32)).astype(BF16)
        gr_out[...] += dot(low_s[...], act[part, :], 0, 0)
        ge_out[...] += dot(normed, inner_s[...], 0, 0)
        back_normed = dot(inner_s[...], w_expand[...], 1, 1)
        small_out[0:1, :] += jnp.sum(back_normed * unit, axis=0, keepdims=True)
        weighted = scale * back_normed
        mean = jnp.mean(weighted * unit, axis=-1, keepdims=True)
        back_hidden = cot_s[...] + (weighted - unit * mean) * rate
        back_pre = back_hidden * slope_pre[part, :]
        low = back_pre.astype(BF16)
        small_out[1:2, :] += jnp.sum(low.astype(F32), axis=0, keepdims=True)
        pair_s[...] += dot(low, jnp.concatenate([feat[part, :], msg[part, :]], axis=1), 0, 0)
        both = dot(low, w_back[...])
        used = jnp.sum(jnp.where(links[:, part] != 0, 1.0, 0.0), axis=0, keepdims=True)
        used = jnp.broadcast_to(used, (16, STEP)).astype(BF16)
        degree = 1.0 + dot(used, jnp.full((16, 128), 1.0 / 16.0, BF16), 0, 0)
        shared_out[part, :] = (both[:, :width] / degree).astype(BF16)
        direct_out[part, :] = back_hidden + both[:, width:]

    blocks = STEP // GROUP
    last = pl.num_programs(0) * (SPAN // GROUP) - 1

    @pl.when(step == 0)
    def _():
        gather(cot_a, 0)
        overflow(cot_a, 0)

    head, tail = slice(0, STEP), slice(STEP, SPAN)
    gather(cot_b, 2 * step * blocks + blocks)
    encode(head, cot_a)
    overflow(cot_b, 2 * step * blocks + blocks)
    encode(tail, cot_b)
    gather(cot_a, 2 * step * blocks + 2 * blocks)
    overflow(cot_a, 2 * step * blocks + 2 * blocks)

    @pl.when(step == pl.num_programs(0) - 1)
    def _():
        gs_out[...] = pair_s[...].T


def encoder(
    table, names, got, links, feat, msg, hid, slope_pre, act, bend, gain, w_expand, w_reduce, w_self, w_neighbor
):
    seg_rows, width = feat.shape
    sources, hidden = table.shape[0] - 8, w_expand.shape[1]
    whole = lambda shape: pl.BlockSpec(shape, lambda i: (0,) * len(shape))
    rows = pl.BlockSpec((SPAN, width), lambda i: (i, 0))
    wide = pl.BlockSpec((SPAN, hidden), lambda i: (i, 0))
    return pl.pallas_call(
        encoder_kernel,
        grid=(seg_rows // SPAN,),
        in_specs=[
            pl.BlockSpec(memory_space=pltpu.SMEM),
            pl.BlockSpec(memory_space=pl.ANY),
            pl.BlockSpec(memory_space=pl.ANY),
            pl.BlockSpec((4, SPAN), lambda i: (0, i)),
            rows,
            rows,
            rows,
            rows,
            wide,
            wide,
            whole((1, width)),
            whole((width, hidden)),
            whole((hidden, width)),
            whole((width, width)),
            whole((width, width)),
        ],
        out_specs=[
            rows,
            rows,
            whole((width, hidden)),
            whole((width, hidden)),
            whole((2 * width, width)),
            whole((8, width)),
        ],
        out_shape=[
            jax.ShapeDtypeStruct((seg_rows, width), BF16),
            jax.ShapeDtypeStruct((seg_rows, width), F32),
            jax.ShapeDtypeStruct((width, hidden), F32),
            jax.ShapeDtypeStruct((width, hidden), F32),
            jax.ShapeDtypeStruct((2 * width, width), F32),
            jax.ShapeDtypeStruct((8, width), F32),
        ],
        scratch_shapes=[
            pltpu.VMEM(got.shape, BF16),
            pltpu.VMEM(names.shape, F32),
            pltpu.VMEM(names.shape, F32),
            pltpu.VMEM((STEP // GROUP, sources * WIN, width), BF16),
            pltpu.VMEM((STEP // GROUP, sources * WIN, GROUP), BF16),
            pltpu.VMEM((STEP, width), F32),
            pltpu.VMEM((STEP, width), F32),
            pltpu.VMEM((STEP, width), BF16),
            pltpu.VMEM((STEP, hidden), BF16),
            pltpu.VMEM((width, 2 * width), F32),
            pltpu.VMEM((width, 2 * width), BF16),
            pltpu.SemaphoreType.DMA((2,)),
        ],
        compiler_params=pltpu.CompilerParams(vmem_limit_bytes=VMEM_LIMIT),
        cost_estimate=pl.CostEstimate(
            flops=seg_rows * width * hidden * 10, bytes_accessed=seg_rows * width * 20, transcendentals=0
        ),
        name="encoder_backward",
    )(
        table, names, got, links, feat, msg, hid, slope_pre, act, bend, gain, w_expand, w_reduce, w_self, w_neighbor
    )


def spread_kernel(
    graph_scale,
    route_scale,
    links,
    shared,
    direct,
    grad_expand,
    grad_reduce,
    grad_pair,
    small,
    out,
    expand_out,
    reduce_out,
    self_out,
    neighbor_out,
    bias_out,
    gain_out,
    ext,
    links_ext,
    mine,
    parts_in,
    part,
    tiles_in,
    whole,
    wholes_in,
    halo_send,
    halo_recv,
    part_send,
    part_recv,
    tile_send,
    tile_recv,
    whole_send,
    whole_recv,
    sem,
):
    step = pl.program_id(0)
    steps = pl.num_programs(0)
    seg_rows, width = shared.shape
    hidden = expand_out.shape[1]
    parts, tiles = parts_in.shape[0], tiles_in.shape[0]
    half = parts // 2
    me, tile = lax.axis_index("dom"), lax.axis_index("rep")
    right, left = lax.rem(me + 1, parts), lax.rem(me + parts - 1, parts)

    def halos():
        tail = pl.ds(seg_rows - HALO, HALO)
        head = pl.ds(0, HALO)
        far = pl.ds(seg_rows + HALO, HALO)
        for n, (source, target, device) in enumerate(
            (
                (shared.at[tail, :], ext.at[head, :], right),
                (shared.at[head, :], ext.at[far, :], left),
                (links.at[:, tail], links_ext.at[:, head], right),
                (links.at[:, head], links_ext.at[:, far], left),
            )
        ):
            yield remote(source, target, halo_send.at[n], halo_recv.at[n], (tile, device))

    def part_copy(k):
        to = lax.rem(me + k, parts)
        return remote(mine.at[to], parts_in.at[me], part_send.at[k], part_recv.at[me], (tile, to))

    def part_arrival(k):
        at = lax.rem(me + k, parts)
        return remote(mine.at[at], parts_in.at[at], part_send.at[k], part_recv.at[at], (tile, at))

    def tile_copy(k):
        to = lax.rem(tile + k, tiles)
        return remote(part, tiles_in.at[tile], tile_send.at[k], tile_recv.at[tile], (to, me))

    def tile_arrival(k):
        at = lax.rem(tile + k, tiles)
        return remote(part, tiles_in.at[at], tile_send.at[k], tile_recv.at[at], (at, me))

    def whole_copy(k):
        to = lax.rem(me + k, parts)
        return remote(whole, wholes_in.at[me], whole_send.at[k], whole_recv.at[me], (tile, to))

    def whole_arrival(k):
        at = lax.rem(me + k, parts)
        return remote(whole, wholes_in.at[at], whole_send.at[k], whole_recv.at[at], (tile, at))

    @pl.when(step == 0)
    def _():
        barrier = pltpu.get_barrier_semaphore()

        @pl.loop(1, parts)
        def _(k):
            greet(barrier, (tile, lax.rem(me + k, parts)))

        for k in range(1, tiles):
            greet(barrier, (lax.rem(tile + k, tiles), me))
        pl.semaphore_wait(barrier, parts + tiles - 2)
        for copy in halos():
            copy.start()
        mine[:half, :, :hidden] = grad_expand[...].astype(BF16)
        mine[half:, :, :hidden] = grad_reduce[...].astype(BF16)
        mine[:, :, hidden : hidden + width] = grad_pair[...].astype(BF16)
        mine[:, :, hidden + width :] = jnp.broadcast_to(small[...][None], (parts, 8, width)).astype(
            BF16
        )
        @pl.loop(1, parts)
        def _(k):
            part_copy(k).start()

        local = pltpu.make_async_copy(shared, ext.at[pl.ds(HALO, seg_rows), :], sem.at[0])
        edges = pltpu.make_async_copy(links, links_ext.at[:, pl.ds(HALO, seg_rows)], sem.at[1])
        local.start()
        edges.start()
        local.wait()
        edges.wait()

    @pl.when(step == 3)
    def _():
        @pl.loop(1, parts)
        def _(k):
            part_arrival(k).wait_recv()

        parts_in[me] = mine[me]
        part[...] = lax.fori_loop(
            1,
            parts,
            lambda p, total: total + parts_in[p].astype(F32),
            parts_in[0].astype(F32),
        )
        for k in range(1, tiles):
            tile_copy(k).start()

    @pl.when(step == 4)
    def _():
        for k in range(1, tiles):
            tile_arrival(k).wait_recv()
        tiles_in[tile] = part[...]
        total = tiles_in[0]
        for t in range(1, tiles):
            total = total + tiles_in[t]
        whole[...] = total.astype(BF16)

        @pl.loop(1, parts)
        def _(k):
            whole_copy(k).start()

    @pl.when(step == steps - 2)
    def _():
        for copy in halos():
            copy.wait_recv()
        head, far = pl.ds(0, HALO), pl.ds(seg_rows + HALO, HALO)
        links_ext[:, head] = jnp.where(me > 0, links_ext[:, head], 0)
        links_ext[:, far] = jnp.where(me < parts - 1, links_ext[:, far], 0)

    at = lax.rem(step + 1, steps) * SPAN
    same = identity()
    for j in range(SPAN // 128):
        base = pl.multiple_of(at + j * 128, 128)
        near = [
            ends(links_ext[:, pl.ds(pl.multiple_of(base + k * 128, 128), 128)]) for k in range(3)
        ]
        table = jnp.concatenate(
            [hits(near[0], -128.0, None), hits(near[1], 0.0, same), hits(near[2], 128.0, None)],
            axis=1,
        )
        summed = dot(table, ext[pl.ds(base, 384), :])
        rows = slice(j * 128, (j + 1) * 128)
        out[rows, :] = (direct[rows, :] + summed).astype(BF16)

    @pl.when(step == steps - 1)
    def _():
        @pl.loop(1, parts)
        def _(k):
            whole_arrival(k).wait_recv()

        wholes_in[me] = whole[...]
        expand = wholes_in[:half, :, :hidden].astype(F32) * route_scale
        reduced = wholes_in[half:, :, :hidden].astype(F32) * route_scale
        pair = wholes_in[:, :, hidden : hidden + width].astype(F32) * graph_scale
        little = wholes_in[0, :, hidden + width :].astype(F32)
        expand_out[...] = expand.reshape(width, hidden)
        reduce_out[...] = reduced.reshape(width, hidden).T
        self_out[...] = pair[:half].reshape(width, width)
        neighbor_out[...] = pair[half:].reshape(width, width)
        gain_out[...] = little[0:1] * route_scale
        bias_out[...] = little[1:2] * graph_scale
        for copy in halos():
            copy.wait_send()

        @pl.loop(1, parts)
        def _(k):
            part_copy(k).wait_send()
            whole_copy(k).wait_send()

        for k in range(1, tiles):
            tile_copy(k).wait_send()


def spread(links, shared, direct, grad_expand, grad_reduce, grad_pair, small, scales):
    seg_rows, width = shared.shape
    hidden = grad_expand.shape[1]
    parts, tiles = lax.axis_size("dom"), lax.axis_size("rep")
    steps = seg_rows // SPAN
    slab = hidden + 2 * width
    cut = lambda a: a.reshape(-1, 8, a.shape[1])
    grads = [cut(grad_expand), cut(grad_reduce), cut(grad_pair)]
    whole = lambda a: pl.BlockSpec(a.shape, lambda i: (0,) * a.ndim)
    rows = pl.BlockSpec((SPAN, width), lambda i: (lax.rem(i + 1, steps), 0))
    dma = pltpu.SemaphoreType.DMA
    totals = [(width, hidden), (hidden, width), (width, width), (width, width), (1, width), (1, width)]
    return pl.pallas_call(
        functools.partial(spread_kernel, *scales),
        grid=(steps,),
        in_specs=[
            pl.BlockSpec(memory_space=pl.ANY),
            pl.BlockSpec(memory_space=pl.ANY),
            rows,
            *[whole(g) for g in grads],
            whole(small),
        ],
        out_specs=[rows, *[pl.BlockSpec(t, lambda i: (0, 0)) for t in totals]],
        out_shape=[
            jax.ShapeDtypeStruct((seg_rows, width), BF16),
            *[jax.ShapeDtypeStruct(t, F32) for t in totals],
        ],
        scratch_shapes=[
            pltpu.VMEM((seg_rows + 2 * HALO, width), BF16),
            pltpu.VMEM((4, seg_rows + 2 * HALO), jnp.int32),
            pltpu.VMEM((parts, 8, slab), BF16),
            pltpu.VMEM((parts, 8, slab), BF16),
            pltpu.VMEM((8, slab), F32),
            pltpu.VMEM((tiles, 8, slab), F32),
            pltpu.VMEM((8, slab), BF16),
            pltpu.VMEM((parts, 8, slab), BF16),
            dma((4,)),
            dma((4,)),
            dma((parts,)),
            dma((parts,)),
            dma((tiles,)),
            dma((tiles,)),
            dma((parts,)),
            dma((parts,)),
            dma((2,)),
        ],
        compiler_params=pltpu.CompilerParams(
            vmem_limit_bytes=VMEM_LIMIT, collective_id=1, has_side_effects=True
        ),
        cost_estimate=pl.CostEstimate(
            flops=seg_rows * 384 * 256, bytes_accessed=seg_rows * width * 8, transcendentals=0
        ),
        name="spread_back",
    )(links, shared, direct, *grads, small)


def finish_kernel(*refs):
    count = len(refs) // 2
    sources, targets, sem = refs[:count], refs[count : 2 * count], refs[-1]
    copies = []
    piece = sources[0].shape[0] // PIECES
    for n in range(PIECES):
        part = pl.ds(n * piece, piece)
        copies.append((sources[0].at[part, :], targets[0].at[part, :]))
    copies.extend(zip(sources[1:], targets[1:]))
    copies = [pltpu.make_async_copy(a, b, sem.at[n]) for n, (a, b) in enumerate(copies)]
    for copy in copies:
        copy.start()
    for copy in copies:
        copy.wait()


def finish(arrays):
    away = pl.BlockSpec(memory_space=pl.ANY)
    return pl.pallas_call(
        finish_kernel,
        in_specs=[away] * len(arrays),
        out_specs=[away] * len(arrays),
        out_shape=[jax.ShapeDtypeStruct(a.shape, a.dtype) for a in arrays],
        scratch_shapes=[pltpu.SemaphoreType.DMA((PIECES + len(arrays) - 1,))],
        compiler_params=pltpu.CompilerParams(vmem_limit_bytes=VMEM_LIMIT),
        name="finish",
    )(*arrays)


def per_device(
    features, edges, route, cotangent, w_self, w_neighbor, bias, gain, w_expand, w_reduce
):
    feat = features[0]
    links = edges[0].T
    seg_rows, width = feat.shape
    parts = lax.axis_size("dom")
    trip_ids = route[0].reshape(-1)
    rows_dev = trip_ids.shape[0]
    capacity = 2 * rows_dev // parts
    cot_rows = cotangent[0].reshape(rows_dev, width)

    bits = (rows_dev - 1).bit_length()
    keys = (trip_ids.astype(jnp.uint32) << bits) | jnp.arange(rows_dev, dtype=jnp.uint32)
    keys = jnp.pad(lax.sort(keys, is_stable=False), (0, 1024))
    order = (keys & (rows_dev - 1)).astype(jnp.int32)
    sorted_ids = (keys >> bits).astype(jnp.int32).reshape(-1, 128)
    edges_of = jnp.arange(parts + 1, dtype=jnp.int32) * seg_rows
    bounds = jnp.sum((trip_ids[None, :] < edges_of[:, None]).astype(jnp.int32), axis=1)
    sent_rows, sent_ids = pack(order, bounds, sorted_ids, cot_rows, parts, capacity, seg_rows)
    msg, hid, slope_pre, act, bend, table, got_rows, _, names = forward(
        links, feat, sent_rows, sent_ids, w_self, w_neighbor, bias[None], gain[None], w_expand
    )
    shared, direct, grad_expand, grad_reduce_t, grad_pair, small = encoder(
        table,
        names,
        got_rows.reshape(parts * capacity, width),
        links,
        feat,
        msg,
        hid,
        slope_pre,
        act,
        bend,
        gain[None],
        w_expand,
        w_reduce,
        w_self,
        w_neighbor,
    )
    tiles = lax.axis_size("rep")
    scales = (
        1.0 / math.sqrt(tiles * parts * seg_rows),
        1.0 / math.sqrt(tiles * parts * rows_dev),
    )
    results = spread(links, shared, direct, grad_expand, grad_reduce_t, grad_pair, small, scales)
    grad_features, grad_expand, grad_reduce, grad_self, grad_neighbor, grad_bias, grad_gain = finish(
        results
    )
    return (
        grad_features[None],
        grad_self,
        grad_neighbor,
        grad_bias[0],
        grad_gain[0],
        grad_expand,
        grad_reduce,
    )


def solution(mesh):
    return jax.shard_map(
        per_device,
        mesh=mesh,
        in_specs=(
            P("rep", "dom", None),
            P("rep", "dom", None),
            P("rep", "dom", None),
            P("rep", "dom", None, None),
            P(),
            P(),
            P(),
            P(),
            P(),
            P(),
        ),
        out_specs=(P("rep", "dom", None), P(), P(), P(), P(), P(), P()),
        check_vma=False,
    )
```

```python
import functools
import math

import jax
import jax.numpy as jnp
from jax import lax
from jax.experimental import pallas as pl
from jax.experimental.pallas import tpu as pltpu
from jax.sharding import PartitionSpec as P

HALO = 128
WIN = 16
GROUP = 256
CHUNK = 256
OWNERS = 4
ROUTE = (
    (2, 1), (1, 2), (2, 3), (3, 2), (2, 2), (0, 2), (2, 0), (1, 1),
    (3, 3), (1, 3), (3, 1), (0, 1), (1, 0), (0, 3), (3, 0),
)
SIDE = 4
PASSES = 2
PIECES = 4
STEP = 1024
SPAN = 2 * STEP
F32 = jnp.float32
BF16 = jnp.bfloat16
VMEM_LIMIT = 56 * 1024 * 1024


def iota(shape, dim, dtype=jnp.int32):
    return lax.broadcasted_iota(jnp.int32, shape, dim).astype(dtype)


def dot(a, b, da=1, db=0):
    return lax.dot_general(a, b, (((da,), (db,)), ((), ())), preferred_element_type=F32)


def sigmoid(value):
    return 0.5 * jnp.tanh(0.5 * value) + 0.5


def pack_kernel(capacity, seg_rows, order, bounds, ids, cot, rows_out, ids_out, rows, stage):
    turn = pl.program_id(0)
    chunk = 512

    @pl.when(turn == 0)
    def _():
        stage[...] = jnp.zeros_like(stage)

        @pl.loop(0, cot.shape[0] // chunk)
        def _(i):
            part = pl.ds(pl.multiple_of(i * chunk, chunk), chunk)
            rows[part, :] = cot[part, :].astype(F32)

    for n in range(OWNERS):
        owner = turn * OWNERS + n
        start = bounds[owner]
        count = bounds[owner + 1] - start
        at = n * capacity

        def move(g, carry):
            base = pl.multiple_of(g * 16, 16)
            for j in range(16):
                source = order[start + base + j]
                stage[pl.ds(base + (at + j), 1), :] = rows[pl.ds(source, 1), :]
            return carry

        lax.fori_loop(0, (count + 15) // 16, move, 0)
        rows_out[n] = stage[at : at + capacity, :].astype(BF16)

        lines = capacity // 128
        shift = lax.rem(start, 128)
        window = ids[pl.ds(start // 128, 8), :]
        turned = pltpu.roll(window, lax.rem(128 - shift, 128), 1)
        lane = iota((lines, 128), 1)
        joined = jnp.where(lane < 128 - shift, turned[:lines], turned[1 : lines + 1])
        place = iota((lines, 128), 0) * 128 + lane
        ids_out[n] = jnp.where(place < count, joined - owner * seg_rows, seg_rows)


def pack(order, bounds, ids, cot, parts, capacity, seg_rows):
    rows_dev, width = cot.shape
    return pl.pallas_call(
        functools.partial(pack_kernel, capacity, seg_rows),
        grid_spec=pltpu.PrefetchScalarGridSpec(
            num_scalar_prefetch=2,
            grid=(parts // OWNERS,),
            in_specs=[
                pl.BlockSpec(ids.shape, lambda i, *_: (0, 0)),
                pl.BlockSpec(cot.shape, lambda i, *_: (0, 0)),
            ],
            out_specs=[
                pl.BlockSpec((OWNERS, capacity, width), lambda i, *_: (i, 0, 0)),
                pl.BlockSpec((OWNERS, capacity // 128, 128), lambda i, *_: (i, 0, 0)),
            ],
            scratch_shapes=[
                pltpu.VMEM((rows_dev, width), F32),
                pltpu.VMEM((OWNERS * capacity, width), F32),
            ],
        ),
        out_shape=[
            jax.ShapeDtypeStruct((parts, capacity, width), BF16),
            jax.ShapeDtypeStruct((parts, capacity // 128, 128), jnp.int32),
        ],
        compiler_params=pltpu.CompilerParams(vmem_limit_bytes=VMEM_LIMIT),
        name="pack_rows",
    )(order, bounds, ids, cot)


def hits(local, shift, same):
    rows = iota((128, 128), 0, F32).astype(BF16)
    table = same
    for slot in range(4):
        wanted = jnp.broadcast_to(local[slot : slot + 1, :] + shift, (16, 128)).astype(BF16)
        wanted = jnp.concatenate([wanted] * 8, axis=0)
        hit = jnp.where(wanted == rows, jnp.ones((), BF16), jnp.zeros((), BF16))
        table = hit if table is None else table + hit
    return table


def identity():
    return jnp.where(iota((128, 128), 0) == iota((128, 128), 1), 1.0, 0.0).astype(BF16)


def ends(links):
    lane = iota(links.shape, 1)
    return jnp.where(links != 0, links + lane, -100000).astype(F32)


def normalised(hid):
    values = hid.astype(F32)
    rate = lax.rsqrt(jnp.mean(values * values, axis=-1, keepdims=True) + 1e-06)
    return values * rate, rate


def remote(source, target, send, recv, device):
    return pltpu.make_async_remote_copy(
        src_ref=source,
        dst_ref=target,
        send_sem=send,
        recv_sem=recv,
        device_id=device,
        device_id_type=pl.DeviceIdType.MESH,
    )


def chip(me, down, along, swap):
    y, x, core = me // (2 * SIDE), lax.rem(me // 2, SIDE), lax.rem(me, 2)
    there = lax.rem(y + down, SIDE) * SIDE + lax.rem(x + along, SIDE)
    return there * 2 + lax.rem(core + swap, 2)


def others(me):
    for swap in range(2):
        for down, along in ROUTE:
            yield chip(me, down, along, swap)
    yield chip(me, 0, 0, 1)


def greet(barrier, device):
    pl.semaphore_signal(barrier, inc=1, device_id=device, device_id_type=pl.DeviceIdType.MESH)


def forward_kernel(
    links,
    feat,
    sent_rows,
    sent_ids,
    w_self,
    w_neighbor,
    bias,
    gain,
    w_expand,
    msg_out,
    hid_out,
    slope_out,
    act_out,
    bend_out,
    degree_out,
    table_out,
    got_rows,
    got_ids,
    names_out,
    ext,
    w_cat,
    ids,
    names,
    halo_send,
    halo_recv,
    rows_send,
    rows_recv,
    ids_send,
    ids_recv,
    sem,
):
    step = pl.program_id(0)
    steps = pl.num_programs(0)
    seg_rows, width = feat.shape
    parts = got_ids.shape[0]
    me, tile = lax.axis_index("dom"), lax.axis_index("rep")
    right, left = lax.rem(me + 1, parts), lax.rem(me + parts - 1, parts)

    def halos():
        tail, head = pl.ds(seg_rows - HALO, HALO), pl.ds(0, HALO)
        far, lanes = pl.ds(seg_rows + HALO, HALO), pl.ds(0, width)
        for n, (source, target, device) in enumerate(
            (
                (feat.at[tail, :], ext.at[head, lanes], right),
                (feat.at[head, :], ext.at[far, lanes], left),
            )
        ):
            yield remote(source, target, halo_send.at[n], halo_recv.at[n], (tile, device))

    def half(h):
        size = sent_rows.shape[1] // PASSES
        return pl.ds(h * size, size)

    def rows_copy(to, h):
        return remote(
            sent_rows.at[to, half(h)],
            got_rows.at[me, half(h)],
            rows_send.at[h, to],
            rows_recv.at[h, me],
            (tile, to),
        )

    def rows_arrival(at, h):
        return remote(
            sent_rows.at[at, half(h)],
            got_rows.at[at, half(h)],
            rows_send.at[h, at],
            rows_recv.at[h, at],
            (tile, at),
        )

    def ids_copy(to):
        return remote(sent_ids.at[to], got_ids.at[me], ids_send.at[to], ids_recv.at[me], (tile, to))

    def ids_arrival(at):
        return remote(sent_ids.at[at], got_ids.at[at], ids_send.at[at], ids_recv.at[at], (tile, at))

    def own_copies():
        yield pltpu.make_async_copy(sent_rows.at[me], got_rows.at[me], sem.at[1])
        yield pltpu.make_async_copy(sent_ids.at[me], got_ids.at[me], sem.at[2])

    @pl.when(step == 0)
    def _():
        barrier = pltpu.get_barrier_semaphore()

        @pl.loop(1, parts)
        def _(k):
            greet(barrier, (tile, lax.rem(me + k, parts)))

        pl.semaphore_wait(barrier, parts - 1)
        for copy in halos():
            copy.start()

        @pl.loop(1, parts)
        def _(k):
            ids_copy(lax.rem(me + k, parts)).start()

        for h in range(PASSES):
            for to in others(me):
                rows_copy(to, h).start()
        local = pltpu.make_async_copy(
            feat, ext.at[pl.ds(HALO, seg_rows), pl.ds(0, width)], sem.at[0]
        )
        local.start()
        for copy in own_copies():
            copy.start()
        ext[:, width:] = jnp.ones((ext.shape[0], width), BF16)
        w_cat[:width, :] = w_self[...]
        w_cat[width:, :] = w_neighbor[...]
        local.wait()

    @pl.when(step == steps - 2)
    def _():
        for copy in halos():
            copy.wait_recv()

    start = lax.rem(step + 1, steps) * STEP
    same = identity()
    for j in range(STEP // 128):
        base = pl.multiple_of(start + j * 128, 128)
        local = ends(links[:, j * 128 : (j + 1) * 128])
        table = jnp.concatenate(
            [hits(local, 128.0, None), hits(local, 0.0, same), hits(local, -128.0, None)], axis=0
        )
        summed = dot(table, ext[pl.ds(base, 384), :], 0, 0)
        messages = summed[:, :width] / summed[:, width:]
        degree_out[j * 128 : (j + 1) * 128, :] = summed[:, width:].astype(BF16)
        msg_out[j * 128 : (j + 1) * 128, :] = messages.astype(BF16)
    own = ext[pl.ds(pl.multiple_of(start + HALO, 128), STEP), :width]
    pre = dot(jnp.concatenate([own, msg_out[...]], axis=1), w_cat[...]) + bias[...]
    gate = sigmoid(pre)
    swish = pre * gate
    hidden = (own.astype(F32) + swish).astype(BF16)
    hid_out[...] = hidden
    slope_out[...] = gate + swish * (1.0 - gate)
    unit, _ = normalised(hidden)
    normed = (unit * gain[...]).astype(BF16)
    for j in range(STEP // CHUNK):
        part = slice(j * CHUNK, (j + 1) * CHUNK)
        inner = dot(normed[part], w_expand[...])
        gate = sigmoid(inner)
        swish = inner * gate
        act_out[part, :] = swish.astype(BF16)
        bend_out[part, :] = (gate + swish * (1.0 - gate)).astype(BF16)

    @pl.when(step == steps - 1)
    def _():
        for copy in own_copies():
            copy.wait()

        @pl.loop(1, parts)
        def _(k):
            ids_arrival(lax.rem(me + k, parts)).wait_recv()

        fetch = pltpu.make_async_copy(got_ids, ids, sem.at[0])
        fetch.start()
        fetch.wait()
        capacity = ids.shape[1] * 128
        stride = capacity + WIN
        place = iota((16, 128), 0)
        weights = jnp.where(place == 0, 128.0, jnp.where(place == 1, 1.0, 0.0)).astype(BF16)
        bound = iota((1, 128), 1, F32) * float(GROUP)
        most = jnp.zeros((1, 128), F32)
        for s in range(parts):
            below = jnp.zeros((1, 128), F32)
            for k in range(ids.shape[1]):
                line = ids[s, k : k + 1, :]
                high = jnp.broadcast_to(line >> 7, (16, 128))
                low = jnp.broadcast_to(line & 127, (16, 128))
                digits = jnp.where(place == 0, high, jnp.where(place == 1, low, 0))
                column = dot(digits.astype(F32).astype(BF16), weights, 0, 0)
                at = s * stride + k * 128
                names[at : at + 128, :] = column
                below += jnp.sum(jnp.where(column < bound, 1.0, 0.0), axis=0, keepdims=True)
            names[s * stride + capacity : (s + 1) * stride, :] = jnp.full((WIN, 128), 1e6, F32)
            table_out[s : s + 1, :] = below.astype(jnp.int32)
            most = jnp.maximum(most, pltpu.roll(below, 127, 1) - below)
        table_out[parts : parts + 8, :] = jnp.broadcast_to(most, (8, 128)).astype(jnp.int32)
        store = pltpu.make_async_copy(names, names_out, sem.at[0])
        store.start()
        for copy in halos():
            copy.wait_send()

        @pl.loop(1, parts)
        def _(k):
            other = lax.rem(me + k, parts)
            ids_copy(other).wait_send()
            for h in range(PASSES):
                rows_arrival(other, h).wait_recv()
                rows_copy(other, h).wait_send()

        store.wait()


def forward(links, feat, sent_rows, sent_ids, w_self, w_neighbor, bias, gain, w_expand):
    seg_rows, width = feat.shape
    hidden = w_expand.shape[1]
    steps, parts = seg_rows // STEP, sent_ids.shape[0]
    columns = parts * (sent_rows.shape[1] + WIN)
    whole = lambda a: pl.BlockSpec(a.shape, lambda i: (0,) * a.ndim)
    rows = lambda n: pl.BlockSpec((STEP, n), lambda i: (lax.rem(i + 1, steps), 0))
    away = pl.BlockSpec(memory_space=pl.ANY)
    dma = pltpu.SemaphoreType.DMA
    return pl.pallas_call(
        forward_kernel,
        grid=(steps,),
        in_specs=[
            pl.BlockSpec((4, STEP), lambda i: (0, lax.rem(i + 1, steps))),
            away,
            away,
            away,
            whole(w_self),
            whole(w_neighbor),
            whole(bias),
            whole(gain),
            whole(w_expand),
        ],
        out_specs=[
            rows(width),
            rows(width),
            rows(width),
            rows(hidden),
            rows(hidden),
            rows(width),
            pl.BlockSpec((parts + 8, 128), lambda i: (0, 0)),
            away,
            away,
            away,
        ],
        out_shape=[
            jax.ShapeDtypeStruct((seg_rows, width), BF16),
            jax.ShapeDtypeStruct((seg_rows, width), BF16),
            jax.ShapeDtypeStruct((seg_rows, width), F32),
            jax.ShapeDtypeStruct((seg_rows, hidden), BF16),
            jax.ShapeDtypeStruct((seg_rows, hidden), BF16),
            jax.ShapeDtypeStruct((seg_rows, width), BF16),
            jax.ShapeDtypeStruct((parts + 8, 128), jnp.int32),
            jax.ShapeDtypeStruct(sent_rows.shape, BF16),
            jax.ShapeDtypeStruct(sent_ids.shape, jnp.int32),
            jax.ShapeDtypeStruct((columns, 128), F32),
        ],
        scratch_shapes=[
            pltpu.VMEM((seg_rows + 2 * HALO, 2 * width), BF16),
            pltpu.VMEM((2 * width, width), BF16),
            pltpu.VMEM(sent_ids.shape, jnp.int32),
            pltpu.VMEM((columns, 128), F32),
            dma((2,)),
            dma((2,)),
            dma((PASSES, parts)),
            dma((PASSES, parts)),
            dma((parts,)),
            dma((parts,)),
            dma((3,)),
        ],
        compiler_params=pltpu.CompilerParams(
            vmem_limit_bytes=VMEM_LIMIT, collective_id=2, has_side_effects=True
        ),
        cost_estimate=pl.CostEstimate(
            flops=seg_rows * 384 * 512, bytes_accessed=seg_rows * width * 12, transcendentals=0
        ),
        name="forward_messages",
    )(links, feat, sent_rows, sent_ids, w_self, w_neighbor, bias, gain, w_expand)


def encoder_kernel(
    table_s,
    names_in,
    got,
    degree,
    feat,
    msg,
    hid,
    slope_pre,
    act,
    bend,
    gain,
    w_expand,
    w_reduce,
    w_self,
    w_neighbor,
    shared_out,
    direct_out,
    ge_out,
    gr_out,
    gs_out,
    small_out,
    landed,
    rows,
    names,
    stage,
    onehot,
    cot_a,
    cot_b,
    low_s,
    inner_s,
    pair_s,
    w_back,
    sem,
):
    step = pl.program_id(0)
    width = feat.shape[1]
    sources = table_s.shape[0] - 8
    capacity = got.shape[0] // sources
    stride = capacity + WIN

    @pl.when(step == 0)
    def _():
        fetch = pltpu.make_async_copy(got, landed, sem.at[0])
        label = pltpu.make_async_copy(names_in, names, sem.at[1])
        fetch.start()
        label.start()
        w_back[:, :width] = w_neighbor[...].astype(F32).T.astype(BF16)
        w_back[:, width:] = w_self[...].astype(F32).T.astype(BF16)
        for total in (ge_out, gr_out, pair_s, small_out):
            total[...] = jnp.zeros_like(total)
        fetch.wait()
        for s in range(sources):
            rows[s * stride : s * stride + capacity, :] = landed[
                s * capacity : (s + 1) * capacity, :
            ].astype(F32)
            rows[s * stride + capacity : (s + 1) * stride, :] = jnp.zeros((WIN, 128), F32)
        label.wait()

    def collect(block, turn, j):
        first = (block * GROUP).astype(F32)
        left = iota((WIN, 128), 1, F32) + first
        for s in range(sources):
            at = jnp.minimum(table_s[s, block] + turn * WIN, capacity) + s * stride
            name = names[pl.ds(at, WIN), :]
            stage[j, s * WIN : (s + 1) * WIN, :] = rows[pl.ds(at, WIN), :].astype(BF16)
            for k in range(GROUP // 128):
                onehot[j, s * WIN : (s + 1) * WIN, k * 128 : (k + 1) * 128] = jnp.where(
                    name == left + 128.0 * k, 1.0, 0.0
                ).astype(BF16)
        return dot(onehot[j], stage[j], 0, 0)

    def gather(target, first):
        blocks = [jnp.minimum(first + j, last) for j in range(STEP // GROUP)]
        for j, block in enumerate(blocks):
            target[j * GROUP : (j + 1) * GROUP, :] = collect(block, 0, j)

    def overflow(target, first):
        for j in range(STEP // GROUP):
            block = jnp.minimum(first + j, last)
            turns = (table_s[sources, block] + (WIN - 1)) // WIN

            @pl.when(turns > 1)
            def _():
                @pl.loop(1, turns)
                def _(turn):
                    target[j * GROUP : (j + 1) * GROUP, :] += collect(block, turn, j)

    def encode(part, cot_s):
        scale = gain[...]
        unit, rate = normalised(hid[part, :])
        normed = (unit * scale).astype(BF16)
        low_s[...] = cot_s[...].astype(BF16)
        for j in range(STEP // CHUNK):
            rows_at = slice(j * CHUNK, (j + 1) * CHUNK)
            back_active = dot(low_s[rows_at, :], w_reduce[...], 1, 1)
            gates = bend[part.start + j * CHUNK : part.start + (j + 1) * CHUNK, :]
            inner_s[rows_at, :] = (back_active * gates.astype(F32)).astype(BF16)
        gr_out[...] += dot(low_s[...], act[part, :], 0, 0)
        ge_out[...] += dot(normed, inner_s[...], 0, 0)
        back_normed = dot(inner_s[...], w_expand[...], 1, 1)
        small_out[0:1, :] += jnp.sum(back_normed * unit, axis=0, keepdims=True)
        weighted = scale * back_normed
        mean = jnp.mean(weighted * unit, axis=-1, keepdims=True)
        back_hidden = cot_s[...] + (weighted - unit * mean) * rate
        back_pre = back_hidden * slope_pre[part, :]
        low = back_pre.astype(BF16)
        small_out[1:2, :] += jnp.sum(low.astype(F32), axis=0, keepdims=True)
        pair_s[...] += dot(low, jnp.concatenate([feat[part, :], msg[part, :]], axis=1), 0, 0)
        both = dot(low, w_back[...])
        shared_out[part, :] = (both[:, :width] / degree[part, :].astype(F32)).astype(BF16)
        direct_out[part, :] = back_hidden + both[:, width:]

    blocks = STEP // GROUP
    last = pl.num_programs(0) * (SPAN // GROUP) - 1

    @pl.when(step == 0)
    def _():
        gather(cot_a, 0)
        overflow(cot_a, 0)

    head, tail = slice(0, STEP), slice(STEP, SPAN)
    gather(cot_b, 2 * step * blocks + blocks)
    encode(head, cot_a)
    overflow(cot_b, 2 * step * blocks + blocks)
    encode(tail, cot_b)
    gather(cot_a, 2 * step * blocks + 2 * blocks)
    overflow(cot_a, 2 * step * blocks + 2 * blocks)

    @pl.when(step == pl.num_programs(0) - 1)
    def _():
        gs_out[...] = pair_s[...].T


def encoder(
    table, names, got, degree, feat, msg, hid, slope_pre, act, bend, gain, w_expand, w_reduce, w_self, w_neighbor
):
    seg_rows, width = feat.shape
    sources, hidden = table.shape[0] - 8, w_expand.shape[1]
    whole = lambda shape: pl.BlockSpec(shape, lambda i: (0,) * len(shape))
    rows = pl.BlockSpec((SPAN, width), lambda i: (i, 0))
    wide = pl.BlockSpec((SPAN, hidden), lambda i: (i, 0))
    return pl.pallas_call(
        encoder_kernel,
        grid=(seg_rows // SPAN,),
        in_specs=[
            pl.BlockSpec(memory_space=pltpu.SMEM),
            pl.BlockSpec(memory_space=pl.ANY),
            pl.BlockSpec(memory_space=pl.ANY),
            rows,
            rows,
            rows,
            rows,
            rows,
            wide,
            wide,
            whole((1, width)),
            whole((width, hidden)),
            whole((hidden, width)),
            whole((width, width)),
            whole((width, width)),
        ],
        out_specs=[
            rows,
            rows,
            whole((width, hidden)),
            whole((width, hidden)),
            whole((2 * width, width)),
            whole((8, width)),
        ],
        out_shape=[
            jax.ShapeDtypeStruct((seg_rows, width), BF16),
            jax.ShapeDtypeStruct((seg_rows, width), F32),
            jax.ShapeDtypeStruct((width, hidden), F32),
            jax.ShapeDtypeStruct((width, hidden), F32),
            jax.ShapeDtypeStruct((2 * width, width), F32),
            jax.ShapeDtypeStruct((8, width), F32),
        ],
        scratch_shapes=[
            pltpu.VMEM(got.shape, BF16),
            pltpu.VMEM(names.shape, F32),
            pltpu.VMEM(names.shape, F32),
            pltpu.VMEM((STEP // GROUP, sources * WIN, width), BF16),
            pltpu.VMEM((STEP // GROUP, sources * WIN, GROUP), BF16),
            pltpu.VMEM((STEP, width), F32),
            pltpu.VMEM((STEP, width), F32),
            pltpu.VMEM((STEP, width), BF16),
            pltpu.VMEM((STEP, hidden), BF16),
            pltpu.VMEM((width, 2 * width), F32),
            pltpu.VMEM((width, 2 * width), BF16),
            pltpu.SemaphoreType.DMA((2,)),
        ],
        compiler_params=pltpu.CompilerParams(vmem_limit_bytes=VMEM_LIMIT),
        cost_estimate=pl.CostEstimate(
            flops=seg_rows * width * hidden * 10, bytes_accessed=seg_rows * width * 20, transcendentals=0
        ),
        name="encoder_backward",
    )(
        table, names, got, degree, feat, msg, hid, slope_pre, act, bend, gain, w_expand, w_reduce, w_self, w_neighbor
    )


def spread_kernel(
    graph_scale,
    route_scale,
    links,
    shared,
    direct,
    grad_expand,
    grad_reduce,
    grad_pair,
    small,
    out,
    expand_out,
    reduce_out,
    self_out,
    neighbor_out,
    bias_out,
    gain_out,
    ext,
    links_ext,
    mine,
    parts_in,
    part,
    tiles_in,
    whole,
    wholes_in,
    halo_send,
    halo_recv,
    part_send,
    part_recv,
    tile_send,
    tile_recv,
    whole_send,
    whole_recv,
    sem,
):
    step = pl.program_id(0)
    steps = pl.num_programs(0)
    seg_rows, width = shared.shape
    hidden = expand_out.shape[1]
    parts, tiles = parts_in.shape[0], tiles_in.shape[0]
    half = parts // 2
    me, tile = lax.axis_index("dom"), lax.axis_index("rep")
    right, left = lax.rem(me + 1, parts), lax.rem(me + parts - 1, parts)

    def halos():
        tail = pl.ds(seg_rows - HALO, HALO)
        head = pl.ds(0, HALO)
        far = pl.ds(seg_rows + HALO, HALO)
        for n, (source, target, device) in enumerate(
            (
                (shared.at[tail, :], ext.at[head, :], right),
                (shared.at[head, :], ext.at[far, :], left),
                (links.at[:, tail], links_ext.at[:, head], right),
                (links.at[:, head], links_ext.at[:, far], left),
            )
        ):
            yield remote(source, target, halo_send.at[n], halo_recv.at[n], (tile, device))

    def part_copy(to):
        return remote(mine.at[to], parts_in.at[me], part_send.at[to], part_recv.at[me], (tile, to))

    def part_arrival(at):
        return remote(mine.at[at], parts_in.at[at], part_send.at[at], part_recv.at[at], (tile, at))

    def tile_copy(k):
        to = lax.rem(tile + k, tiles)
        return remote(part, tiles_in.at[tile], tile_send.at[k], tile_recv.at[tile], (to, me))

    def tile_arrival(k):
        at = lax.rem(tile + k, tiles)
        return remote(part, tiles_in.at[at], tile_send.at[k], tile_recv.at[at], (at, me))

    def whole_copy(to):
        return remote(whole, wholes_in.at[me], whole_send.at[to], whole_recv.at[me], (tile, to))

    def whole_arrival(at):
        return remote(whole, wholes_in.at[at], whole_send.at[at], whole_recv.at[at], (tile, at))

    @pl.when(step == 0)
    def _():
        barrier = pltpu.get_barrier_semaphore()

        @pl.loop(1, parts)
        def _(k):
            greet(barrier, (tile, lax.rem(me + k, parts)))

        for k in range(1, tiles):
            greet(barrier, (lax.rem(tile + k, tiles), me))
        pl.semaphore_wait(barrier, parts + tiles - 2)
        for copy in halos():
            copy.start()
        mine[:half, :, :hidden] = grad_expand[...].astype(BF16)
        mine[half:, :, :hidden] = grad_reduce[...].astype(BF16)
        mine[:, :, hidden : hidden + width] = grad_pair[...].astype(BF16)
        mine[:, :, hidden + width :] = jnp.broadcast_to(small[...][None], (parts, 8, width)).astype(
            BF16
        )
        for to in others(me):
            part_copy(to).start()

        local = pltpu.make_async_copy(shared, ext.at[pl.ds(HALO, seg_rows), :], sem.at[0])
        edges = pltpu.make_async_copy(links, links_ext.at[:, pl.ds(HALO, seg_rows)], sem.at[1])
        local.start()
        edges.start()
        local.wait()
        edges.wait()

    @pl.when(step == 3)
    def _():
        @pl.loop(1, parts)
        def _(k):
            part_arrival(lax.rem(me + k, parts)).wait_recv()

        parts_in[me] = mine[me]
        part[...] = lax.fori_loop(
            1,
            parts,
            lambda p, total: total + parts_in[p].astype(F32),
            parts_in[0].astype(F32),
        )
        for k in range(1, tiles):
            tile_copy(k).start()

    @pl.when(step == 4)
    def _():
        for k in range(1, tiles):
            tile_arrival(k).wait_recv()
        tiles_in[tile] = part[...]
        total = tiles_in[0]
        for t in range(1, tiles):
            total = total + tiles_in[t]
        whole[...] = total.astype(BF16)
        for to in others(me):
            whole_copy(to).start()

    @pl.when(step == steps - 2)
    def _():
        for copy in halos():
            copy.wait_recv()
        head, far = pl.ds(0, HALO), pl.ds(seg_rows + HALO, HALO)
        links_ext[:, head] = jnp.where(me > 0, links_ext[:, head], 0)
        links_ext[:, far] = jnp.where(me < parts - 1, links_ext[:, far], 0)

    at = lax.rem(step + 1, steps) * SPAN
    same = identity()
    for j in range(SPAN // 128):
        base = pl.multiple_of(at + j * 128, 128)
        near = [
            ends(links_ext[:, pl.ds(pl.multiple_of(base + k * 128, 128), 128)]) for k in range(3)
        ]
        table = jnp.concatenate(
            [hits(near[0], -128.0, None), hits(near[1], 0.0, same), hits(near[2], 128.0, None)],
            axis=1,
        )
        summed = dot(table, ext[pl.ds(base, 384), :])
        rows = slice(j * 128, (j + 1) * 128)
        out[rows, :] = (direct[rows, :] + summed).astype(BF16)

    @pl.when(step == steps - 1)
    def _():
        @pl.loop(1, parts)
        def _(k):
            whole_arrival(lax.rem(me + k, parts)).wait_recv()

        wholes_in[me] = whole[...]
        expand = wholes_in[:half, :, :hidden].astype(F32) * route_scale
        reduced = wholes_in[half:, :, :hidden].astype(F32) * route_scale
        pair = wholes_in[:, :, hidden : hidden + width].astype(F32) * graph_scale
        little = wholes_in[0, :, hidden + width :].astype(F32)
        expand_out[...] = expand.reshape(width, hidden)
        reduce_out[...] = reduced.reshape(width, hidden).T
        self_out[...] = pair[:half].reshape(width, width)
        neighbor_out[...] = pair[half:].reshape(width, width)
        gain_out[...] = little[0:1] * route_scale
        bias_out[...] = little[1:2] * graph_scale
        for copy in halos():
            copy.wait_send()

        @pl.loop(1, parts)
        def _(k):
            part_copy(lax.rem(me + k, parts)).wait_send()
            whole_copy(lax.rem(me + k, parts)).wait_send()

        for k in range(1, tiles):
            tile_copy(k).wait_send()


def spread(links, shared, direct, grad_expand, grad_reduce, grad_pair, small, scales):
    seg_rows, width = shared.shape
    hidden = grad_expand.shape[1]
    parts, tiles = lax.axis_size("dom"), lax.axis_size("rep")
    steps = seg_rows // SPAN
    slab = hidden + 2 * width
    cut = lambda a: a.reshape(-1, 8, a.shape[1])
    grads = [cut(grad_expand), cut(grad_reduce), cut(grad_pair)]
    whole = lambda a: pl.BlockSpec(a.shape, lambda i: (0,) * a.ndim)
    rows = pl.BlockSpec((SPAN, width), lambda i: (lax.rem(i + 1, steps), 0))
    dma = pltpu.SemaphoreType.DMA
    totals = [(width, hidden), (hidden, width), (width, width), (width, width), (1, width), (1, width)]
    return pl.pallas_call(
        functools.partial(spread_kernel, *scales),
        grid=(steps,),
        in_specs=[
            pl.BlockSpec(memory_space=pl.ANY),
            pl.BlockSpec(memory_space=pl.ANY),
            rows,
            *[whole(g) for g in grads],
            whole(small),
        ],
        out_specs=[rows, *[pl.BlockSpec(t, lambda i: (0, 0)) for t in totals]],
        out_shape=[
            jax.ShapeDtypeStruct((seg_rows, width), BF16),
            *[jax.ShapeDtypeStruct(t, F32) for t in totals],
        ],
        scratch_shapes=[
            pltpu.VMEM((seg_rows + 2 * HALO, width), BF16),
            pltpu.VMEM((4, seg_rows + 2 * HALO), jnp.int32),
            pltpu.VMEM((parts, 8, slab), BF16),
            pltpu.VMEM((parts, 8, slab), BF16),
            pltpu.VMEM((8, slab), F32),
            pltpu.VMEM((tiles, 8, slab), F32),
            pltpu.VMEM((8, slab), BF16),
            pltpu.VMEM((parts, 8, slab), BF16),
            dma((4,)),
            dma((4,)),
            dma((parts,)),
            dma((parts,)),
            dma((tiles,)),
            dma((tiles,)),
            dma((parts,)),
            dma((parts,)),
            dma((2,)),
        ],
        compiler_params=pltpu.CompilerParams(
            vmem_limit_bytes=VMEM_LIMIT, collective_id=1, has_side_effects=True
        ),
        cost_estimate=pl.CostEstimate(
            flops=seg_rows * 384 * 256, bytes_accessed=seg_rows * width * 8, transcendentals=0
        ),
        name="spread_back",
    )(links, shared, direct, *grads, small)


def finish_kernel(*refs):
    count = len(refs) // 2
    refs[count][...] = refs[0][...]

    @pl.when(pl.program_id(0) == 0)
    def _():
        for source, target in zip(refs[1:count], refs[count + 1 :]):
            target[...] = source[...]


def finish(arrays):
    rows, width = arrays[0].shape
    specs = [pl.BlockSpec((rows // PIECES, width), lambda i: (i, 0))]
    specs += [pl.BlockSpec(a.shape, lambda i: (0, 0)) for a in arrays[1:]]
    return pl.pallas_call(
        finish_kernel,
        grid=(PIECES,),
        in_specs=specs,
        out_specs=specs,
        out_shape=[jax.ShapeDtypeStruct(a.shape, a.dtype) for a in arrays],
        compiler_params=pltpu.CompilerParams(vmem_limit_bytes=VMEM_LIMIT),
        name="finish",
    )(*arrays)


def per_device(
    features, edges, route, cotangent, w_self, w_neighbor, bias, gain, w_expand, w_reduce
):
    feat = features[0]
    links = edges[0].T
    seg_rows, width = feat.shape
    parts = lax.axis_size("dom")
    trip_ids = route[0].reshape(-1)
    rows_dev = trip_ids.shape[0]
    capacity = 2 * rows_dev // parts
    cot_rows = cotangent[0].reshape(rows_dev, width)

    bits = (rows_dev - 1).bit_length()
    keys = (trip_ids.astype(jnp.uint32) << bits) | jnp.arange(rows_dev, dtype=jnp.uint32)
    keys = jnp.pad(lax.sort(keys, is_stable=False), (0, 1024))
    order = (keys & (rows_dev - 1)).astype(jnp.int32)
    sorted_ids = (keys >> bits).astype(jnp.int32).reshape(-1, 128)
    edges_of = jnp.arange(parts + 1, dtype=jnp.int32) * seg_rows
    bounds = jnp.sum((trip_ids[None, :] < edges_of[:, None]).astype(jnp.int32), axis=1)
    sent_rows, sent_ids = pack(order, bounds, sorted_ids, cot_rows, parts, capacity, seg_rows)
    msg, hid, slope_pre, act, bend, degree, table, got_rows, _, names = forward(
        links, feat, sent_rows, sent_ids, w_self, w_neighbor, bias[None], gain[None], w_expand
    )
    shared, direct, grad_expand, grad_reduce_t, grad_pair, small = encoder(
        table,
        names,
        got_rows.reshape(parts * capacity, width),
        degree,
        feat,
        msg,
        hid,
        slope_pre,
        act,
        bend,
        gain[None],
        w_expand,
        w_reduce,
        w_self,
        w_neighbor,
    )
    tiles = lax.axis_size("rep")
    scales = (
        1.0 / math.sqrt(tiles * parts * seg_rows),
        1.0 / math.sqrt(tiles * parts * rows_dev),
    )
    results = spread(links, shared, direct, grad_expand, grad_reduce_t, grad_pair, small, scales)
    grad_features, grad_expand, grad_reduce, grad_self, grad_neighbor, grad_bias, grad_gain = finish(
        results
    )
    return (
        grad_features[None],
        grad_self,
        grad_neighbor,
        grad_bias[0],
        grad_gain[0],
        grad_expand,
        grad_reduce,
    )


def solution(mesh):
    return jax.shard_map(
        per_device,
        mesh=mesh,
        in_specs=(
            P("rep", "dom", None),
            P("rep", "dom", None),
            P("rep", "dom", None),
            P("rep", "dom", None, None),
            P(),
            P(),
            P(),
            P(),
            P(),
            P(),
        ),
        out_specs=(P("rep", "dom", None), P(), P(), P(), P(), P(), P()),
        check_vma=False,
    )
```

```python
import functools
import math

import jax
import jax.numpy as jnp
from jax import lax
from jax.experimental import pallas as pl
from jax.experimental.pallas import tpu as pltpu
from jax.sharding import PartitionSpec as P

HALO = 128
WIN = 16
GROUP = 256
CHUNK = 256
OWNERS = 4
ROUTE = (
    (2, 1), (1, 2), (2, 3), (3, 2), (2, 2), (0, 2), (2, 0), (1, 1),
    (3, 3), (1, 3), (3, 1), (0, 1), (1, 0), (0, 3), (3, 0),
)
SIDE = 4
PASSES = 2
PIECES = 2
STEP = 1024
SPAN = 2 * STEP
F32 = jnp.float32
BF16 = jnp.bfloat16
VMEM_LIMIT = 56 * 1024 * 1024


def iota(shape, dim, dtype=jnp.int32):
    return lax.broadcasted_iota(jnp.int32, shape, dim).astype(dtype)


def dot(a, b, da=1, db=0):
    return lax.dot_general(a, b, (((da,), (db,)), ((), ())), preferred_element_type=F32)


def sigmoid(value):
    return 0.5 * jnp.tanh(0.5 * value) + 0.5


def pack_kernel(capacity, seg_rows, order, bounds, ids, cot, rows_out, ids_out, rows, stage):
    turn = pl.program_id(0)
    chunk = 512

    @pl.when(turn == 0)
    def _():
        stage[...] = jnp.zeros_like(stage)

        @pl.loop(0, cot.shape[0] // chunk)
        def _(i):
            part = pl.ds(pl.multiple_of(i * chunk, chunk), chunk)
            rows[part, :] = cot[part, :].astype(F32)

    for n in range(OWNERS):
        owner = turn * OWNERS + n
        start = bounds[owner]
        count = bounds[owner + 1] - start
        at = n * capacity

        def move(g, carry):
            base = pl.multiple_of(g * 16, 16)
            for j in range(16):
                source = order[start + base + j]
                stage[pl.ds(base + (at + j), 1), :] = rows[pl.ds(source, 1), :]
            return carry

        lax.fori_loop(0, (count + 15) // 16, move, 0)
        rows_out[n] = stage[at : at + capacity, :].astype(BF16)

        lines = capacity // 128
        shift = lax.rem(start, 128)
        window = ids[pl.ds(start // 128, 8), :]
        turned = pltpu.roll(window, lax.rem(128 - shift, 128), 1)
        lane = iota((lines, 128), 1)
        joined = jnp.where(lane < 128 - shift, turned[:lines], turned[1 : lines + 1])
        place = iota((lines, 128), 0) * 128 + lane
        ids_out[n] = jnp.where(place < count, joined - owner * seg_rows, seg_rows)


def pack(order, bounds, ids, cot, parts, capacity, seg_rows):
    rows_dev, width = cot.shape
    return pl.pallas_call(
        functools.partial(pack_kernel, capacity, seg_rows),
        grid_spec=pltpu.PrefetchScalarGridSpec(
            num_scalar_prefetch=2,
            grid=(parts // OWNERS,),
            in_specs=[
                pl.BlockSpec(ids.shape, lambda i, *_: (0, 0)),
                pl.BlockSpec(cot.shape, lambda i, *_: (0, 0)),
            ],
            out_specs=[
                pl.BlockSpec((OWNERS, capacity, width), lambda i, *_: (i, 0, 0)),
                pl.BlockSpec((OWNERS, capacity // 128, 128), lambda i, *_: (i, 0, 0)),
            ],
            scratch_shapes=[
                pltpu.VMEM((rows_dev, width), F32),
                pltpu.VMEM((OWNERS * capacity, width), F32),
            ],
        ),
        out_shape=[
            jax.ShapeDtypeStruct((parts, capacity, width), BF16),
            jax.ShapeDtypeStruct((parts, capacity // 128, 128), jnp.int32),
        ],
        compiler_params=pltpu.CompilerParams(vmem_limit_bytes=VMEM_LIMIT),
        name="pack_rows",
    )(order, bounds, ids, cot)


def hits(local, shift, same):
    rows = iota((128, 128), 0, F32).astype(BF16)
    table = same
    for slot in range(4):
        wanted = jnp.broadcast_to(local[slot : slot + 1, :] + shift, (16, 128)).astype(BF16)
        wanted = jnp.concatenate([wanted] * 8, axis=0)
        hit = jnp.where(wanted == rows, jnp.ones((), BF16), jnp.zeros((), BF16))
        table = hit if table is None else table + hit
    return table


def identity():
    return jnp.where(iota((128, 128), 0) == iota((128, 128), 1), 1.0, 0.0).astype(BF16)


def ends(links):
    lane = iota(links.shape, 1)
    return jnp.where(links != 0, links + lane, -100000).astype(F32)


def normalised(hid):
    values = hid.astype(F32)
    rate = lax.rsqrt(jnp.mean(values * values, axis=-1, keepdims=True) + 1e-06)
    return values * rate, rate


def remote(source, target, send, recv, device):
    return pltpu.make_async_remote_copy(
        src_ref=source,
        dst_ref=target,
        send_sem=send,
        recv_sem=recv,
        device_id=device,
        device_id_type=pl.DeviceIdType.MESH,
    )


def chip(me, down, along, swap):
    y, x, core = me // (2 * SIDE), lax.rem(me // 2, SIDE), lax.rem(me, 2)
    there = lax.rem(y + down, SIDE) * SIDE + lax.rem(x + along, SIDE)
    return there * 2 + lax.rem(core + swap, 2)


def others(me):
    for swap in range(2):
        for down, along in ROUTE:
            yield chip(me, down, along, swap)
    yield chip(me, 0, 0, 1)


def greet(barrier, device):
    pl.semaphore_signal(barrier, inc=1, device_id=device, device_id_type=pl.DeviceIdType.MESH)


def forward_kernel(
    links,
    feat,
    sent_rows,
    sent_ids,
    w_self,
    w_neighbor,
    bias,
    gain,
    w_expand,
    msg_out,
    hid_out,
    slope_out,
    act_out,
    bend_out,
    degree_out,
    table_out,
    got_rows,
    got_ids,
    names_out,
    ext,
    w_cat,
    ids,
    names,
    halo_send,
    halo_recv,
    rows_send,
    rows_recv,
    ids_send,
    ids_recv,
    sem,
):
    step = pl.program_id(0)
    steps = pl.num_programs(0)
    seg_rows, width = feat.shape
    parts = got_ids.shape[0]
    me, tile = lax.axis_index("dom"), lax.axis_index("rep")
    right, left = lax.rem(me + 1, parts), lax.rem(me + parts - 1, parts)

    def halos():
        tail, head = pl.ds(seg_rows - HALO, HALO), pl.ds(0, HALO)
        far, lanes = pl.ds(seg_rows + HALO, HALO), pl.ds(0, width)
        for n, (source, target, device) in enumerate(
            (
                (feat.at[tail, :], ext.at[head, lanes], right),
                (feat.at[head, :], ext.at[far, lanes], left),
            )
        ):
            yield remote(source, target, halo_send.at[n], halo_recv.at[n], (tile, device))

    def half(h):
        size = sent_rows.shape[1] // PASSES
        return pl.ds(h * size, size)

    def rows_copy(to, h):
        return remote(
            sent_rows.at[to, half(h)],
            got_rows.at[me, half(h)],
            rows_send.at[h, to],
            rows_recv.at[h, me],
            (tile, to),
        )

    def rows_arrival(at, h):
        return remote(
            sent_rows.at[at, half(h)],
            got_rows.at[at, half(h)],
            rows_send.at[h, at],
            rows_recv.at[h, at],
            (tile, at),
        )

    def ids_copy(to):
        return remote(sent_ids.at[to], got_ids.at[me], ids_send.at[to], ids_recv.at[me], (tile, to))

    def ids_arrival(at):
        return remote(sent_ids.at[at], got_ids.at[at], ids_send.at[at], ids_recv.at[at], (tile, at))

    def own_copies():
        yield pltpu.make_async_copy(sent_rows.at[me], got_rows.at[me], sem.at[1])
        yield pltpu.make_async_copy(sent_ids.at[me], got_ids.at[me], sem.at[2])

    @pl.when(step == 0)
    def _():
        barrier = pltpu.get_barrier_semaphore()

        @pl.loop(1, parts)
        def _(k):
            greet(barrier, (tile, lax.rem(me + k, parts)))

        pl.semaphore_wait(barrier, parts - 1)
        for copy in halos():
            copy.start()

        for h in range(PASSES):
            for to in others(me):
                rows_copy(to, h).start()
            if h == 0:

                @pl.loop(1, parts)
                def _(k):
                    ids_copy(lax.rem(me + k, parts)).start()

        local = pltpu.make_async_copy(
            feat, ext.at[pl.ds(HALO, seg_rows), pl.ds(0, width)], sem.at[0]
        )
        local.start()
        for copy in own_copies():
            copy.start()
        ext[:, width:] = jnp.ones((ext.shape[0], width), BF16)
        w_cat[:width, :] = w_self[...]
        w_cat[width:, :] = w_neighbor[...]
        local.wait()

    @pl.when(step == steps - 2)
    def _():
        for copy in halos():
            copy.wait_recv()

    start = lax.rem(step + 1, steps) * STEP
    same = identity()
    for j in range(STEP // 128):
        base = pl.multiple_of(start + j * 128, 128)
        local = ends(links[:, j * 128 : (j + 1) * 128])
        table = jnp.concatenate(
            [hits(local, 128.0, None), hits(local, 0.0, same), hits(local, -128.0, None)], axis=0
        )
        summed = dot(table, ext[pl.ds(base, 384), :], 0, 0)
        messages = summed[:, :width] / summed[:, width:]
        degree_out[j * 128 : (j + 1) * 128, :] = summed[:, width:].astype(BF16)
        msg_out[j * 128 : (j + 1) * 128, :] = messages.astype(BF16)
    own = ext[pl.ds(pl.multiple_of(start + HALO, 128), STEP), :width]
    pre = dot(jnp.concatenate([own, msg_out[...]], axis=1), w_cat[...]) + bias[...]
    gate = sigmoid(pre)
    swish = pre * gate
    hidden = (own.astype(F32) + swish).astype(BF16)
    hid_out[...] = hidden
    slope_out[...] = gate + swish * (1.0 - gate)
    unit, _ = normalised(hidden)
    normed = (unit * gain[...]).astype(BF16)
    for j in range(STEP // CHUNK):
        part = slice(j * CHUNK, (j + 1) * CHUNK)
        inner = dot(normed[part], w_expand[...])
        gate = sigmoid(inner)
        swish = inner * gate
        act_out[part, :] = swish.astype(BF16)
        bend_out[part, :] = (gate + swish * (1.0 - gate)).astype(BF16)

    @pl.when(step == steps - 1)
    def _():
        for copy in own_copies():
            copy.wait()

        @pl.loop(1, parts)
        def _(k):
            ids_arrival(lax.rem(me + k, parts)).wait_recv()

        fetch = pltpu.make_async_copy(got_ids, ids, sem.at[0])
        fetch.start()
        fetch.wait()
        capacity = ids.shape[1] * 128
        stride = capacity + WIN
        place = iota((16, 128), 0)
        weights = jnp.where(place == 0, 128.0, jnp.where(place == 1, 1.0, 0.0)).astype(BF16)
        bound = iota((1, 128), 1, F32) * float(GROUP)
        most = jnp.zeros((1, 128), F32)
        for s in range(parts):
            below = jnp.zeros((1, 128), F32)
            for k in range(ids.shape[1]):
                line = ids[s, k : k + 1, :]
                high = jnp.broadcast_to(line >> 7, (16, 128))
                low = jnp.broadcast_to(line & 127, (16, 128))
                digits = jnp.where(place == 0, high, jnp.where(place == 1, low, 0))
                column = dot(digits.astype(F32).astype(BF16), weights, 0, 0)
                at = s * stride + k * 128
                names[at : at + 128, :] = column
                below += jnp.sum(jnp.where(column < bound, 1.0, 0.0), axis=0, keepdims=True)
            names[s * stride + capacity : (s + 1) * stride, :] = jnp.full((WIN, 128), 1e6, F32)
            table_out[s : s + 1, :] = below.astype(jnp.int32)
            most = jnp.maximum(most, pltpu.roll(below, 127, 1) - below)
        table_out[parts : parts + 8, :] = jnp.broadcast_to(most, (8, 128)).astype(jnp.int32)
        store = pltpu.make_async_copy(names, names_out, sem.at[0])
        store.start()
        for copy in halos():
            copy.wait_send()

        @pl.loop(1, parts)
        def _(k):
            other = lax.rem(me + k, parts)
            ids_copy(other).wait_send()
            for h in range(PASSES):
                rows_arrival(other, h).wait_recv()
                rows_copy(other, h).wait_send()

        store.wait()


def forward(links, feat, sent_rows, sent_ids, w_self, w_neighbor, bias, gain, w_expand):
    seg_rows, width = feat.shape
    hidden = w_expand.shape[1]
    steps, parts = seg_rows // STEP, sent_ids.shape[0]
    columns = parts * (sent_rows.shape[1] + WIN)
    whole = lambda a: pl.BlockSpec(a.shape, lambda i: (0,) * a.ndim)
    rows = lambda n: pl.BlockSpec((STEP, n), lambda i: (lax.rem(i + 1, steps), 0))
    away = pl.BlockSpec(memory_space=pl.ANY)
    dma = pltpu.SemaphoreType.DMA
    return pl.pallas_call(
        forward_kernel,
        grid=(steps,),
        in_specs=[
            pl.BlockSpec((4, STEP), lambda i: (0, lax.rem(i + 1, steps))),
            away,
            away,
            away,
            whole(w_self),
            whole(w_neighbor),
            whole(bias),
            whole(gain),
            whole(w_expand),
        ],
        out_specs=[
            rows(width),
            rows(width),
            rows(width),
            rows(hidden),
            rows(hidden),
            rows(width),
            pl.BlockSpec((parts + 8, 128), lambda i: (0, 0)),
            away,
            away,
            away,
        ],
        out_shape=[
            jax.ShapeDtypeStruct((seg_rows, width), BF16),
            jax.ShapeDtypeStruct((seg_rows, width), BF16),
            jax.ShapeDtypeStruct((seg_rows, width), F32),
            jax.ShapeDtypeStruct((seg_rows, hidden), BF16),
            jax.ShapeDtypeStruct((seg_rows, hidden), BF16),
            jax.ShapeDtypeStruct((seg_rows, width), BF16),
            jax.ShapeDtypeStruct((parts + 8, 128), jnp.int32),
            jax.ShapeDtypeStruct(sent_rows.shape, BF16),
            jax.ShapeDtypeStruct(sent_ids.shape, jnp.int32),
            jax.ShapeDtypeStruct((columns, 128), F32),
        ],
        scratch_shapes=[
            pltpu.VMEM((seg_rows + 2 * HALO, 2 * width), BF16),
            pltpu.VMEM((2 * width, width), BF16),
            pltpu.VMEM(sent_ids.shape, jnp.int32),
            pltpu.VMEM((columns, 128), F32),
            dma((2,)),
            dma((2,)),
            dma((PASSES, parts)),
            dma((PASSES, parts)),
            dma((parts,)),
            dma((parts,)),
            dma((3,)),
        ],
        compiler_params=pltpu.CompilerParams(
            vmem_limit_bytes=VMEM_LIMIT, collective_id=2, has_side_effects=True
        ),
        cost_estimate=pl.CostEstimate(
            flops=seg_rows * 384 * 512, bytes_accessed=seg_rows * width * 12, transcendentals=0
        ),
        name="forward_messages",
    )(links, feat, sent_rows, sent_ids, w_self, w_neighbor, bias, gain, w_expand)


def encoder_kernel(
    table_s,
    names_in,
    got,
    degree,
    feat,
    msg,
    hid,
    slope_pre,
    act,
    bend,
    gain,
    w_expand,
    w_reduce,
    w_self,
    w_neighbor,
    shared_out,
    direct_out,
    ge_out,
    gr_out,
    gs_out,
    small_out,
    landed,
    rows,
    names,
    stage,
    onehot,
    cot_a,
    cot_b,
    low_s,
    inner_s,
    pair_s,
    w_back,
    sem,
):
    step = pl.program_id(0)
    width = feat.shape[1]
    sources = table_s.shape[0] - 8
    capacity = got.shape[0] // sources
    stride = capacity + WIN

    @pl.when(step == 0)
    def _():
        fetch = pltpu.make_async_copy(got, landed, sem.at[0])
        label = pltpu.make_async_copy(names_in, names, sem.at[1])
        fetch.start()
        label.start()
        w_back[:, :width] = w_neighbor[...].astype(F32).T.astype(BF16)
        w_back[:, width:] = w_self[...].astype(F32).T.astype(BF16)
        for total in (ge_out, gr_out, pair_s, small_out):
            total[...] = jnp.zeros_like(total)
        fetch.wait()
        for s in range(sources):
            rows[s * stride : s * stride + capacity, :] = landed[
                s * capacity : (s + 1) * capacity, :
            ].astype(F32)
            rows[s * stride + capacity : (s + 1) * stride, :] = jnp.zeros((WIN, 128), F32)
        label.wait()

    def collect(block, turn, j):
        first = (block * GROUP).astype(F32)
        left = iota((WIN, 128), 1, F32) + first
        for s in range(sources):
            at = jnp.minimum(table_s[s, block] + turn * WIN, capacity) + s * stride
            name = names[pl.ds(at, WIN), :]
            stage[j, s * WIN : (s + 1) * WIN, :] = rows[pl.ds(at, WIN), :].astype(BF16)
            for k in range(GROUP // 128):
                onehot[j, s * WIN : (s + 1) * WIN, k * 128 : (k + 1) * 128] = jnp.where(
                    name == left + 128.0 * k, 1.0, 0.0
                ).astype(BF16)
        return dot(onehot[j], stage[j], 0, 0)

    def gather(target, first):
        blocks = [jnp.minimum(first + j, last) for j in range(STEP // GROUP)]
        for j, block in enumerate(blocks):
            target[j * GROUP : (j + 1) * GROUP, :] = collect(block, 0, j)

    def overflow(target, first):
        for j in range(STEP // GROUP):
            block = jnp.minimum(first + j, last)
            turns = (table_s[sources, block] + (WIN - 1)) // WIN

            @pl.when(turns > 1)
            def _():
                @pl.loop(1, turns)
                def _(turn):
                    target[j * GROUP : (j + 1) * GROUP, :] += collect(block, turn, j)

    def encode(part, cot_s):
        scale = gain[...]
        unit, rate = normalised(hid[part, :])
        normed = (unit * scale).astype(BF16)
        low_s[...] = cot_s[...].astype(BF16)
        for j in range(STEP // CHUNK):
            rows_at = slice(j * CHUNK, (j + 1) * CHUNK)
            back_active = dot(low_s[rows_at, :], w_reduce[...], 1, 1)
            gates = bend[part.start + j * CHUNK : part.start + (j + 1) * CHUNK, :]
            inner_s[rows_at, :] = (back_active * gates.astype(F32)).astype(BF16)
        gr_out[...] += dot(low_s[...], act[part, :], 0, 0)
        ge_out[...] += dot(normed, inner_s[...], 0, 0)
        back_normed = dot(inner_s[...], w_expand[...], 1, 1)
        small_out[0:1, :] += jnp.sum(back_normed * unit, axis=0, keepdims=True)
        weighted = scale * back_normed
        mean = jnp.mean(weighted * unit, axis=-1, keepdims=True)
        back_hidden = cot_s[...] + (weighted - unit * mean) * rate
        back_pre = back_hidden * slope_pre[part, :]
        low = back_pre.astype(BF16)
        small_out[1:2, :] += jnp.sum(low.astype(F32), axis=0, keepdims=True)
        pair_s[...] += dot(low, jnp.concatenate([feat[part, :], msg[part, :]], axis=1), 0, 0)
        both = dot(low, w_back[...])
        shared_out[part, :] = (both[:, :width] / degree[part, :].astype(F32)).astype(BF16)
        direct_out[part, :] = back_hidden + both[:, width:]

    blocks = STEP // GROUP
    last = pl.num_programs(0) * (SPAN // GROUP) - 1

    @pl.when(step == 0)
    def _():
        gather(cot_a, 0)
        overflow(cot_a, 0)

    head, tail = slice(0, STEP), slice(STEP, SPAN)
    gather(cot_b, 2 * step * blocks + blocks)
    encode(head, cot_a)
    overflow(cot_b, 2 * step * blocks + blocks)
    encode(tail, cot_b)
    gather(cot_a, 2 * step * blocks + 2 * blocks)
    overflow(cot_a, 2 * step * blocks + 2 * blocks)

    @pl.when(step == pl.num_programs(0) - 1)
    def _():
        gs_out[...] = pair_s[...].T


def encoder(
    table, names, got, degree, feat, msg, hid, slope_pre, act, bend, gain, w_expand, w_reduce, w_self, w_neighbor
):
    seg_rows, width = feat.shape
    sources, hidden = table.shape[0] - 8, w_expand.shape[1]
    whole = lambda shape: pl.BlockSpec(shape, lambda i: (0,) * len(shape))
    rows = pl.BlockSpec((SPAN, width), lambda i: (i, 0))
    wide = pl.BlockSpec((SPAN, hidden), lambda i: (i, 0))
    return pl.pallas_call(
        encoder_kernel,
        grid=(seg_rows // SPAN,),
        in_specs=[
            pl.BlockSpec(memory_space=pltpu.SMEM),
            pl.BlockSpec(memory_space=pl.ANY),
            pl.BlockSpec(memory_space=pl.ANY),
            rows,
            rows,
            rows,
            rows,
            rows,
            wide,
            wide,
            whole((1, width)),
            whole((width, hidden)),
            whole((hidden, width)),
            whole((width, width)),
            whole((width, width)),
        ],
        out_specs=[
            rows,
            rows,
            whole((width, hidden)),
            whole((width, hidden)),
            whole((2 * width, width)),
            whole((8, width)),
        ],
        out_shape=[
            jax.ShapeDtypeStruct((seg_rows, width), BF16),
            jax.ShapeDtypeStruct((seg_rows, width), F32),
            jax.ShapeDtypeStruct((width, hidden), F32),
            jax.ShapeDtypeStruct((width, hidden), F32),
            jax.ShapeDtypeStruct((2 * width, width), F32),
            jax.ShapeDtypeStruct((8, width), F32),
        ],
        scratch_shapes=[
            pltpu.VMEM(got.shape, BF16),
            pltpu.VMEM(names.shape, F32),
            pltpu.VMEM(names.shape, F32),
            pltpu.VMEM((STEP // GROUP, sources * WIN, width), BF16),
            pltpu.VMEM((STEP // GROUP, sources * WIN, GROUP), BF16),
            pltpu.VMEM((STEP, width), F32),
            pltpu.VMEM((STEP, width), F32),
            pltpu.VMEM((STEP, width), BF16),
            pltpu.VMEM((STEP, hidden), BF16),
            pltpu.VMEM((width, 2 * width), F32),
            pltpu.VMEM((width, 2 * width), BF16),
            pltpu.SemaphoreType.DMA((2,)),
        ],
        compiler_params=pltpu.CompilerParams(vmem_limit_bytes=VMEM_LIMIT),
        cost_estimate=pl.CostEstimate(
            flops=seg_rows * width * hidden * 10, bytes_accessed=seg_rows * width * 20, transcendentals=0
        ),
        name="encoder_backward",
    )(
        table, names, got, degree, feat, msg, hid, slope_pre, act, bend, gain, w_expand, w_reduce, w_self, w_neighbor
    )


def spread_kernel(
    graph_scale,
    route_scale,
    links,
    shared,
    direct,
    grad_expand,
    grad_reduce,
    grad_pair,
    small,
    out,
    expand_out,
    reduce_out,
    self_out,
    neighbor_out,
    bias_out,
    gain_out,
    ext,
    links_ext,
    mine,
    parts_in,
    part,
    tiles_in,
    whole,
    wholes_in,
    halo_send,
    halo_recv,
    part_send,
    part_recv,
    tile_send,
    tile_recv,
    whole_send,
    whole_recv,
    sem,
):
    step = pl.program_id(0)
    steps = pl.num_programs(0)
    seg_rows, width = shared.shape
    hidden = expand_out.shape[1]
    parts, tiles = parts_in.shape[0], tiles_in.shape[0]
    half = parts // 2
    me, tile = lax.axis_index("dom"), lax.axis_index("rep")
    right, left = lax.rem(me + 1, parts), lax.rem(me + parts - 1, parts)

    def halos():
        tail = pl.ds(seg_rows - HALO, HALO)
        head = pl.ds(0, HALO)
        far = pl.ds(seg_rows + HALO, HALO)
        for n, (source, target, device) in enumerate(
            (
                (shared.at[tail, :], ext.at[head, :], right),
                (shared.at[head, :], ext.at[far, :], left),
                (links.at[:, tail], links_ext.at[:, head], right),
                (links.at[:, head], links_ext.at[:, far], left),
            )
        ):
            yield remote(source, target, halo_send.at[n], halo_recv.at[n], (tile, device))

    def part_copy(to):
        return remote(mine.at[to], parts_in.at[me], part_send.at[to], part_recv.at[me], (tile, to))

    def part_arrival(at):
        return remote(mine.at[at], parts_in.at[at], part_send.at[at], part_recv.at[at], (tile, at))

    def tile_copy(k):
        to = lax.rem(tile + k, tiles)
        return remote(part, tiles_in.at[tile], tile_send.at[k], tile_recv.at[tile], (to, me))

    def tile_arrival(k):
        at = lax.rem(tile + k, tiles)
        return remote(part, tiles_in.at[at], tile_send.at[k], tile_recv.at[at], (at, me))

    def whole_copy(to):
        return remote(whole, wholes_in.at[me], whole_send.at[to], whole_recv.at[me], (tile, to))

    def whole_arrival(at):
        return remote(whole, wholes_in.at[at], whole_send.at[at], whole_recv.at[at], (tile, at))

    @pl.when(step == 0)
    def _():
        barrier = pltpu.get_barrier_semaphore()

        @pl.loop(1, parts)
        def _(k):
            greet(barrier, (tile, lax.rem(me + k, parts)))

        for k in range(1, tiles):
            greet(barrier, (lax.rem(tile + k, tiles), me))
        local = pltpu.make_async_copy(shared, ext.at[pl.ds(HALO, seg_rows), :], sem.at[0])
        edges = pltpu.make_async_copy(links, links_ext.at[:, pl.ds(HALO, seg_rows)], sem.at[1])
        local.start()
        edges.start()
        mine[:half, :, :hidden] = grad_expand[...].astype(BF16)
        mine[half:, :, :hidden] = grad_reduce[...].astype(BF16)
        mine[:, :, hidden : hidden + width] = grad_pair[...].astype(BF16)
        mine[:, :, hidden + width :] = jnp.broadcast_to(small[...][None], (parts, 8, width)).astype(
            BF16
        )
        pl.semaphore_wait(barrier, parts + tiles - 2)
        for to in others(me):
            part_copy(to).start()
        for copy in halos():
            copy.start()
        local.wait()
        edges.wait()

    @pl.when(step == 3)
    def _():
        @pl.loop(1, parts)
        def _(k):
            part_arrival(lax.rem(me + k, parts)).wait_recv()

        parts_in[me] = mine[me]
        part[...] = lax.fori_loop(
            1,
            parts,
            lambda p, total: total + parts_in[p].astype(F32),
            parts_in[0].astype(F32),
        )
        for k in range(1, tiles):
            tile_copy(k).start()

    @pl.when(step == 4)
    def _():
        for k in range(1, tiles):
            tile_arrival(k).wait_recv()
        tiles_in[tile] = part[...]
        total = tiles_in[0]
        for t in range(1, tiles):
            total = total + tiles_in[t]
        whole[...] = total.astype(BF16)
        for to in others(me):
            whole_copy(to).start()

    @pl.when(step == steps - 2)
    def _():
        for copy in halos():
            copy.wait_recv()
        head, far = pl.ds(0, HALO), pl.ds(seg_rows + HALO, HALO)
        links_ext[:, head] = jnp.where(me > 0, links_ext[:, head], 0)
        links_ext[:, far] = jnp.where(me < parts - 1, links_ext[:, far], 0)

    at = lax.rem(step + 1, steps) * SPAN
    same = identity()
    for j in range(SPAN // 128):
        base = pl.multiple_of(at + j * 128, 128)
        near = [
            ends(links_ext[:, pl.ds(pl.multiple_of(base + k * 128, 128), 128)]) for k in range(3)
        ]
        table = jnp.concatenate(
            [hits(near[0], -128.0, None), hits(near[1], 0.0, same), hits(near[2], 128.0, None)],
            axis=1,
        )
        summed = dot(table, ext[pl.ds(base, 384), :])
        rows = slice(j * 128, (j + 1) * 128)
        out[rows, :] = (direct[rows, :] + summed).astype(BF16)

    @pl.when(step == steps - 1)
    def _():
        @pl.loop(1, parts)
        def _(k):
            whole_arrival(lax.rem(me + k, parts)).wait_recv()

        wholes_in[me] = whole[...]
        expand = wholes_in[:half, :, :hidden].astype(F32) * route_scale
        reduced = wholes_in[half:, :, :hidden].astype(F32) * route_scale
        pair = wholes_in[:, :, hidden : hidden + width].astype(F32) * graph_scale
        little = wholes_in[0, :, hidden + width :].astype(F32)
        expand_out[...] = expand.reshape(width, hidden)
        reduce_out[...] = reduced.reshape(width, hidden).T
        self_out[...] = pair[:half].reshape(width, width)
        neighbor_out[...] = pair[half:].reshape(width, width)
        gain_out[...] = little[0:1] * route_scale
        bias_out[...] = little[1:2] * graph_scale
        for copy in halos():
            copy.wait_send()

        @pl.loop(1, parts)
        def _(k):
            part_copy(lax.rem(me + k, parts)).wait_send()
            whole_copy(lax.rem(me + k, parts)).wait_send()

        for k in range(1, tiles):
            tile_copy(k).wait_send()


def spread(links, shared, direct, grad_expand, grad_reduce, grad_pair, small, scales):
    seg_rows, width = shared.shape
    hidden = grad_expand.shape[1]
    parts, tiles = lax.axis_size("dom"), lax.axis_size("rep")
    steps = seg_rows // SPAN
    slab = hidden + 2 * width
    cut = lambda a: a.reshape(-1, 8, a.shape[1])
    grads = [cut(grad_expand), cut(grad_reduce), cut(grad_pair)]
    whole = lambda a: pl.BlockSpec(a.shape, lambda i: (0,) * a.ndim)
    rows = pl.BlockSpec((SPAN, width), lambda i: (lax.rem(i + 1, steps), 0))
    dma = pltpu.SemaphoreType.DMA
    totals = [(width, hidden), (hidden, width), (width, width), (width, width), (1, width), (1, width)]
    return pl.pallas_call(
        functools.partial(spread_kernel, *scales),
        grid=(steps,),
        in_specs=[
            pl.BlockSpec(memory_space=pl.ANY),
            pl.BlockSpec(memory_space=pl.ANY),
            rows,
            *[whole(g) for g in grads],
            whole(small),
        ],
        out_specs=[rows, *[pl.BlockSpec(t, lambda i: (0, 0)) for t in totals]],
        out_shape=[
            jax.ShapeDtypeStruct((seg_rows, width), BF16),
            *[jax.ShapeDtypeStruct(t, F32) for t in totals],
        ],
        scratch_shapes=[
            pltpu.VMEM((seg_rows + 2 * HALO, width), BF16),
            pltpu.VMEM((4, seg_rows + 2 * HALO), jnp.int32),
            pltpu.VMEM((parts, 8, slab), BF16),
            pltpu.VMEM((parts, 8, slab), BF16),
            pltpu.VMEM((8, slab), F32),
            pltpu.VMEM((tiles, 8, slab), F32),
            pltpu.VMEM((8, slab), BF16),
            pltpu.VMEM((parts, 8, slab), BF16),
            dma((4,)),
            dma((4,)),
            dma((parts,)),
            dma((parts,)),
            dma((tiles,)),
            dma((tiles,)),
            dma((parts,)),
            dma((parts,)),
            dma((2,)),
        ],
        compiler_params=pltpu.CompilerParams(
            vmem_limit_bytes=VMEM_LIMIT, collective_id=1, has_side_effects=True
        ),
        cost_estimate=pl.CostEstimate(
            flops=seg_rows * 384 * 256, bytes_accessed=seg_rows * width * 8, transcendentals=0
        ),
        name="spread_back",
    )(links, shared, direct, *grads, small)


def finish_kernel(*refs):
    count = len(refs) // 2
    refs[count][...] = refs[0][...]

    @pl.when(pl.program_id(0) == 0)
    def _():
        for source, target in zip(refs[1:count], refs[count + 1 :]):
            target[...] = source[...]


def finish(arrays):
    rows, width = arrays[0].shape
    specs = [pl.BlockSpec((rows // PIECES, width), lambda i: (i, 0))]
    specs += [pl.BlockSpec(a.shape, lambda i: (0, 0)) for a in arrays[1:]]
    return pl.pallas_call(
        finish_kernel,
        grid=(PIECES,),
        in_specs=specs,
        out_specs=specs,
        out_shape=[jax.ShapeDtypeStruct(a.shape, a.dtype) for a in arrays],
        compiler_params=pltpu.CompilerParams(vmem_limit_bytes=VMEM_LIMIT),
        name="finish",
    )(*arrays)


def per_device(
    features, edges, route, cotangent, w_self, w_neighbor, bias, gain, w_expand, w_reduce
):
    feat = features[0]
    links = edges[0].T
    seg_rows, width = feat.shape
    parts = lax.axis_size("dom")
    trip_ids = route[0].reshape(-1)
    rows_dev = trip_ids.shape[0]
    capacity = 2 * rows_dev // parts
    cot_rows = cotangent[0].reshape(rows_dev, width)

    bits = (rows_dev - 1).bit_length()
    keys = (trip_ids.astype(jnp.uint32) << bits) | jnp.arange(rows_dev, dtype=jnp.uint32)
    keys = jnp.pad(lax.sort(keys, is_stable=False), (0, 1024))
    order = (keys & (rows_dev - 1)).astype(jnp.int32)
    sorted_ids = (keys >> bits).astype(jnp.int32).reshape(-1, 128)
    edges_of = jnp.arange(parts + 1, dtype=jnp.int32) * seg_rows
    bounds = jnp.sum((trip_ids[None, :] < edges_of[:, None]).astype(jnp.int32), axis=1)
    sent_rows, sent_ids = pack(order, bounds, sorted_ids, cot_rows, parts, capacity, seg_rows)
    msg, hid, slope_pre, act, bend, degree, table, got_rows, _, names = forward(
        links, feat, sent_rows, sent_ids, w_self, w_neighbor, bias[None], gain[None], w_expand
    )
    shared, direct, grad_expand, grad_reduce_t, grad_pair, small = encoder(
        table,
        names,
        got_rows.reshape(parts * capacity, width),
        degree,
        feat,
        msg,
        hid,
        slope_pre,
        act,
        bend,
        gain[None],
        w_expand,
        w_reduce,
        w_self,
        w_neighbor,
    )
    tiles = lax.axis_size("rep")
    scales = (
        1.0 / math.sqrt(tiles * parts * seg_rows),
        1.0 / math.sqrt(tiles * parts * rows_dev),
    )
    results = spread(links, shared, direct, grad_expand, grad_reduce_t, grad_pair, small, scales)
    grad_features, grad_expand, grad_reduce, grad_self, grad_neighbor, grad_bias, grad_gain = finish(
        results
    )
    return (
        grad_features[None],
        grad_self,
        grad_neighbor,
        grad_bias[0],
        grad_gain[0],
        grad_expand,
        grad_reduce,
    )


def solution(mesh):
    return jax.shard_map(
        per_device,
        mesh=mesh,
        in_specs=(
            P("rep", "dom", None),
            P("rep", "dom", None),
            P("rep", "dom", None),
            P("rep", "dom", None, None),
            P(),
            P(),
            P(),
            P(),
            P(),
            P(),
        ),
        out_specs=(P("rep", "dom", None), P(), P(), P(), P(), P(), P()),
        check_vma=False,
    )
```

```python
import functools
import math

import jax
import jax.numpy as jnp
from jax import lax
from jax.experimental import pallas as pl
from jax.experimental.pallas import tpu as pltpu
from jax.sharding import PartitionSpec as P

HALO = 128
WIN = 16
GROUP = 256
CHUNK = 256
OWNERS = 4
ROUTE = (
    (2, 1), (1, 2), (2, 3), (3, 2), (2, 2), (0, 2), (2, 0), (1, 1),
    (3, 3), (1, 3), (3, 1), (0, 1), (1, 0), (0, 3), (3, 0),
)
SIDE = 4
PASSES = 2
PIECES = 2
STEP = 1024
SPAN = 2 * STEP
F32 = jnp.float32
BF16 = jnp.bfloat16
VMEM_LIMIT = 56 * 1024 * 1024


def iota(shape, dim, dtype=jnp.int32):
    return lax.broadcasted_iota(jnp.int32, shape, dim).astype(dtype)


def dot(a, b, da=1, db=0):
    return lax.dot_general(a, b, (((da,), (db,)), ((), ())), preferred_element_type=F32)


def sigmoid(value):
    return 0.5 * jnp.tanh(0.5 * value) + 0.5


def pack_kernel(capacity, seg_rows, order, bounds, ids, cot, rows_out, ids_out, rows, stage):
    turn = pl.program_id(0)
    chunk = 512

    @pl.when(turn == 0)
    def _():
        stage[...] = jnp.zeros_like(stage)

        @pl.loop(0, cot.shape[0] // chunk)
        def _(i):
            part = pl.ds(pl.multiple_of(i * chunk, chunk), chunk)
            rows[part, :] = cot[part, :].astype(F32)

    for n in range(OWNERS):
        owner = turn * OWNERS + n
        start = bounds[owner]
        count = bounds[owner + 1] - start
        at = n * capacity

        def move(g, carry):
            base = pl.multiple_of(g * 16, 16)
            for j in range(16):
                source = order[start + base + j]
                stage[pl.ds(base + (at + j), 1), :] = rows[pl.ds(source, 1), :]
            return carry

        lax.fori_loop(0, (count + 15) // 16, move, 0)
        rows_out[n] = stage[at : at + capacity, :].astype(BF16)

        lines = capacity // 128
        shift = lax.rem(start, 128)
        window = ids[pl.ds(start // 128, 8), :]
        turned = pltpu.roll(window, lax.rem(128 - shift, 128), 1)
        lane = iota((lines, 128), 1)
        joined = jnp.where(lane < 128 - shift, turned[:lines], turned[1 : lines + 1])
        place = iota((lines, 128), 0) * 128 + lane
        ids_out[n] = jnp.where(place < count, joined - owner * seg_rows, seg_rows)


def pack(order, bounds, ids, cot, parts, capacity, seg_rows):
    rows_dev, width = cot.shape
    return pl.pallas_call(
        functools.partial(pack_kernel, capacity, seg_rows),
        grid_spec=pltpu.PrefetchScalarGridSpec(
            num_scalar_prefetch=2,
            grid=(parts // OWNERS,),
            in_specs=[
                pl.BlockSpec(ids.shape, lambda i, *_: (0, 0)),
                pl.BlockSpec(cot.shape, lambda i, *_: (0, 0)),
            ],
            out_specs=[
                pl.BlockSpec((OWNERS, capacity, width), lambda i, *_: (i, 0, 0)),
                pl.BlockSpec((OWNERS, capacity // 128, 128), lambda i, *_: (i, 0, 0)),
            ],
            scratch_shapes=[
                pltpu.VMEM((rows_dev, width), F32),
                pltpu.VMEM((OWNERS * capacity, width), F32),
            ],
        ),
        out_shape=[
            jax.ShapeDtypeStruct((parts, capacity, width), BF16),
            jax.ShapeDtypeStruct((parts, capacity // 128, 128), jnp.int32),
        ],
        compiler_params=pltpu.CompilerParams(vmem_limit_bytes=VMEM_LIMIT),
        name="pack_rows",
    )(order, bounds, ids, cot)


def hits(local, shift, same):
    rows = iota((128, 128), 0, F32).astype(BF16)
    table = same
    for slot in range(4):
        wanted = jnp.broadcast_to(local[slot : slot + 1, :] + shift, (16, 128)).astype(BF16)
        wanted = jnp.concatenate([wanted] * 8, axis=0)
        hit = jnp.where(wanted == rows, jnp.ones((), BF16), jnp.zeros((), BF16))
        table = hit if table is None else table + hit
    return table


def identity():
    return jnp.where(iota((128, 128), 0) == iota((128, 128), 1), 1.0, 0.0).astype(BF16)


def ends(links):
    lane = iota(links.shape, 1)
    return jnp.where(links != 0, links + lane, -100000).astype(F32)


def normalised(hid):
    values = hid.astype(F32)
    rate = lax.rsqrt(jnp.mean(values * values, axis=-1, keepdims=True) + 1e-06)
    return values * rate, rate


def remote(source, target, send, recv, device):
    return pltpu.make_async_remote_copy(
        src_ref=source,
        dst_ref=target,
        send_sem=send,
        recv_sem=recv,
        device_id=device,
        device_id_type=pl.DeviceIdType.MESH,
    )


def chip(me, down, along, swap):
    y, x, core = me // (2 * SIDE), lax.rem(me // 2, SIDE), lax.rem(me, 2)
    there = lax.rem(y + down, SIDE) * SIDE + lax.rem(x + along, SIDE)
    return there * 2 + lax.rem(core + swap, 2)


def others(me):
    for swap in range(2):
        for down, along in ROUTE:
            yield chip(me, down, along, swap)
    yield chip(me, 0, 0, 1)


def greet(barrier, device):
    pl.semaphore_signal(barrier, inc=1, device_id=device, device_id_type=pl.DeviceIdType.MESH)


def forward_kernel(
    links,
    feat,
    sent_rows,
    sent_ids,
    w_self,
    w_neighbor,
    bias,
    gain,
    w_expand,
    msg_out,
    hid_out,
    slope_out,
    act_out,
    bend_out,
    degree_out,
    table_out,
    got_rows,
    got_ids,
    names_out,
    ext,
    w_cat,
    ids,
    names,
    halo_send,
    halo_recv,
    rows_send,
    rows_recv,
    ids_send,
    ids_recv,
    sem,
):
    step = pl.program_id(0)
    steps = pl.num_programs(0)
    seg_rows, width = feat.shape
    parts = got_ids.shape[0]
    me, tile = lax.axis_index("dom"), lax.axis_index("rep")
    right, left = lax.rem(me + 1, parts), lax.rem(me + parts - 1, parts)

    def halos():
        tail, head = pl.ds(seg_rows - HALO, HALO), pl.ds(0, HALO)
        far, lanes = pl.ds(seg_rows + HALO, HALO), pl.ds(0, width)
        for n, (source, target, device) in enumerate(
            (
                (feat.at[tail, :], ext.at[head, lanes], right),
                (feat.at[head, :], ext.at[far, lanes], left),
            )
        ):
            yield remote(source, target, halo_send.at[n], halo_recv.at[n], (tile, device))

    def half(h):
        size = sent_rows.shape[1] // PASSES
        return pl.ds(h * size, size)

    def rows_copy(to, h):
        return remote(
            sent_rows.at[to, half(h)],
            got_rows.at[me, half(h)],
            rows_send.at[h, to],
            rows_recv.at[h, me],
            (tile, to),
        )

    def rows_arrival(at, h):
        return remote(
            sent_rows.at[at, half(h)],
            got_rows.at[at, half(h)],
            rows_send.at[h, at],
            rows_recv.at[h, at],
            (tile, at),
        )

    def ids_copy(to):
        return remote(sent_ids.at[to], got_ids.at[me], ids_send.at[to], ids_recv.at[me], (tile, to))

    def ids_arrival(at):
        return remote(sent_ids.at[at], got_ids.at[at], ids_send.at[at], ids_recv.at[at], (tile, at))

    def own_copies():
        yield pltpu.make_async_copy(sent_rows.at[me], got_rows.at[me], sem.at[1])
        yield pltpu.make_async_copy(sent_ids.at[me], got_ids.at[me], sem.at[2])

    @pl.when(step == 0)
    def _():
        barrier = pltpu.get_barrier_semaphore()

        @pl.loop(1, parts)
        def _(k):
            greet(barrier, (tile, lax.rem(me + k, parts)))

        pl.semaphore_wait(barrier, parts - 1)
        for copy in halos():
            copy.start()

        for h in range(PASSES):
            for to in others(me):
                rows_copy(to, h).start()
            if h == 0:

                @pl.loop(1, parts)
                def _(k):
                    ids_copy(lax.rem(me + k, parts)).start()

        local = pltpu.make_async_copy(
            feat, ext.at[pl.ds(HALO, seg_rows), pl.ds(0, width)], sem.at[0]
        )
        local.start()
        for copy in own_copies():
            copy.start()
        ext[:, width:] = jnp.ones((ext.shape[0], width), BF16)
        w_cat[:width, :] = w_self[...]
        w_cat[width:, :] = w_neighbor[...]
        local.wait()

    @pl.when(step == steps - 2)
    def _():
        for copy in halos():
            copy.wait_recv()

    start = lax.rem(step + 1, steps) * STEP
    same = identity()
    for j in range(STEP // 128):
        base = pl.multiple_of(start + j * 128, 128)
        local = ends(links[:, j * 128 : (j + 1) * 128])
        table = jnp.concatenate(
            [hits(local, 128.0, None), hits(local, 0.0, same), hits(local, -128.0, None)], axis=0
        )
        summed = dot(table, ext[pl.ds(base, 384), :], 0, 0)
        messages = summed[:, :width] / summed[:, width:]
        degree_out[j * 128 : (j + 1) * 128, :] = summed[:, width:].astype(BF16)
        msg_out[j * 128 : (j + 1) * 128, :] = messages.astype(BF16)
    own = ext[pl.ds(pl.multiple_of(start + HALO, 128), STEP), :width]
    pre = dot(jnp.concatenate([own, msg_out[...]], axis=1), w_cat[...]) + bias[...]
    gate = sigmoid(pre)
    swish = pre * gate
    hidden = (own.astype(F32) + swish).astype(BF16)
    hid_out[...] = hidden
    slope_out[...] = gate + swish * (1.0 - gate)
    unit, _ = normalised(hidden)
    normed = (unit * gain[...]).astype(BF16)
    for j in range(STEP // CHUNK):
        part = slice(j * CHUNK, (j + 1) * CHUNK)
        inner = dot(normed[part], w_expand[...])
        gate = sigmoid(inner)
        swish = inner * gate
        act_out[part, :] = swish.astype(BF16)
        bend_out[part, :] = (gate + swish * (1.0 - gate)).astype(BF16)

    @pl.when(step == steps - 1)
    def _():
        for copy in own_copies():
            copy.wait()

        @pl.loop(1, parts)
        def _(k):
            ids_arrival(lax.rem(me + k, parts)).wait_recv()

        fetch = pltpu.make_async_copy(got_ids, ids, sem.at[0])
        fetch.start()
        fetch.wait()
        capacity = ids.shape[1] * 128
        stride = capacity + WIN
        place = iota((16, 128), 0)
        weights = jnp.where(place == 0, 128.0, jnp.where(place == 1, 1.0, 0.0)).astype(BF16)
        bound = iota((1, 128), 1, F32) * float(GROUP)
        most = jnp.zeros((1, 128), F32)
        for s in range(parts):
            below = jnp.zeros((1, 128), F32)
            for k in range(ids.shape[1]):
                line = ids[s, k : k + 1, :]
                high = jnp.broadcast_to(line >> 7, (16, 128))
                low = jnp.broadcast_to(line & 127, (16, 128))
                digits = jnp.where(place == 0, high, jnp.where(place == 1, low, 0))
                column = dot(digits.astype(F32).astype(BF16), weights, 0, 0)
                at = s * stride + k * 128
                names[at : at + 128, :] = column
                below += jnp.sum(jnp.where(column < bound, 1.0, 0.0), axis=0, keepdims=True)
            names[s * stride + capacity : (s + 1) * stride, :] = jnp.full((WIN, 128), 1e6, F32)
            table_out[s : s + 1, :] = below.astype(jnp.int32)
            most = jnp.maximum(most, pltpu.roll(below, 127, 1) - below)
        table_out[parts : parts + 8, :] = jnp.broadcast_to(most, (8, 128)).astype(jnp.int32)
        store = pltpu.make_async_copy(names, names_out, sem.at[0])
        store.start()
        for copy in halos():
            copy.wait_send()

        @pl.loop(1, parts)
        def _(k):
            other = lax.rem(me + k, parts)
            ids_copy(other).wait_send()
            for h in range(PASSES):
                rows_arrival(other, h).wait_recv()
                rows_copy(other, h).wait_send()

        store.wait()


def forward(links, feat, sent_rows, sent_ids, w_self, w_neighbor, bias, gain, w_expand):
    seg_rows, width = feat.shape
    hidden = w_expand.shape[1]
    steps, parts = seg_rows // STEP, sent_ids.shape[0]
    columns = parts * (sent_rows.shape[1] + WIN)
    whole = lambda a: pl.BlockSpec(a.shape, lambda i: (0,) * a.ndim)
    rows = lambda n: pl.BlockSpec((STEP, n), lambda i: (lax.rem(i + 1, steps), 0))
    away = pl.BlockSpec(memory_space=pl.ANY)
    dma = pltpu.SemaphoreType.DMA
    return pl.pallas_call(
        forward_kernel,
        grid=(steps,),
        in_specs=[
            pl.BlockSpec((4, STEP), lambda i: (0, lax.rem(i + 1, steps))),
            away,
            away,
            away,
            whole(w_self),
            whole(w_neighbor),
            whole(bias),
            whole(gain),
            whole(w_expand),
        ],
        out_specs=[
            rows(width),
            rows(width),
            rows(width),
            rows(hidden),
            rows(hidden),
            rows(width),
            pl.BlockSpec((parts + 8, 128), lambda i: (0, 0)),
            away,
            away,
            away,
        ],
        out_shape=[
            jax.ShapeDtypeStruct((seg_rows, width), BF16),
            jax.ShapeDtypeStruct((seg_rows, width), BF16),
            jax.ShapeDtypeStruct((seg_rows, width), F32),
            jax.ShapeDtypeStruct((seg_rows, hidden), BF16),
            jax.ShapeDtypeStruct((seg_rows, hidden), BF16),
            jax.ShapeDtypeStruct((seg_rows, width), BF16),
            jax.ShapeDtypeStruct((parts + 8, 128), jnp.int32),
            jax.ShapeDtypeStruct(sent_rows.shape, BF16),
            jax.ShapeDtypeStruct(sent_ids.shape, jnp.int32),
            jax.ShapeDtypeStruct((columns, 128), F32),
        ],
        scratch_shapes=[
            pltpu.VMEM((seg_rows + 2 * HALO, 2 * width), BF16),
            pltpu.VMEM((2 * width, width), BF16),
            pltpu.VMEM(sent_ids.shape, jnp.int32),
            pltpu.VMEM((columns, 128), F32),
            dma((2,)),
            dma((2,)),
            dma((PASSES, parts)),
            dma((PASSES, parts)),
            dma((parts,)),
            dma((parts,)),
            dma((3,)),
        ],
        compiler_params=pltpu.CompilerParams(
            vmem_limit_bytes=VMEM_LIMIT, collective_id=2, has_side_effects=True
        ),
        cost_estimate=pl.CostEstimate(
            flops=seg_rows * 384 * 512, bytes_accessed=seg_rows * width * 12, transcendentals=0
        ),
        name="forward_messages",
    )(links, feat, sent_rows, sent_ids, w_self, w_neighbor, bias, gain, w_expand)


def encoder_kernel(
    table_s,
    names_in,
    got,
    degree,
    feat,
    msg,
    hid,
    slope_pre,
    act,
    bend,
    gain,
    w_expand,
    w_reduce,
    w_self,
    w_neighbor,
    shared_out,
    direct_out,
    ge_out,
    gr_out,
    gs_out,
    small_out,
    landed,
    rows,
    names,
    stage,
    onehot,
    cot_a,
    cot_b,
    low_s,
    inner_s,
    pair_s,
    w_back,
    sem,
):
    step = pl.program_id(0)
    width = feat.shape[1]
    sources = table_s.shape[0] - 8
    capacity = got.shape[0] // sources
    stride = capacity + WIN

    @pl.when(step == 0)
    def _():
        fetch = pltpu.make_async_copy(got, landed, sem.at[0])
        label = pltpu.make_async_copy(names_in, names, sem.at[1])
        fetch.start()
        label.start()
        w_back[:, :width] = w_neighbor[...].astype(F32).T.astype(BF16)
        w_back[:, width:] = w_self[...].astype(F32).T.astype(BF16)
        for total in (ge_out, gr_out, pair_s, small_out):
            total[...] = jnp.zeros_like(total)
        fetch.wait()
        for s in range(sources):
            rows[s * stride : s * stride + capacity, :] = landed[
                s * capacity : (s + 1) * capacity, :
            ].astype(F32)
            rows[s * stride + capacity : (s + 1) * stride, :] = jnp.zeros((WIN, 128), F32)
        label.wait()

    def collect(block, turn, j):
        first = (block * GROUP).astype(F32)
        left = iota((WIN, 128), 1, F32) + first
        for s in range(sources):
            at = jnp.minimum(table_s[s, block] + turn * WIN, capacity) + s * stride
            name = names[pl.ds(at, WIN), :]
            stage[j, s * WIN : (s + 1) * WIN, :] = rows[pl.ds(at, WIN), :].astype(BF16)
            for k in range(GROUP // 128):
                onehot[j, s * WIN : (s + 1) * WIN, k * 128 : (k + 1) * 128] = jnp.where(
                    name == left + 128.0 * k, 1.0, 0.0
                ).astype(BF16)
        return dot(onehot[j], stage[j], 0, 0)

    def gather(target, first):
        blocks = [jnp.minimum(first + j, last) for j in range(STEP // GROUP)]
        for j, block in enumerate(blocks):
            target[j * GROUP : (j + 1) * GROUP, :] = collect(block, 0, j)

    def overflow(target, first):
        for j in range(STEP // GROUP):
            block = jnp.minimum(first + j, last)
            turns = (table_s[sources, block] + (WIN - 1)) // WIN

            @pl.when(turns > 1)
            def _():
                @pl.loop(1, turns)
                def _(turn):
                    target[j * GROUP : (j + 1) * GROUP, :] += collect(block, turn, j)

    def encode(part, cot_s):
        scale = gain[...]
        unit, rate = normalised(hid[part, :])
        normed = (unit * scale).astype(BF16)
        low_s[...] = cot_s[...].astype(BF16)
        for j in range(STEP // CHUNK):
            rows_at = slice(j * CHUNK, (j + 1) * CHUNK)
            back_active = dot(low_s[rows_at, :], w_reduce[...], 1, 1)
            gates = bend[part.start + j * CHUNK : part.start + (j + 1) * CHUNK, :]
            inner_s[rows_at, :] = (back_active * gates.astype(F32)).astype(BF16)
        gr_out[...] += dot(low_s[...], act[part, :], 0, 0)
        ge_out[...] += dot(normed, inner_s[...], 0, 0)
        back_normed = dot(inner_s[...], w_expand[...], 1, 1)
        small_out[0:1, :] += jnp.sum(back_normed * unit, axis=0, keepdims=True)
        weighted = scale * back_normed
        mean = jnp.mean(weighted * unit, axis=-1, keepdims=True)
        back_hidden = cot_s[...] + (weighted - unit * mean) * rate
        back_pre = back_hidden * slope_pre[part, :]
        low = back_pre.astype(BF16)
        small_out[1:2, :] += jnp.sum(low.astype(F32), axis=0, keepdims=True)
        pair_s[...] += dot(low, jnp.concatenate([feat[part, :], msg[part, :]], axis=1), 0, 0)
        both = dot(low, w_back[...])
        shared_out[part, :] = (both[:, :width] / degree[part, :].astype(F32)).astype(BF16)
        direct_out[part, :] = back_hidden + both[:, width:]

    blocks = STEP // GROUP
    last = pl.num_programs(0) * (SPAN // GROUP) - 1

    @pl.when(step == 0)
    def _():
        gather(cot_a, 0)
        overflow(cot_a, 0)

    head, tail = slice(0, STEP), slice(STEP, SPAN)
    gather(cot_b, 2 * step * blocks + blocks)
    encode(head, cot_a)
    overflow(cot_b, 2 * step * blocks + blocks)
    encode(tail, cot_b)
    gather(cot_a, 2 * step * blocks + 2 * blocks)
    overflow(cot_a, 2 * step * blocks + 2 * blocks)

    @pl.when(step == pl.num_programs(0) - 1)
    def _():
        gs_out[...] = pair_s[...].T


def encoder(
    table, names, got, degree, feat, msg, hid, slope_pre, act, bend, gain, w_expand, w_reduce, w_self, w_neighbor
):
    seg_rows, width = feat.shape
    sources, hidden = table.shape[0] - 8, w_expand.shape[1]
    whole = lambda shape: pl.BlockSpec(shape, lambda i: (0,) * len(shape))
    rows = pl.BlockSpec((SPAN, width), lambda i: (i, 0))
    wide = pl.BlockSpec((SPAN, hidden), lambda i: (i, 0))
    return pl.pallas_call(
        encoder_kernel,
        grid=(seg_rows // SPAN,),
        in_specs=[
            pl.BlockSpec(memory_space=pltpu.SMEM),
            pl.BlockSpec(memory_space=pl.ANY),
            pl.BlockSpec(memory_space=pl.ANY),
            rows,
            rows,
            rows,
            rows,
            rows,
            wide,
            wide,
            whole((1, width)),
            whole((width, hidden)),
            whole((hidden, width)),
            whole((width, width)),
            whole((width, width)),
        ],
        out_specs=[
            rows,
            rows,
            whole((width, hidden)),
            whole((width, hidden)),
            whole((2 * width, width)),
            whole((8, width)),
        ],
        out_shape=[
            jax.ShapeDtypeStruct((seg_rows, width), BF16),
            jax.ShapeDtypeStruct((seg_rows, width), F32),
            jax.ShapeDtypeStruct((width, hidden), F32),
            jax.ShapeDtypeStruct((width, hidden), F32),
            jax.ShapeDtypeStruct((2 * width, width), F32),
            jax.ShapeDtypeStruct((8, width), F32),
        ],
        scratch_shapes=[
            pltpu.VMEM(got.shape, BF16),
            pltpu.VMEM(names.shape, F32),
            pltpu.VMEM(names.shape, F32),
            pltpu.VMEM((STEP // GROUP, sources * WIN, width), BF16),
            pltpu.VMEM((STEP // GROUP, sources * WIN, GROUP), BF16),
            pltpu.VMEM((STEP, width), F32),
            pltpu.VMEM((STEP, width), F32),
            pltpu.VMEM((STEP, width), BF16),
            pltpu.VMEM((STEP, hidden), BF16),
            pltpu.VMEM((width, 2 * width), F32),
            pltpu.VMEM((width, 2 * width), BF16),
            pltpu.SemaphoreType.DMA((2,)),
        ],
        compiler_params=pltpu.CompilerParams(vmem_limit_bytes=VMEM_LIMIT),
        cost_estimate=pl.CostEstimate(
            flops=seg_rows * width * hidden * 10, bytes_accessed=seg_rows * width * 20, transcendentals=0
        ),
        name="encoder_backward",
    )(
        table, names, got, degree, feat, msg, hid, slope_pre, act, bend, gain, w_expand, w_reduce, w_self, w_neighbor
    )


def spread_kernel(
    graph_scale,
    route_scale,
    links,
    shared,
    direct,
    grad_expand,
    grad_reduce,
    grad_pair,
    small,
    out,
    expand_out,
    reduce_out,
    self_out,
    neighbor_out,
    bias_out,
    gain_out,
    ext,
    links_ext,
    mine,
    parts_in,
    part,
    tiles_in,
    whole,
    wholes_in,
    halo_send,
    halo_recv,
    part_send,
    part_recv,
    tile_send,
    tile_recv,
    whole_send,
    whole_recv,
    sem,
):
    step = pl.program_id(0)
    steps = pl.num_programs(0)
    seg_rows, width = shared.shape
    hidden = expand_out.shape[1]
    parts, tiles = parts_in.shape[0], tiles_in.shape[0]
    half = parts // 2
    me, tile = lax.axis_index("dom"), lax.axis_index("rep")
    right, left = lax.rem(me + 1, parts), lax.rem(me + parts - 1, parts)

    def halos():
        tail = pl.ds(seg_rows - HALO, HALO)
        head = pl.ds(0, HALO)
        far = pl.ds(seg_rows + HALO, HALO)
        for n, (source, target, device) in enumerate(
            (
                (shared.at[tail, :], ext.at[head, :], right),
                (shared.at[head, :], ext.at[far, :], left),
                (links.at[:, tail], links_ext.at[:, head], right),
                (links.at[:, head], links_ext.at[:, far], left),
            )
        ):
            yield remote(source, target, halo_send.at[n], halo_recv.at[n], (tile, device))

    def part_copy(to):
        return remote(mine.at[to], parts_in.at[me], part_send.at[to], part_recv.at[me], (tile, to))

    def part_arrival(at):
        return remote(mine.at[at], parts_in.at[at], part_send.at[at], part_recv.at[at], (tile, at))

    def tile_copy(k):
        to = lax.rem(tile + k, tiles)
        return remote(part, tiles_in.at[tile], tile_send.at[k], tile_recv.at[tile], (to, me))

    def tile_arrival(k):
        at = lax.rem(tile + k, tiles)
        return remote(part, tiles_in.at[at], tile_send.at[k], tile_recv.at[at], (at, me))

    def whole_copy(to):
        return remote(whole, wholes_in.at[me], whole_send.at[to], whole_recv.at[me], (tile, to))

    def whole_arrival(at):
        return remote(whole, wholes_in.at[at], whole_send.at[at], whole_recv.at[at], (tile, at))

    @pl.when(step == 0)
    def _():
        barrier = pltpu.get_barrier_semaphore()

        @pl.loop(1, parts)
        def _(k):
            greet(barrier, (tile, lax.rem(me + k, parts)))

        for k in range(1, tiles):
            greet(barrier, (lax.rem(tile + k, tiles), me))
        local = pltpu.make_async_copy(shared, ext.at[pl.ds(HALO, seg_rows), :], sem.at[0])
        edges = pltpu.make_async_copy(links, links_ext.at[:, pl.ds(HALO, seg_rows)], sem.at[1])
        local.start()
        edges.start()
        mine[:half, :, :hidden] = grad_expand[...].astype(BF16)
        mine[half:, :, :hidden] = grad_reduce[...].astype(BF16)
        mine[:, :, hidden : hidden + width] = grad_pair[...].astype(BF16)
        mine[:, :, hidden + width :] = jnp.broadcast_to(small[...][None], (parts, 8, width)).astype(
            BF16
        )
        pl.semaphore_wait(barrier, parts + tiles - 2)
        for to in others(me):
            part_copy(to).start()
        for copy in halos():
            copy.start()
        local.wait()
        edges.wait()

    @pl.when(step == 3)
    def _():
        @pl.loop(1, parts)
        def _(k):
            part_arrival(lax.rem(me + k, parts)).wait_recv()

        parts_in[me] = mine[me]
        part[...] = lax.fori_loop(
            1,
            parts,
            lambda p, total: total + parts_in[p].astype(F32),
            parts_in[0].astype(F32),
        )
        for k in range(1, tiles):
            tile_copy(k).start()

    @pl.when(step == 5)
    def _():
        for k in range(1, tiles):
            tile_arrival(k).wait_recv()
        tiles_in[tile] = part[...]
        total = tiles_in[0]
        for t in range(1, tiles):
            total = total + tiles_in[t]
        whole[...] = total.astype(BF16)
        for to in others(me):
            whole_copy(to).start()

    @pl.when(step == steps - 2)
    def _():
        for copy in halos():
            copy.wait_recv()
        head, far = pl.ds(0, HALO), pl.ds(seg_rows + HALO, HALO)
        links_ext[:, head] = jnp.where(me > 0, links_ext[:, head], 0)
        links_ext[:, far] = jnp.where(me < parts - 1, links_ext[:, far], 0)

    at = lax.rem(step + 1, steps) * SPAN
    same = identity()
    for j in range(SPAN // 128):
        base = pl.multiple_of(at + j * 128, 128)
        near = [
            ends(links_ext[:, pl.ds(pl.multiple_of(base + k * 128, 128), 128)]) for k in range(3)
        ]
        table = jnp.concatenate(
            [hits(near[0], -128.0, None), hits(near[1], 0.0, same), hits(near[2], 128.0, None)],
            axis=1,
        )
        summed = dot(table, ext[pl.ds(base, 384), :])
        rows = slice(j * 128, (j + 1) * 128)
        out[rows, :] = (direct[rows, :] + summed).astype(BF16)

    @pl.when(step == steps - 1)
    def _():
        @pl.loop(1, parts)
        def _(k):
            whole_arrival(lax.rem(me + k, parts)).wait_recv()

        wholes_in[me] = whole[...]
        expand = wholes_in[:half, :, :hidden].astype(F32) * route_scale
        reduced = wholes_in[half:, :, :hidden].astype(F32) * route_scale
        pair = wholes_in[:, :, hidden : hidden + width].astype(F32) * graph_scale
        little = wholes_in[0, :, hidden + width :].astype(F32)
        expand_out[...] = expand.reshape(width, hidden)
        reduce_out[...] = reduced.reshape(width, hidden).T
        self_out[...] = pair[:half].reshape(width, width)
        neighbor_out[...] = pair[half:].reshape(width, width)
        gain_out[...] = little[0:1] * route_scale
        bias_out[...] = little[1:2] * graph_scale
        for copy in halos():
            copy.wait_send()

        @pl.loop(1, parts)
        def _(k):
            part_copy(lax.rem(me + k, parts)).wait_send()
            whole_copy(lax.rem(me + k, parts)).wait_send()

        for k in range(1, tiles):
            tile_copy(k).wait_send()


def spread(links, shared, direct, grad_expand, grad_reduce, grad_pair, small, scales):
    seg_rows, width = shared.shape
    hidden = grad_expand.shape[1]
    parts, tiles = lax.axis_size("dom"), lax.axis_size("rep")
    steps = seg_rows // SPAN
    slab = hidden + 2 * width
    cut = lambda a: a.reshape(-1, 8, a.shape[1])
    grads = [cut(grad_expand), cut(grad_reduce), cut(grad_pair)]
    whole = lambda a: pl.BlockSpec(a.shape, lambda i: (0,) * a.ndim)
    rows = pl.BlockSpec((SPAN, width), lambda i: (lax.rem(i + 1, steps), 0))
    dma = pltpu.SemaphoreType.DMA
    totals = [(width, hidden), (hidden, width), (width, width), (width, width), (1, width), (1, width)]
    return pl.pallas_call(
        functools.partial(spread_kernel, *scales),
        grid=(steps,),
        in_specs=[
            pl.BlockSpec(memory_space=pl.ANY),
            pl.BlockSpec(memory_space=pl.ANY),
            rows,
            *[whole(g) for g in grads],
            whole(small),
        ],
        out_specs=[rows, *[pl.BlockSpec(t, lambda i: (0, 0)) for t in totals]],
        out_shape=[
            jax.ShapeDtypeStruct((seg_rows, width), BF16),
            *[jax.ShapeDtypeStruct(t, F32) for t in totals],
        ],
        scratch_shapes=[
            pltpu.VMEM((seg_rows + 2 * HALO, width), BF16),
            pltpu.VMEM((4, seg_rows + 2 * HALO), jnp.int32),
            pltpu.VMEM((parts, 8, slab), BF16),
            pltpu.VMEM((parts, 8, slab), BF16),
            pltpu.VMEM((8, slab), F32),
            pltpu.VMEM((tiles, 8, slab), F32),
            pltpu.VMEM((8, slab), BF16),
            pltpu.VMEM((parts, 8, slab), BF16),
            dma((4,)),
            dma((4,)),
            dma((parts,)),
            dma((parts,)),
            dma((tiles,)),
            dma((tiles,)),
            dma((parts,)),
            dma((parts,)),
            dma((2,)),
        ],
        compiler_params=pltpu.CompilerParams(
            vmem_limit_bytes=VMEM_LIMIT, collective_id=1, has_side_effects=True
        ),
        cost_estimate=pl.CostEstimate(
            flops=seg_rows * 384 * 256, bytes_accessed=seg_rows * width * 8, transcendentals=0
        ),
        name="spread_back",
    )(links, shared, direct, *grads, small)


def finish_kernel(*refs):
    count = len(refs) // 2
    refs[count][...] = refs[0][...]

    @pl.when(pl.program_id(0) == 0)
    def _():
        for source, target in zip(refs[1:count], refs[count + 1 :]):
            target[...] = source[...]


def finish(arrays):
    rows, width = arrays[0].shape
    specs = [pl.BlockSpec((rows // PIECES, width), lambda i: (i, 0))]
    specs += [pl.BlockSpec(a.shape, lambda i: (0, 0)) for a in arrays[1:]]
    return pl.pallas_call(
        finish_kernel,
        grid=(PIECES,),
        in_specs=specs,
        out_specs=specs,
        out_shape=[jax.ShapeDtypeStruct(a.shape, a.dtype) for a in arrays],
        compiler_params=pltpu.CompilerParams(vmem_limit_bytes=VMEM_LIMIT),
        name="finish",
    )(*arrays)


def per_device(
    features, edges, route, cotangent, w_self, w_neighbor, bias, gain, w_expand, w_reduce
):
    feat = features[0]
    links = edges[0].T
    seg_rows, width = feat.shape
    parts = lax.axis_size("dom")
    trip_ids = route[0].reshape(-1)
    rows_dev = trip_ids.shape[0]
    capacity = 2 * rows_dev // parts
    cot_rows = cotangent[0].reshape(rows_dev, width)

    bits = (rows_dev - 1).bit_length()
    keys = (trip_ids.astype(jnp.uint32) << bits) | jnp.arange(rows_dev, dtype=jnp.uint32)
    keys = jnp.pad(lax.sort(keys, is_stable=False), (0, 1024))
    order = (keys & (rows_dev - 1)).astype(jnp.int32)
    sorted_ids = (keys >> bits).astype(jnp.int32).reshape(-1, 128)
    edges_of = jnp.arange(parts + 1, dtype=jnp.int32) * seg_rows
    bounds = jnp.sum((trip_ids[None, :] < edges_of[:, None]).astype(jnp.int32), axis=1)
    sent_rows, sent_ids = pack(order, bounds, sorted_ids, cot_rows, parts, capacity, seg_rows)
    msg, hid, slope_pre, act, bend, degree, table, got_rows, _, names = forward(
        links, feat, sent_rows, sent_ids, w_self, w_neighbor, bias[None], gain[None], w_expand
    )
    shared, direct, grad_expand, grad_reduce_t, grad_pair, small = encoder(
        table,
        names,
        got_rows.reshape(parts * capacity, width),
        degree,
        feat,
        msg,
        hid,
        slope_pre,
        act,
        bend,
        gain[None],
        w_expand,
        w_reduce,
        w_self,
        w_neighbor,
    )
    tiles = lax.axis_size("rep")
    scales = (
        1.0 / math.sqrt(tiles * parts * seg_rows),
        1.0 / math.sqrt(tiles * parts * rows_dev),
    )
    results = spread(links, shared, direct, grad_expand, grad_reduce_t, grad_pair, small, scales)
    grad_features, grad_expand, grad_reduce, grad_self, grad_neighbor, grad_bias, grad_gain = finish(
        results
    )
    return (
        grad_features[None],
        grad_self,
        grad_neighbor,
        grad_bias[0],
        grad_gain[0],
        grad_expand,
        grad_reduce,
    )


def solution(mesh):
    return jax.shard_map(
        per_device,
        mesh=mesh,
        in_specs=(
            P("rep", "dom", None),
            P("rep", "dom", None),
            P("rep", "dom", None),
            P("rep", "dom", None, None),
            P(),
            P(),
            P(),
            P(),
            P(),
            P(),
        ),
        out_specs=(P("rep", "dom", None), P(), P(), P(), P(), P(), P()),
        check_vma=False,
    )
```
